32 devices in a mesh: ctx: 16 (over z, y, x), wshard: 2 (over core).
Axes of the slice: x: 2, y: 2, z: 4, core: 2. Of those that a mesh axis runs over, the one named last changes fastest.
Arguments:
- inputs: bfloat16 [2, 10240, 512], P('wshard', 'ctx'), may hold values from -6 to 6
- cotangent: bfloat16 [2, 10240, 512], P('wshard', 'ctx'), may hold values from -6 to 6
- segments: int32 [2, 10240], P('wshard', 'ctx'), may hold values from 0 to 2, as said below
- routes: int32 [2, 10240, 2], P('wshard', 'ctx'), may hold values from 0 to 7, all different within a row
- norm_first: bfloat16 [512], P('wshard'), may hold values from 0.5 to 1.5
- w_query: bfloat16 [512, 512], P('wshard'), may hold values from -0.25 to 0.25
- w_keyval: bfloat16 [512, 128], P('wshard'), may hold values from -0.25 to 0.25
- w_router: bfloat16 [512, 8], P('wshard'), may hold values from -0.1875 to 0.1875
- w_out: bfloat16 [512, 512], P('wshard'), may hold values from -24 to 24
- norm_second: bfloat16 [512], P('wshard'), may hold values from 0.5 to 1.5
- w_up: bfloat16 [512, 2048], P('wshard'), may hold values from -0.25 to 0.25
- w_down: bfloat16 [2048, 512], P('wshard'), may hold values from -0.125 to 0.125
Outputs:
- output: bfloat16 [2, 10240, 512], P('wshard', 'ctx')
- input_grad: float32 [2, 10240, 512], P('wshard', 'ctx')
- grad_norm_first: float32 [512], P('wshard')
- grad_query: float32 [512, 512], P('wshard')
- grad_keyval: float32 [512, 128], P('wshard')
- grad_router: float32 [512, 8], P('wshard')
- grad_out: float32 [512, 512], P('wshard')
- grad_norm_second: float32 [512], P('wshard')
- grad_up: float32 [512, 2048], P('wshard')
- grad_down: float32 [2048, 512], P('wshard')
The draws below stay inside these ranges and needn't reach their ends.
Inputs may be any that keep to these rules, and one draw needn't show every extreme that they name: `segments`: in each group the tokens come in aligned units of 1024; the prompt fills 8192 // 1024 of them in any positions, each continuation exactly one. `routes`: each token names 2 different heads.
All inputs are finite; a program needn't handle non-finite values.
Results may differ from the reference program's by a relative error of at most 0.015.
Values may be sent and summed in bfloat16 or wider, within the bound.
No kernel may reach another device: no remote copies, remote signals or barrier semaphores. Data moves between devices by JAX's collectives and lax.ppermute only.
A program may use at most 128 MiB of HBM per device.

```python
import math
import jax
import jax.numpy as jnp
from jax import lax

D = 512
HEADS = 8
HEAD = 64
FF = 2048
TOP = 2
PROMPT = 8192
CONT = 1024
GROUP_TOK = 10240
GROUPS = 2


def draw_segments(key, part):
    unit_count = GROUP_TOK // CONT
    prompt_units = PROMPT // CONT

    def one_group(group_key):
        rank_of = jax.random.permutation(group_key, unit_count).astype(jnp.int32)
        labels = jnp.where(rank_of < prompt_units, 0, rank_of - prompt_units + 1)
        return jnp.repeat(labels, CONT, total_repeat_length=GROUP_TOK)
    group_keys = jax.vmap(lambda index: jax.random.fold_in(key, index))(jnp.arange(GROUPS))
    return jax.vmap(one_group)(group_keys).astype(jnp.int32)


def steps_of(stream_key, shape, shards, smallest, largest):
    def one(axis_at, shards_of):
        draws = jax.random.uniform(jax.random.fold_in(jax.random.fold_in(stream_key, 6), axis_at), (shards_of,), jnp.float32, smallest / len(shards), largest / len(shards))
        return jnp.repeat(jnp.exp(draws), shape[axis_at] // shards_of).reshape((-1,) + (1,) * (len(shape) - axis_at - 1))

    factor_of = one(*shards[0])
    for cut in shards[1:]:
        factor_of = factor_of * one(*cut)
    return factor_of


def different_ones(own_key, rows, number_of, top, lift):
    sequence = jax.random.permutation(jax.random.fold_in(own_key, 1), number_of)
    boost = sequence
    for power in range(3):
        boost = boost * boost // number_of
    boost = boost * lift // number_of
    chance = jax.random.randint(jax.random.fold_in(own_key, 2), (rows, number_of), 0, 4096) + boost
    sure = jax.random.permutation(jax.random.fold_in(own_key, 3), rows)[jnp.arange(number_of) % rows]
    chance = jnp.where(jnp.arange(rows)[:, None] == sure[None, :], 1 << 14, chance)
    priority = chance * number_of + jnp.arange(number_of)
    return lax.top_k(priority.astype(jnp.int32), top)[1].astype(jnp.int32)


def scatter_about(rng, extent, deviation, reach, pieces=(), kind=jnp.bfloat16):
    array = jax.random.normal(rng, extent, jnp.float32) * deviation
    if len(pieces) > 0:
        array = steps_of(rng, extent, pieces, -0.22, 0.18) * array
    return jnp.clip(array, min=-reach, max=reach).astype(kind)


def setup_inputs(seed: int = 0) -> dict:
    streams_of = jax.random.split(jax.random.key(seed), 13)
    return {
        "inputs": scatter_about(streams_of[0], (GROUPS, GROUP_TOK, D), 1.0, 6.0, ((0, 2), (1, 16))),
        "cotangent": scatter_about(streams_of[1], (GROUPS, GROUP_TOK, D), 1.0, 6.0, ((0, 2), (1, 16))),
        "segments": draw_segments(jax.random.fold_in(streams_of[12], 71), 0),
        "routes": different_ones(streams_of[3], GROUPS * GROUP_TOK, HEADS, TOP, 2048).reshape((GROUPS, GROUP_TOK, TOP)),
        "norm_first": jnp.clip(1.0 + 0.1 * jax.random.normal(streams_of[4], (D,), jnp.float32), 0.5, 1.5).astype(jnp.bfloat16),
        "w_query": scatter_about(streams_of[5], (D, HEADS * HEAD), D ** -0.5, 0.25, ((0, 2),)),
        "w_keyval": scatter_about(streams_of[6], (D, 2 * HEAD), D ** -0.5, 0.25, ((0, 2),)),
        "w_router": scatter_about(streams_of[7], (D, HEADS), (2 * D) ** -0.5, 0.1875, ((0, 2),)),
        "w_out": scatter_about(streams_of[8], (HEADS * HEAD, D), 4.0, 24.0, ((0, 2),)),
        "norm_second": jnp.clip(1.0 + 0.1 * jax.random.normal(streams_of[9], (D,), jnp.float32), 0.5, 1.5).astype(jnp.bfloat16),
        "w_up": scatter_about(streams_of[10], (D, FF), D ** -0.5, 0.25, ((0, 2),)),
        "w_down": scatter_about(streams_of[11], (FF, D), FF ** -0.5, 0.125, ((0, 2),)),
    }


@jax.custom_vjp
def low(v):
    return lax.optimization_barrier(v.astype(jnp.bfloat16)).astype(jnp.float32)

@jax.custom_vjp
def low_back(v):
    return v

def low_keep(v):
    return (low(v), None)

def low_pass(kept, grad):
    return (grad,)

def back_keep(v):
    return (v, None)

def back_low(kept, grad):
    return (low(grad),)
low.defvjp(low_keep, low_pass)
low_back.defvjp(back_keep, back_low)

def matmul(lhs_mat, rhs_mat):
    return jnp.dot(lhs_mat, rhs_mat, precision=lax.Precision.HIGHEST)

def layer_norm(values, gain_vec):
    mean_val = lax.optimization_barrier(jnp.mean(values, axis=-1, keepdims=True))
    centered = values - mean_val
    variance = lax.optimization_barrier(jnp.mean(centered * centered, axis=-1, keepdims=True))
    return centered * lax.rsqrt(variance + 1e-05) * gain_vec

def forward(inputs_f, norm_a, query_w, keyval_w, router_w, out_w, norm_b, up_w, down_w, seg_row, chosen):
    length = inputs_f.shape[0]
    head_count = router_w.shape[1]
    head_width = keyval_w.shape[1] // 2
    normed = low(layer_norm(inputs_f, norm_a))
    logits = matmul(normed, router_w)
    lifted = jnp.where(chosen, logits, -1e+30)
    peak_val = lax.optimization_barrier(jnp.max(lifted, axis=-1, keepdims=True))
    raised = jnp.where(chosen, jnp.exp(lifted - peak_val), 0.0)
    gate_vals = raised / lax.optimization_barrier(jnp.sum(raised, axis=-1, keepdims=True))
    queries = low(low_back(matmul(normed, query_w))).reshape(length, head_count, head_width)
    keyval = low(low_back(matmul(normed, keyval_w)))
    key_rows = keyval[:, :head_width]
    value_rows = keyval[:, head_width:]
    positions = jnp.arange(length, dtype=jnp.int32)
    block_rows = math.gcd(length, 512)

    def attend(packed):
        query_block, pos_block, seg_block = packed
        same_seg = (seg_row[None, :] == seg_block[:, None]) & (positions[None, :] <= pos_block[:, None])
        from_prompt = (seg_row[None, :] == 0) & (seg_block[:, None] != 0)
        usable = same_seg | from_prompt
        scores = low_back(jnp.einsum('thd,jd->thj', query_block, key_rows, precision=lax.Precision.HIGHEST) * 0.125)
        scores = jnp.where(usable[:, None, :], scores, -1e+30)
        weights = jax.nn.softmax(scores, axis=-1)
        return jnp.einsum('thj,jd->thd', low(weights), value_rows, precision=lax.Precision.HIGHEST)
    attended = lax.map(jax.checkpoint(attend), (queries.reshape(length // block_rows, block_rows, head_count, head_width), positions.reshape(length // block_rows, block_rows), seg_row.reshape(length // block_rows, block_rows)))
    attended = low_back(attended.reshape(length, head_count, head_width))
    mixed_in = low(gate_vals[:, :, None] * attended).reshape(length, head_count * head_width)
    middle = inputs_f + low_back(matmul(mixed_in, out_w))
    normed_b = low(layer_norm(middle, norm_b))
    hidden = low(jax.nn.gelu(low_back(matmul(normed_b, up_w)), approximate=True))
    return middle + low_back(matmul(hidden, down_w))

def reference(inputs, cotangent, segments, routes, norm_first, w_query, w_keyval, w_router, w_out, norm_second, w_up, w_down):
    weights_f = tuple((weight.astype(jnp.float32) for weight in (norm_first, w_query, w_keyval, w_router, w_out, norm_second, w_up, w_down)))
    head_count = w_router.shape[1]

    def one_group(running, packed):
        group_in, group_cot, group_seg, group_routes = packed
        chosen = jnp.any(group_routes[:, :, None] == jnp.arange(head_count, dtype=jnp.int32)[None, None, :], axis=1)

        def forward_of(inputs_f, *params):
            return forward(inputs_f, *params, group_seg, chosen)
        result, pull_back = jax.vjp(forward_of, group_in.astype(jnp.float32), *weights_f)
        gradients = pull_back(group_cot.astype(jnp.float32))
        running = tuple((summed + grad_part for summed, grad_part in zip(running, gradients[1:])))
        return (running, (result.astype(jnp.bfloat16), gradients[0]))
    zeros_init = tuple((jnp.zeros_like(weight) for weight in weights_f))
    totals, (output, input_grad) = lax.scan(one_group, zeros_init, (inputs, cotangent, segments, routes))
    return (output, input_grad, totals[0], totals[1], totals[2], totals[3], totals[4], totals[5], totals[6], totals[7])
```

```python
import functools
import math

import jax
import jax.numpy as jnp
from jax import lax
from jax.experimental import pallas as pl
from jax.experimental.pallas import tpu as pltpu
from jax.sharding import Mesh, PartitionSpec as P

F32 = jnp.float32
BF = jnp.bfloat16
UNIT = 1024
TB = 64
INNER = UNIT // TB
RUN = 8
LOG2E = 1.4426950408889634
BIG = 2.0**100


def dot(lhs, rhs):
    return lax.dot_general(lhs, rhs, (((1,), (0,)), ((), ())), preferred_element_type=F32)


def inner(lhs, rhs):
    return lax.dot_general(lhs, rhs, (((0,), (0,)), ((), ())), preferred_element_type=F32)


def outer(lhs, rhs):
    return lax.dot_general(lhs, rhs, (((1,), (1,)), ((), ())), preferred_element_type=F32)


def split3(x):
    a = x.astype(BF)
    rest = x - a.astype(F32)
    b = rest.astype(BF)
    return a, b, (rest - b.astype(F32)).astype(BF)


def to_lanes(x, heads, hw):
    xt = x.T
    return jnp.concatenate([xt[h * hw : (h + 1) * hw] for h in range(heads)], axis=1)


def key_offsets(index, me):
    owner = jnp.bitwise_xor(index >> 6, me)
    rest = index & (TB - 1)
    return (rest >> 3) * (RUN * INNER) + owner * RUN + (rest & 7)


def query_offsets(index, me):
    rest = index & (TB - 1)
    return (rest >> 3) * (RUN * INNER) + me * RUN + (rest & 7)


def unit_rows(halves, slot, part):
    half = halves[0].shape[1] // TB
    first = slot * INNER
    if part < half:
        tile = halves[0][first : first + INNER, part * TB : (part + 1) * TB, :]
    else:
        tile = halves[1][first : first + INNER, (part - half) * TB : (part - half + 1) * TB, :]
    return tile.reshape(UNIT, tile.shape[-1])


def fwd_kernel(
    useg, place, kva_ref, kvb_ref, q_ref, o_ref, ot_ref, l_ref, qt_ref,
    kaug, vt, qa, acc, ref_row, plist, rank, bad, *, nb, slots, heads, hw
):
    me, group = place[0], place[1]
    scale = LOG2E / math.sqrt(hw)
    lanes = heads * TB
    units = slots * nb

    def scan(u, n):
        rank[u] = n
        plist[n] = jnp.bitwise_xor(u // nb, group) * nb + u % nb
        return n + jnp.where(useg[u] == 0, 1, 0)

    prompt_units = lax.fori_loop(0, units, scan, jnp.int32(0))
    lane = lax.broadcasted_iota(jnp.int32, (UNIT, 2 * hw), 1)
    row = lax.broadcasted_iota(jnp.int32, (2 * hw, UNIT), 0)
    extra = jnp.where(lane < hw + 3, 1.0, 0.0).astype(BF)
    for slot in range(slots):
        for part in range(nb):
            rel = slot * nb + part
            tile = unit_rows((kva_ref, kvb_ref), slot, part)
            kaug[rel] = jnp.where(lane < hw, tile, extra)
            flip = tile.T
            vt[rel] = jnp.where(row < hw, jnp.ones_like(flip), flip)

    def block(i, carry):
        own = group * nb + i
        full_units = jnp.where(useg[own] != 0, prompt_units, rank[own])
        rows = pl.ds(pl.multiple_of(i * TB, TB), TB)
        qt = to_lanes(q_ref[rows, :], heads, hw)
        qt_ref[i] = qt
        qa[0:hw, :] = qt
        qa[hw:, :] = jnp.zeros((hw, lanes), BF)
        mask = key_offsets(
            lax.broadcasted_iota(jnp.int32, (UNIT, lanes), 0), me
        ) <= query_offsets(lax.broadcasted_iota(jnp.int32, (UNIT, lanes), 1), me)
        ref_row[...] = jnp.max(
            jnp.where(mask, dot(kaug[i], qa[...]), -1e30), axis=0, keepdims=True
        )
        bad[0] = 1

        def attempt(turn, carry):
            @pl.when(bad[0] != 0)
            def _():
                @pl.when(turn == 1)
                def _():
                    qa[hw:, :] = jnp.zeros((hw, lanes), BF)

                    def highest(k, carry):
                        ref_row[...] = jnp.maximum(
                            ref_row[...],
                            jnp.max(dot(kaug[plist[k]], qa[...]), axis=0, keepdims=True),
                        )
                        return carry

                    lax.fori_loop(0, full_units, highest, 0)

                a, b, c = split3(-ref_row[...])
                qa[hw:, :] = jnp.concatenate([a, b, c, jnp.zeros((hw - 3, lanes), BF)], axis=0)
                s = jnp.where(mask, dot(kaug[i], qa[...]) * scale, -1e30)
                acc[...] = dot(vt[i], jnp.exp2(s).astype(BF))

                def full(k, carry):
                    u = plist[k]
                    p = jnp.exp2(dot(kaug[u], qa[...]) * scale).astype(BF)
                    acc[...] += dot(vt[u], p)
                    return carry

                lax.fori_loop(0, full_units, full, 0)
                bad[0] = jnp.where(jnp.max(acc[0:1, :]) < BIG, 0, 1)

            return carry

        lax.fori_loop(0, 2, attempt, 0)
        ot = acc[hw:, :] / acc[0:hw, :]
        ot_ref[i] = ot
        l_ref[i] = ref_row[...] + jnp.log2(acc[0:1, :]) / scale
        on = jnp.concatenate([ot[:, h * TB : (h + 1) * TB] for h in range(heads)], axis=0)
        o_ref[rows, :] = on.T
        return carry

    lax.fori_loop(0, nb, block, 0)


def attention_forward(useg, place, kva, kvb, q, heads, hw):
    rows = q.shape[0]
    nb = rows // TB
    slots = kva.shape[0] // INNER
    lanes = heads * TB
    units = slots * nb
    vm = pl.BlockSpec(memory_space=pltpu.VMEM)
    sm = pl.BlockSpec(memory_space=pltpu.SMEM)
    return pl.pallas_call(
        functools.partial(fwd_kernel, nb=nb, slots=slots, heads=heads, hw=hw),
        out_shape=(
            jax.ShapeDtypeStruct((rows, heads * hw), F32),
            jax.ShapeDtypeStruct((nb, hw, lanes), F32),
            jax.ShapeDtypeStruct((nb, 1, lanes), F32),
            jax.ShapeDtypeStruct((nb, hw, lanes), BF),
        ),
        in_specs=[sm, sm, vm, vm, vm],
        out_specs=(vm,) * 4,
        scratch_shapes=[
            pltpu.VMEM((units, UNIT, 2 * hw), BF),
            pltpu.VMEM((units, 2 * hw, UNIT), BF),
            pltpu.VMEM((2 * hw, lanes), BF),
            pltpu.VMEM((2 * hw, lanes), F32),
            pltpu.VMEM((1, lanes), F32),
            pltpu.SMEM((units + 1,), jnp.int32),
            pltpu.SMEM((units + 1,), jnp.int32),
            pltpu.SMEM((1,), jnp.int32),
        ],
        compiler_params=pltpu.CompilerParams(vmem_limit_bytes=60 << 20),
        cost_estimate=pl.CostEstimate(
            flops=40 * 10**9, bytes_accessed=8 << 20, transcendentals=26 * 10**6
        ),
        name="attention_forward",
    )(useg, place, kva, kvb, q)


def bwd_kernel(
    useg, place, kva_ref, kvb_ref, qt_ref, ot_ref, l_ref, do_ref, dq_ref, dkv_ref,
    kt, vt, qa, doa, dot_t, dqacc, dkvt, ktile, *, nb, slots, heads, hw
):
    rel = pl.program_id(0)
    me, group = place[0], place[1]
    slot, part = rel // nb, rel % nb
    unit = jnp.bitwise_xor(slot, group) * nb + part
    scale = LOG2E / math.sqrt(hw)
    lanes = heads * TB

    @pl.when(rel == 0)
    def _():
        dqacc[...] = jnp.zeros_like(dqacc)

        def prepare(i, carry):
            rows = pl.ds(pl.multiple_of(i * TB, TB), TB)
            pad = jnp.zeros((hw - 3, lanes), BF)
            a, b, c = split3(-l_ref[i])
            qa[i] = jnp.concatenate([qt_ref[i], a, b, c, pad], axis=0).T
            dt = to_lanes(do_ref[rows, :], heads, hw)
            dot_t[i] = dt
            total = jnp.sum(dt.astype(F32) * ot_ref[i], axis=0, keepdims=True)
            a, b, c = split3(-total)
            doa[i] = jnp.concatenate([dt, a, b, c, pad], axis=0).T
            return carry

        lax.fori_loop(0, nb, prepare, 0)

    half = kva_ref.shape[1] // TB
    for s in range(INNER):
        @pl.when(part < half)
        def _(s=s):
            ktile[s * TB : (s + 1) * TB, :] = kva_ref[
                slot * INNER + s, pl.ds(pl.multiple_of(part * TB, TB), TB), :
            ]

        @pl.when(part >= half)
        def _(s=s):
            ktile[s * TB : (s + 1) * TB, :] = kvb_ref[
                slot * INNER + s, pl.ds(pl.multiple_of((part - half) * TB, TB), TB), :
            ]

    flip = ktile[...].T
    row = lax.broadcasted_iota(jnp.int32, (hw, UNIT), 0)
    ones = jnp.where(row < 3, 1.0, 0.0).astype(BF)
    kt[...] = jnp.concatenate([flip[:hw], ones], axis=0)
    vt[...] = jnp.concatenate([flip[hw:], ones], axis=0)
    dkvt[...] = jnp.zeros_like(dkvt)
    unit_seg = useg[unit]

    def block(i, carry):
        own = group * nb + i

        def step(masked):
            s = dot(qa[i], kt[...]) * scale
            if masked:
                mask = key_offsets(
                    lax.broadcasted_iota(jnp.int32, (lanes, UNIT), 1), me
                ) <= query_offsets(lax.broadcasted_iota(jnp.int32, (lanes, UNIT), 0), me)
                s = jnp.where(mask, s, -1e30)
            p = jnp.exp2(s)
            ds = (p * dot(doa[i], vt[...])).astype(BF)
            dkvt[hw:, :] += dot(dot_t[i], p.astype(BF))
            dkvt[:hw, :] += dot(qt_ref[i], ds)
            dqacc[i] += dot(ds, ktile[...])

        @pl.when((unit_seg == 0) & (own != unit) & ((useg[own] != 0) | (own > unit)))
        def _():
            step(False)

        @pl.when(own == unit)
        def _():
            step(True)

        return carry

    lax.fori_loop(0, nb, block, 0)
    factor = jnp.where(
        lax.broadcasted_iota(jnp.int32, (2 * hw, 1), 0) < hw, 1 / math.sqrt(hw), 1.0
    )
    dkv = (dkvt[...] * factor).astype(BF).T
    for s in range(INNER):
        dkv_ref[jnp.bitwise_xor(me, s)] = dkv[s * TB : (s + 1) * TB, :]

    @pl.when(rel == pl.num_programs(0) - 1)
    def _():
        def finish(i, carry):
            rows = pl.ds(pl.multiple_of(i * TB, TB), TB)
            a = dqacc[i]
            dq_ref[rows, :] = (
                jnp.concatenate([a[h * TB : (h + 1) * TB, :hw] for h in range(heads)], axis=1)
                * (1 / math.sqrt(hw))
            ).astype(BF)
            return carry

        lax.fori_loop(0, nb, finish, 0)


def attention_backward(useg, place, kva, kvb, qt, ot, low, do, heads, hw):
    rows = do.shape[0]
    nb = rows // TB
    slots = kva.shape[0] // INNER
    lanes = heads * TB
    vm = pl.BlockSpec(memory_space=pltpu.VMEM)
    return pl.pallas_call(
        functools.partial(bwd_kernel, nb=nb, slots=slots, heads=heads, hw=hw),
        out_shape=(
            jax.ShapeDtypeStruct((rows, heads * hw), BF),
            jax.ShapeDtypeStruct((slots * INNER, rows, 2 * hw), BF),
        ),
        grid_spec=pltpu.PrefetchScalarGridSpec(
            num_scalar_prefetch=2,
            grid=(slots * nb,),
            in_specs=[vm] * 6,
            out_specs=(
                pl.BlockSpec((rows, heads * hw), lambda u, seg, place: (0, 0)),
                pl.BlockSpec(
                    (INNER, TB, 2 * hw),
                    lambda u, seg, place: (jnp.bitwise_xor(u // nb, place[1]), u % nb, 0),
                ),
            ),
            scratch_shapes=[
                pltpu.VMEM((2 * hw, UNIT), BF),
                pltpu.VMEM((2 * hw, UNIT), BF),
                pltpu.VMEM((nb, lanes, 2 * hw), BF),
                pltpu.VMEM((nb, lanes, 2 * hw), BF),
                pltpu.VMEM((nb, hw, lanes), BF),
                pltpu.VMEM((nb, lanes, 2 * hw), F32),
                pltpu.VMEM((2 * hw, UNIT), F32),
                pltpu.VMEM((UNIT, 2 * hw), BF),
            ],
        ),
        compiler_params=pltpu.CompilerParams(vmem_limit_bytes=60 << 20),
        cost_estimate=pl.CostEstimate(
            flops=80 * 10**9, bytes_accessed=12 << 20, transcendentals=26 * 10**6
        ),
        name="attention_backward",
    )(useg, place, kva, kvb, qt, ot, low, do)


class Layout:
    def __init__(self, ctx_count):
        sizes = [4]
        while math.prod(sizes) < ctx_count:
            sizes.append(2)
        assert math.prod(sizes) == ctx_count
        self.sizes = tuple(sizes)
        self.axes = tuple(f"c{k}" for k in range(len(sizes)))
        cut = len(sizes)
        while math.prod(sizes[cut:]) < INNER:
            cut -= 1
        assert math.prod(sizes[cut:]) == INNER
        self.outer_axes, self.inner_axes = self.axes[:cut], self.axes[cut:]
        self.count = ctx_count


def exchange(x, axis, size, step):
    return lax.ppermute(x, axis, [(i, i ^ step) for i in range(size)])


def gather_xor(x, order, lay):
    have = {axis: 1 for axis in lay.axes}
    stacked = x[None]
    done = []
    for axis in order:
        size = lay.sizes[lay.axes.index(axis)]
        stacked = jnp.stack(
            [stacked] + [exchange(stacked, axis, size, step) for step in range(1, size)]
        )
        stacked = stacked.reshape((-1,) + x.shape)
        done.insert(0, axis)
    if done != list(lay.axes):
        sizes = [lay.sizes[lay.axes.index(axis)] for axis in done]
        stacked = stacked.reshape(tuple(sizes) + x.shape)
        turn = [done.index(axis) for axis in lay.axes]
        rest = list(range(len(done), stacked.ndim))
        stacked = stacked.transpose(turn + rest).reshape((-1,) + x.shape)
    return stacked


def deal(x, lay):
    rows, width = x.shape
    packed = x.reshape(rows // (RUN * INNER), INNER, RUN, width).transpose(1, 0, 2, 3)
    packed = packed.reshape(INNER, rows // INNER, width)
    return lax.all_to_all(packed, lay.inner_axes, 0, 0, tiled=True)


def undeal(x, lay):
    rows, width = x.shape
    back = lax.all_to_all(
        x.reshape(INNER, rows // INNER, width), lay.inner_axes, 0, 0, tiled=True
    )
    back = back.reshape(INNER, rows // (RUN * INNER), RUN, width).transpose(1, 0, 2, 3)
    return back.reshape(rows, width)


def reorder_kernel(mine, x_ref, o_ref):
    o_ref[...] = x_ref[...].astype(F32)


def reorder(x, mine):
    count, rows, width = x.shape
    return pl.pallas_call(
        reorder_kernel,
        out_shape=jax.ShapeDtypeStruct(x.shape, F32),
        grid_spec=pltpu.PrefetchScalarGridSpec(
            num_scalar_prefetch=1,
            grid=(count,),
            in_specs=[
                pl.BlockSpec((1, rows, width), lambda c, mine: (jnp.bitwise_xor(c, mine[0]), 0, 0))
            ],
            out_specs=pl.BlockSpec((1, rows, width), lambda c, mine: (c, 0, 0)),
        ),
        name="reorder",
    )(mine, x)


def reduce_grads(parts, lay, mine):
    core = lax.axis_index("w")
    sends, keeps, heights = [], [], []
    smallest = min(part.size for part in parts) // (2 * lay.count)
    across = 512 if smallest % 512 == 0 else 128
    for part in parts:
        rows, width = part.shape
        halves = part.astype(BF).reshape(2, lay.count, part.size // (2 * lay.count * across), across)
        sends.append(lax.dynamic_index_in_dim(halves, 1 - core, 0, keepdims=False))
        keeps.append(lax.dynamic_index_in_dim(halves, core, 0, keepdims=False))
        heights.append(halves.shape[2])
    send = jnp.concatenate(sends, axis=1)
    keep = jnp.concatenate(keeps, axis=1)
    other = exchange(send, "w", 2, 1)
    both = (keep.astype(F32) + other.astype(F32)).astype(BF)
    pieces = lax.all_to_all(both, lay.axes, 0, 0, tiled=True)
    total = jnp.sum(pieces.astype(F32), axis=0).astype(BF)
    every = reorder(gather_xor(total, lay.axes[::-1], lay), mine)
    out, first = [], 0
    for part, height in zip(parts, heights):
        rows, width = part.shape
        out.append(every[:, first : first + height, :].reshape(rows // 2, width))
        first += height
    return out


def layer_norm(values, gain_vec):
    mean_val = jnp.mean(values, axis=-1, keepdims=True)
    centered = values - mean_val
    variance = jnp.mean(centered * centered, axis=-1, keepdims=True)
    return centered * lax.rsqrt(variance + 1e-05) * gain_vec


def on_device(
    lay, inputs, cotangent, segments, routes, norm_first, w_query, w_keyval, w_router, w_out,
    norm_second, w_up, w_down
):
    def whole(shard):
        return lax.all_gather(shard, "w", axis=0, tiled=True)

    rows, width = inputs.shape[1:]
    head_count = w_router.shape[1]
    head_width = w_keyval.shape[1] // 2
    nb = rows // TB
    group_count = lay.count // INNER
    me = lax.axis_index(lay.inner_axes)
    group = lax.axis_index(lay.outer_axes) if lay.outer_axes else jnp.int32(0)
    place = jnp.stack([me, group]).astype(jnp.int32)
    mine = (group * INNER + me).astype(jnp.int32)[None]

    norm_a, norm_b = whole(norm_first), whole(norm_second)
    query_w, keyval_w, router_w = whole(w_query), whole(w_keyval), whole(w_router)
    out_w, up_w, down_w = whole(w_out), whole(w_up), whole(w_down)

    rows_in = deal(inputs[0], lay).reshape(rows, width).astype(F32)

    spans = rows // (RUN * INNER)
    span_seg = jnp.pad(segments[:, :: RUN * INNER], ((0, 0), (0, 128 - spans)))
    all_seg = gather_xor(span_seg, lay.axes[::-1], lay)[:, 0]
    source = jnp.bitwise_xor(jnp.arange(lay.count, dtype=jnp.int32), mine)
    at = source[:, None] * spans + jnp.arange(128, dtype=jnp.int32)[None]
    at = jnp.where(jnp.arange(128)[None] < spans, at, -1)
    first = jnp.arange(group_count * nb, dtype=jnp.int32) * (UNIT // (RUN * INNER))
    useg = jnp.sum(jnp.where(at[None] == first[:, None, None], all_seg[None], 0), axis=(1, 2))

    code = (routes[0, :, 0] * head_count + routes[0, :, 1]).astype(BF)
    slot_rows = rows // INNER
    code = code.reshape(rows // (RUN * INNER), INNER, RUN).transpose(1, 0, 2)
    code = jnp.pad(code.reshape(INNER, 1, slot_rows), ((0, 0), (0, RUN - 1), (0, width - slot_rows)))
    packed = cotangent[0].reshape(rows // (RUN * INNER), INNER, RUN, width).transpose(1, 0, 2, 3)
    packed = jnp.concatenate([packed.reshape(INNER, slot_rows, width), code], axis=1)
    dealt = lax.all_to_all(packed, lay.inner_axes, 0, 0, tiled=True)
    grad_top = dealt[:, :slot_rows].reshape(rows, width)
    code = dealt[:, slot_rows, :slot_rows].reshape(rows).astype(jnp.int32)
    heads_of = jnp.arange(head_count, dtype=jnp.int32)[None]
    chosen = (code[:, None] // head_count == heads_of) | (code[:, None] % head_count == heads_of)

    normed_f, norm_a_pull = jax.vjp(layer_norm, rows_in, norm_a.astype(F32))
    normed = normed_f.astype(BF)
    keyval = dot(normed, keyval_w).astype(BF)
    half = (nb // 2) * TB
    last = lay.axes[-2:]
    kva = gather_xor(keyval[:half], lay.axes[::-1][2:][::-1] + last[::-1], lay)
    kvb = gather_xor(keyval[half:], lay.axes[::-1][2:][::-1] + last, lay)
    queries = dot(normed, query_w).astype(BF)
    attended, ot, low, qt = attention_forward(
        useg, place, kva, kvb, queries, head_count, head_width
    )

    logits = dot(normed, router_w)
    lifted = jnp.where(chosen, logits, -1e30)
    raised = jnp.where(chosen, jnp.exp(lifted - jnp.max(lifted, axis=-1, keepdims=True)), 0.0)
    gate_vals = raised / jnp.sum(raised, axis=-1, keepdims=True)
    spread = (
        jnp.arange(head_count * head_width)[None] // head_width == jnp.arange(head_count)[:, None]
    ).astype(F32)
    gates = jnp.dot(gate_vals, spread, precision=lax.Precision.HIGHEST)

    mixed_in = (gates * attended).astype(BF)
    middle = rows_in + dot(mixed_in, out_w)
    normed_bf, norm_b_pull = jax.vjp(layer_norm, middle, norm_b.astype(F32))
    normed_b = normed_bf.astype(BF)
    pre_act = dot(normed_b, up_w)
    hidden_f, gelu_pull = jax.vjp(functools.partial(jax.nn.gelu, approximate=True), pre_act)
    hidden = hidden_f.astype(BF)
    result = (middle + dot(hidden, down_w)).astype(BF)
    output = undeal(result, lay)[None]
    down_grad = inner(hidden, grad_top)
    pre_grad = gelu_pull(outer(grad_top, down_w))[0].astype(BF)
    up_grad = inner(normed_b, pre_grad)
    middle_norm, norm_b_grad = norm_b_pull(outer(pre_grad, up_w))
    middle_grad = grad_top.astype(F32) + middle_norm
    branch_grad = middle_grad.astype(BF)
    out_grad = inner(mixed_in, branch_grad)
    mixed_grad = outer(branch_grad, out_w)
    gate_grad = lax.dot_general(
        mixed_grad * attended, spread, (((1,), (1,)), ((), ())), precision=lax.Precision.HIGHEST
    )
    logit_grad = gate_vals * (gate_grad - jnp.sum(gate_vals * gate_grad, axis=-1, keepdims=True))
    att_grad = (gates * mixed_grad).astype(BF)

    up_sum, down_sum, out_sum = reduce_grads([up_grad, down_grad, out_grad], lay, mine)

    query_grad, dkv = attention_backward(
        useg, place, kva, kvb, qt, ot, low, att_grad, head_count, head_width
    )
    dkv = lax.all_to_all(dkv, lay.axes, 0, 0, tiled=True)
    keyval_grad = jnp.sum(dkv.astype(F32), axis=0).astype(BF)

    logit_low = logit_grad.astype(BF)
    query_w_grad = inner(normed, query_grad)
    keyval_w_grad = inner(normed, keyval_grad)
    router_grad = inner(normed, logit_low)
    normed_grad = (
        outer(query_grad, query_w) + outer(keyval_grad, keyval_w) + outer(logit_low, router_w)
    )
    input_norm, norm_a_grad = norm_a_pull(normed_grad)
    input_grad = undeal((middle_grad + input_norm).astype(BF), lay).astype(F32)[None]

    small = jnp.concatenate([router_grad, norm_a_grad[:, None], norm_b_grad[:, None]], axis=1)
    small = jnp.pad(small, ((0, 0), (0, 128 - small.shape[1])))
    query_sum, keyval_sum, small_sum = reduce_grads(
        [query_w_grad, keyval_w_grad, small], lay, mine
    )
    return (
        output,
        input_grad,
        small_sum[:, head_count],
        query_sum,
        keyval_sum,
        small_sum[:, :head_count],
        out_sum,
        small_sum[:, head_count + 1],
        up_sum,
        down_sum,
    )


def solution(mesh):
    ctx_count, core_count = mesh.shape["ctx"], mesh.shape["wshard"]
    lay = Layout(ctx_count)
    grid = Mesh(mesh.devices.reshape(lay.sizes + (core_count,)), lay.axes + ("w",))
    ctx = lay.axes
    tokens = P("w", ctx, None)
    return jax.shard_map(
        functools.partial(on_device, lay),
        mesh=grid,
        in_specs=(
            tokens, tokens, P("w", ctx), tokens,
            P("w"), P("w", None), P("w", None), P("w", None), P("w", None),
            P("w"), P("w", None), P("w", None),
        ),
        out_specs=(
            tokens, tokens,
            P("w"), P("w", None), P("w", None), P("w", None), P("w", None),
            P("w"), P("w", None), P("w", None),
        ),
        check_vma=False,
    )
```

```python
import functools
import math

import jax
import jax.numpy as jnp
from jax import lax
from jax.experimental import pallas as pl
from jax.experimental.pallas import tpu as pltpu
from jax.sharding import Mesh, PartitionSpec as P

F32 = jnp.float32
BF = jnp.bfloat16
UNIT = 1024
TB = 64
INNER = UNIT // TB
RUN = 8
LOG2E = 1.4426950408889634
BIG = 2.0**100


def dot(lhs, rhs):
    return lax.dot_general(lhs, rhs, (((1,), (0,)), ((), ())), preferred_element_type=F32)


def inner(lhs, rhs):
    return lax.dot_general(lhs, rhs, (((0,), (0,)), ((), ())), preferred_element_type=F32)


def outer(lhs, rhs):
    return lax.dot_general(lhs, rhs, (((1,), (1,)), ((), ())), preferred_element_type=F32)


def split3(x):
    a = x.astype(BF)
    rest = x - a.astype(F32)
    b = rest.astype(BF)
    return a, b, (rest - b.astype(F32)).astype(BF)


def to_lanes(x, heads, hw):
    xt = x.T
    return jnp.concatenate([xt[h * hw : (h + 1) * hw] for h in range(heads)], axis=1)


def key_offsets(index, me):
    owner = jnp.bitwise_xor(index >> 6, me)
    rest = index & (TB - 1)
    return (rest >> 3) * (RUN * INNER) + owner * RUN + (rest & 7)


def query_offsets(index, me):
    rest = index & (TB - 1)
    return (rest >> 3) * (RUN * INNER) + me * RUN + (rest & 7)


def unit_rows(ref, where, slot, part):
    pieces = [
        ref[where[slot * INNER + k], part * TB : (part + 1) * TB, :] for k in range(INNER)
    ]
    return jnp.concatenate(pieces, axis=0)


def fwd_kernel(
    useg, place, kva_ref, kvb_ref, q_ref, o_ref, ot_ref, l_ref, qt_ref, kaug, vt,
    qa, acc, ref_row, plist, rank, bad, *, nb, slots, heads, hw, tables
):
    me, group = place[0], place[1]
    scale = LOG2E / math.sqrt(hw)
    lanes = heads * TB
    units = slots * nb

    def scan(u, n):
        rank[u] = n
        plist[n] = jnp.bitwise_xor(u // nb, group) * nb + u % nb
        return n + jnp.where(useg[u] == 0, 1, 0)

    prompt_units = lax.fori_loop(0, units, scan, jnp.int32(0))
    lane = lax.broadcasted_iota(jnp.int32, (UNIT, 2 * hw), 1)
    row = lax.broadcasted_iota(jnp.int32, (2 * hw, UNIT), 0)
    extra = jnp.where(lane < hw + 3, 1.0, 0.0).astype(BF)
    for slot in range(slots):
        for part in range(nb):
            rel = slot * nb + part
            half = nb // 2
            if part < half:
                tile = unit_rows(kva_ref, tables[0], slot, part)
            else:
                tile = unit_rows(kvb_ref, tables[1], slot, part - half)
            kaug[rel] = jnp.where(lane < hw, tile, extra)
            flip = tile.T
            vt[rel] = jnp.where(row < hw, jnp.ones_like(flip), flip)

    def block(i, carry):
        own = group * nb + i
        full_units = jnp.where(useg[own] != 0, prompt_units, rank[own])
        rows = pl.ds(pl.multiple_of(i * TB, TB), TB)
        qt = to_lanes(q_ref[rows, :], heads, hw)
        qt_ref[i] = qt
        qa[0:hw, :] = qt
        qa[hw:, :] = jnp.zeros((hw, lanes), BF)
        mask = key_offsets(
            lax.broadcasted_iota(jnp.int32, (UNIT, lanes), 0), me
        ) <= query_offsets(lax.broadcasted_iota(jnp.int32, (UNIT, lanes), 1), me)
        ref_row[...] = jnp.max(
            jnp.where(mask, dot(kaug[i], qa[...]), -1e30), axis=0, keepdims=True
        )
        bad[0] = 1

        def attempt(turn, carry):
            @pl.when(bad[0] != 0)
            def _():
                @pl.when(turn == 1)
                def _():
                    qa[hw:, :] = jnp.zeros((hw, lanes), BF)

                    def highest(k, carry):
                        ref_row[...] = jnp.maximum(
                            ref_row[...],
                            jnp.max(dot(kaug[plist[k]], qa[...]), axis=0, keepdims=True),
                        )
                        return carry

                    lax.fori_loop(0, full_units, highest, 0)

                a, b, c = split3(-ref_row[...])
                qa[hw:, :] = jnp.concatenate([a, b, c, jnp.zeros((hw - 3, lanes), BF)], axis=0)
                s = jnp.where(mask, dot(kaug[i], qa[...]) * scale, -1e30)
                acc[...] = dot(vt[i], jnp.exp2(s).astype(BF))

                def full(k, carry):
                    u = plist[k]
                    p = jnp.exp2(dot(kaug[u], qa[...]) * scale).astype(BF)
                    acc[...] += dot(vt[u], p)
                    return carry

                lax.fori_loop(0, full_units, full, 0)
                bad[0] = jnp.where(jnp.max(acc[0:1, :]) < BIG, 0, 1)

            return carry

        lax.fori_loop(0, 2, attempt, 0)
        ot = acc[hw:, :] / acc[0:hw, :]
        ot_ref[i] = ot
        l_ref[i] = ref_row[...] + jnp.log2(acc[0:1, :]) / scale
        on = jnp.concatenate([ot[:, h * TB : (h + 1) * TB] for h in range(heads)], axis=0)
        o_ref[rows, :] = on.T
        return carry

    lax.fori_loop(0, nb, block, 0)


def attention_forward(useg, place, kva, kvb, q, heads, hw, tables):
    rows = q.shape[0]
    nb = rows // TB
    slots = kva.shape[0] // INNER
    lanes = heads * TB
    units = slots * nb
    vm = pl.BlockSpec(memory_space=pltpu.VMEM)
    sm = pl.BlockSpec(memory_space=pltpu.SMEM)
    return pl.pallas_call(
        functools.partial(fwd_kernel, nb=nb, slots=slots, heads=heads, hw=hw, tables=tables),
        out_shape=(
            jax.ShapeDtypeStruct((rows, heads * hw), F32),
            jax.ShapeDtypeStruct((nb, hw, lanes), F32),
            jax.ShapeDtypeStruct((nb, 1, lanes), F32),
            jax.ShapeDtypeStruct((nb, hw, lanes), BF),
            jax.ShapeDtypeStruct((units, UNIT, 2 * hw), BF),
            jax.ShapeDtypeStruct((units, 2 * hw, UNIT), BF),
        ),
        in_specs=[sm, sm, vm, vm, vm],
        out_specs=(vm,) * 6,
        scratch_shapes=[
            pltpu.VMEM((2 * hw, lanes), BF),
            pltpu.VMEM((2 * hw, lanes), F32),
            pltpu.VMEM((1, lanes), F32),
            pltpu.SMEM((units + 1,), jnp.int32),
            pltpu.SMEM((units + 1,), jnp.int32),
            pltpu.SMEM((1,), jnp.int32),
        ],
        compiler_params=pltpu.CompilerParams(vmem_limit_bytes=60 << 20),
        cost_estimate=pl.CostEstimate(
            flops=40 * 10**9, bytes_accessed=8 << 20, transcendentals=26 * 10**6
        ),
        name="attention_forward",
    )(useg, place, kva, kvb, q)


def prepare_kernel(qt_ref, ot_ref, l_ref, do_ref, qa_ref, doa_ref, dot_ref, *, nb, heads, hw):
    pad = jnp.zeros((hw - 3, heads * TB), BF)

    def prepare(i, carry):
        rows = pl.ds(pl.multiple_of(i * TB, TB), TB)
        a, b, c = split3(-l_ref[i])
        qa_ref[i] = jnp.concatenate([qt_ref[i], a, b, c, pad], axis=0).T
        dt = to_lanes(do_ref[rows, :], heads, hw)
        dot_ref[i] = dt
        total = jnp.sum(dt.astype(F32) * ot_ref[i], axis=0, keepdims=True)
        a, b, c = split3(-total)
        doa_ref[i] = jnp.concatenate([a, b, c, pad, dt], axis=0).T
        return carry

    lax.fori_loop(0, nb, prepare, 0)


def attention_prepare(qt, ot, low, do, heads, hw):
    nb, _, lanes = qt.shape
    vm = pl.BlockSpec(memory_space=pltpu.VMEM)
    return pl.pallas_call(
        functools.partial(prepare_kernel, nb=nb, heads=heads, hw=hw),
        out_shape=(
            jax.ShapeDtypeStruct((nb, lanes, 2 * hw), BF),
            jax.ShapeDtypeStruct((nb, lanes, 2 * hw), BF),
            jax.ShapeDtypeStruct((nb, hw, lanes), BF),
        ),
        in_specs=[vm] * 4,
        out_specs=(vm,) * 3,
        compiler_params=pltpu.CompilerParams(vmem_limit_bytes=40 << 20),
        cost_estimate=pl.CostEstimate(flops=10**9, bytes_accessed=8 << 20, transcendentals=0),
        name="attention_prepare",
    )(qt, ot, low, do)


def bwd_kernel(
    useg, place, kaug_ref, vt_ref, qa, doa, qt, dot_t, *rest, nb, parts, first, last, heads, hw
):
    if first:
        dqacc, dkv_ref, kt, dkvt = rest
    elif last:
        dqold, dq_ref, dkv_ref, dqacc, kt, dkvt = rest
    else:
        dqold, dqacc, dkv_ref, kt, dkvt = rest
    step_at = pl.program_id(0)
    me, group = place[0], place[1]
    slot, part = step_at // len(parts), step_at % len(parts) + parts[0]
    unit = jnp.bitwise_xor(slot, group) * nb + part
    scale = LOG2E / math.sqrt(hw)
    lanes = heads * TB

    @pl.when(step_at == 0)
    def _():
        dqacc[...] = jnp.zeros_like(dqacc) if first else dqold[...]

    kt[...] = kaug_ref[0].T
    dkvt[...] = jnp.zeros_like(dkvt)
    unit_seg = useg[unit]

    def block(i, carry):
        own = group * nb + i

        def step(masked):
            s = dot(qa[i], kt[...]) * scale
            if masked:
                mask = key_offsets(
                    lax.broadcasted_iota(jnp.int32, (lanes, UNIT), 1), me
                ) <= query_offsets(lax.broadcasted_iota(jnp.int32, (lanes, UNIT), 0), me)
                s = jnp.where(mask, s, -1e30)
            p = jnp.exp2(s)
            ds = (p * dot(doa[i], vt_ref[0])).astype(BF)
            dkvt[hw:, :] += dot(dot_t[i], p.astype(BF))
            dkvt[:hw, :] += dot(qt[i], ds)
            dqacc[i] += dot(ds, kaug_ref[0])

        @pl.when((unit_seg == 0) & (own != unit) & ((useg[own] != 0) | (own > unit)))
        def _():
            step(False)

        @pl.when(own == unit)
        def _():
            step(True)

        return carry

    lax.fori_loop(0, nb, block, 0)
    factor = jnp.where(
        lax.broadcasted_iota(jnp.int32, (2 * hw, 1), 0) < hw, 1 / math.sqrt(hw), 1.0
    )
    dkv = (dkvt[...] * factor).astype(BF).T
    for s in range(INNER):
        dkv_ref[jnp.bitwise_xor(me, s)] = dkv[s * TB : (s + 1) * TB, :]

    if last:
        @pl.when(step_at == pl.num_programs(0) - 1)
        def _():
            def finish(i, carry):
                rows = pl.ds(pl.multiple_of(i * TB, TB), TB)
                a = dqacc[i]
                dq_ref[rows, :] = (
                    jnp.concatenate([a[h * TB : (h + 1) * TB, :hw] for h in range(heads)], axis=1)
                    * (1 / math.sqrt(hw))
                ).astype(BF)
                return carry

            lax.fori_loop(0, nb, finish, 0)


def attention_backward(useg, place, kaug, vt, qa, doa, qt, dot_t, dqold, parts, heads, hw):
    nb, lanes, _ = qa.shape
    slots = kaug.shape[0] // nb
    first, last = dqold is None, parts[-1] == nb - 1
    vm = pl.BlockSpec(memory_space=pltpu.VMEM)
    acc_shape = jax.ShapeDtypeStruct((nb, lanes, 2 * hw), F32)
    count = len(parts)

    def at(u, seg, place):
        return (u // count * nb + u % count + parts[0], 0, 0)

    return pl.pallas_call(
        functools.partial(
            bwd_kernel, nb=nb, parts=parts, first=first, last=last, heads=heads, hw=hw
        ),
        out_shape=(
            jax.ShapeDtypeStruct((nb * TB, heads * hw), BF) if last else acc_shape,
            jax.ShapeDtypeStruct((slots * INNER, count * TB, 2 * hw), BF),
        ),
        grid_spec=pltpu.PrefetchScalarGridSpec(
            num_scalar_prefetch=2,
            grid=(slots * count,),
            in_specs=[
                pl.BlockSpec((1, UNIT, 2 * hw), at),
                pl.BlockSpec((1, 2 * hw, UNIT), at),
            ]
            + [vm] * (4 if first else 5),
            out_specs=(
                vm,
                pl.BlockSpec(
                    (INNER, TB, 2 * hw),
                    lambda u, seg, place: (jnp.bitwise_xor(u // count, place[1]), u % count, 0),
                ),
            ),
            scratch_shapes=([pltpu.VMEM(acc_shape.shape, F32)] if last and not first else [])
            + [
                pltpu.VMEM((2 * hw, UNIT), BF),
                pltpu.VMEM((2 * hw, UNIT), F32),
            ],
        ),
        compiler_params=pltpu.CompilerParams(vmem_limit_bytes=60 << 20),
        cost_estimate=pl.CostEstimate(
            flops=8 * 10**9 * count, bytes_accessed=12 << 20, transcendentals=2 * 10**6 * count
        ),
        name="attention_backward",
    )(useg, place, kaug, vt, qa, doa, qt, dot_t, *([] if first else [dqold]))


class Layout:
    def __init__(self, ctx_count):
        sizes = [4]
        while math.prod(sizes) < ctx_count:
            sizes.append(2)
        assert math.prod(sizes) == ctx_count
        self.sizes = tuple(sizes)
        self.axes = tuple(f"c{k}" for k in range(len(sizes)))
        cut = len(sizes)
        while math.prod(sizes[cut:]) < INNER:
            cut -= 1
        assert math.prod(sizes[cut:]) == INNER
        self.outer_axes, self.inner_axes = self.axes[:cut], self.axes[cut:]
        self.count = ctx_count


def exchange(x, axis, size, step):
    return lax.ppermute(x, axis, [(i, i ^ step) for i in range(size)])


def spread(x, order, lay, start=0, stop=None):
    for axis in order[start:stop]:
        size = lay.sizes[lay.axes.index(axis)]
        x = jnp.concatenate([x] + [exchange(x, axis, size, step) for step in range(1, size)])
    return x


def positions(order, lay):
    found = [0] * lay.count
    for index in range(lay.count):
        rest, digit = index, {}
        for axis in order:
            size = lay.sizes[lay.axes.index(axis)]
            digit[axis] = rest % size
            rest //= size
        s = 0
        for axis, size in zip(lay.axes, lay.sizes):
            s = s * size + digit[axis]
        found[s] = index
    return found


def deal(x, lay):
    rows, width = x.shape
    packed = x.reshape(rows // (RUN * INNER), INNER, RUN, width).transpose(1, 0, 2, 3)
    packed = packed.reshape(INNER, rows // INNER, width)
    return lax.all_to_all(packed, lay.inner_axes, 0, 0, tiled=True)


def undeal(x, lay):
    rows, width = x.shape
    back = lax.all_to_all(
        x.reshape(INNER, rows // INNER, width), lay.inner_axes, 0, 0, tiled=True
    )
    back = back.reshape(INNER, rows // (RUN * INNER), RUN, width).transpose(1, 0, 2, 3)
    return back.reshape(rows, width)


def tie(*values):
    return lax.optimization_barrier(values)


def pack_half(part, lay, across):
    core = lax.axis_index("w")
    rows, width = part.shape
    piece = rows // 2 // lay.count
    halves = part.astype(BF).reshape(2, lay.count, piece, width // across, across)
    halves = halves.transpose(0, 1, 3, 2, 4).reshape(2, lay.count, -1, across)
    return (
        lax.dynamic_index_in_dim(halves, core, 0, keepdims=False),
        lax.dynamic_index_in_dim(halves, 1 - core, 0, keepdims=False),
    )


def core_sum(parts, lay, across):
    packed = [pack_half(part, lay, across) for part in parts]
    keep = jnp.concatenate([p[0] for p in packed], axis=1)
    send = jnp.concatenate([p[1] for p in packed], axis=1)
    other = exchange(send, "w", 2, 1)
    return (keep.astype(F32) + other.astype(F32)).astype(BF)


def swap_pieces(both, lay):
    return lax.all_to_all(both, lay.axes, 0, 0, tiled=True)


def add_pieces(pieces):
    return jnp.sum(pieces.astype(F32), axis=0).astype(BF)


def place_kernel(where, x_ref, *outs, count, across):
    for c in range(count):
        at = where[c]
        first = 0
        for out in outs:
            piece = out.shape[0] // count
            for k in range(out.shape[1] // across):
                out[c * piece : (c + 1) * piece, k * across : (k + 1) * across] = x_ref[
                    at, first : first + piece, :
                ].astype(F32)
                first += piece


def place_pieces(every, where, shapes, across):
    vm = pl.BlockSpec(memory_space=pltpu.VMEM)
    return pl.pallas_call(
        functools.partial(place_kernel, count=every.shape[0], across=across),
        out_shape=tuple(jax.ShapeDtypeStruct(shape, F32) for shape in shapes),
        in_specs=[pl.BlockSpec(memory_space=pltpu.SMEM), vm],
        out_specs=(vm,) * len(shapes),
        compiler_params=pltpu.CompilerParams(vmem_limit_bytes=40 << 20),
        cost_estimate=pl.CostEstimate(
            flops=0, bytes_accessed=3 * every.size * 2, transcendentals=0
        ),
        name="place_pieces",
    )(where, every)


def sum_all(x, lay):
    for axis, size in zip(lay.axes, lay.sizes):
        terms = [x.astype(F32)] + [
            exchange(x, axis, size, step).astype(F32) for step in range(1, size)
        ]
        while len(terms) > 1:
            terms = [terms[k] + terms[k + 1] for k in range(0, len(terms), 2)]
        x = terms[0].astype(BF)
    return x


def layer_norm(values, gain_vec):
    mean_val = jnp.mean(values, axis=-1, keepdims=True)
    centered = values - mean_val
    variance = jnp.mean(centered * centered, axis=-1, keepdims=True)
    return centered * lax.rsqrt(variance + 1e-05) * gain_vec


def on_device(
    lay, inputs, cotangent, segments, routes, norm_first, w_query, w_keyval, w_router, w_out,
    norm_second, w_up, w_down
):
    def whole(shard):
        return lax.all_gather(shard, "w", axis=0, tiled=True)

    rows, width = inputs.shape[1:]
    head_count = w_router.shape[1]
    head_width = w_keyval.shape[1] // 2
    nb = rows // TB
    group_count = lay.count // INNER
    me = lax.axis_index(lay.inner_axes)
    group = lax.axis_index(lay.outer_axes) if lay.outer_axes else jnp.int32(0)
    place = jnp.stack([me, group]).astype(jnp.int32)
    mine = (group * INNER + me).astype(jnp.int32)[None]

    head_of = jnp.arange(head_count, dtype=jnp.int32)[None]
    order_a = lay.axes[:1] + lay.axes[1:][::-1]
    order_b = lay.axes
    tables = (positions(order_a, lay), positions(order_b, lay))
    from_me = jnp.bitwise_xor(jnp.arange(lay.count, dtype=jnp.int32), mine)
    where_b = jnp.array(tables[1], jnp.int32)[from_me]

    rows_in = deal(inputs[0], lay).reshape(rows, width).astype(F32)
    narrow = whole(
        jnp.concatenate([w_router, norm_first[:, None], norm_second[:, None]], axis=1)
    )
    router_w = narrow[:, :head_count]
    norm_a, norm_b = narrow[:, head_count], narrow[:, head_count + 1]
    query_w, keyval_w = whole(w_query), whole(w_keyval)
    out_w, up_w, down_w = whole(w_out), whole(w_up), whole(w_down)

    spans = rows // (RUN * INNER)
    span_seg = jnp.pad(segments[:, :: RUN * INNER], ((0, 0), (0, 128 - spans)))
    span_seg, rows_in = tie(span_seg, rows_in)
    all_seg = spread(span_seg, order_b, lay)
    source = jnp.zeros((lay.count,), jnp.int32).at[jnp.array(tables[1])].set(from_me)
    at = source[:, None] * spans + jnp.arange(128, dtype=jnp.int32)[None]
    at = jnp.where(jnp.arange(128)[None] < spans, at, -1)
    first = jnp.arange(group_count * nb, dtype=jnp.int32) * (UNIT // (RUN * INNER))
    useg = jnp.sum(jnp.where(at[None] == first[:, None, None], all_seg[None], 0), axis=(1, 2))

    normed_f, norm_a_pull = jax.vjp(layer_norm, rows_in, norm_a.astype(F32))
    normed = normed_f.astype(BF)
    keyval = dot(normed, keyval_w).astype(BF)
    half = (nb // 2) * TB
    near = spread(keyval[None], order_b, lay, 0, 1)
    kva = spread(near[:, :half], order_a, lay, 1)
    kvb = spread(near[:, half:], order_b, lay, 1)
    queries = dot(normed, query_w).astype(BF)

    code = (routes[0, :, 0] * head_count + routes[0, :, 1]).astype(BF)
    slot_rows = rows // INNER
    code = code.reshape(rows // (RUN * INNER), INNER, RUN).transpose(1, 0, 2)
    code = jnp.pad(code.reshape(INNER, 1, slot_rows), ((0, 0), (0, RUN - 1), (0, width - slot_rows)))
    packed = cotangent[0].reshape(rows // (RUN * INNER), INNER, RUN, width).transpose(1, 0, 2, 3)
    packed = jnp.concatenate([packed.reshape(INNER, slot_rows, width), code], axis=1)
    packed, kva, kvb = tie(packed, kva, kvb)
    dealt = lax.all_to_all(packed, lay.inner_axes, 0, 0, tiled=True)
    attended, ot, low, qt, kaug, vt = attention_forward(
        useg, place, kva, kvb, queries, head_count, head_width, tables
    )
    attended, dealt = tie(attended, dealt)
    grad_top = dealt[:, :slot_rows].reshape(rows, width)
    code = dealt[:, slot_rows, :slot_rows].reshape(rows).astype(jnp.int32)
    chosen = (code[:, None] // head_count == head_of) | (code[:, None] % head_count == head_of)

    logits = dot(normed, router_w)
    lifted = jnp.where(chosen, logits, -1e30)
    raised = jnp.where(chosen, jnp.exp(lifted - jnp.max(lifted, axis=-1, keepdims=True)), 0.0)
    gate_vals = raised / jnp.sum(raised, axis=-1, keepdims=True)
    widen = (
        jnp.arange(head_count * head_width)[None] // head_width == jnp.arange(head_count)[:, None]
    ).astype(F32)
    gates = jnp.dot(gate_vals, widen, precision=lax.Precision.HIGHEST)

    mixed_in = (gates * attended).astype(BF)
    middle = rows_in + dot(mixed_in, out_w)
    normed_bf, norm_b_pull = jax.vjp(layer_norm, middle, norm_b.astype(F32))
    normed_b = normed_bf.astype(BF)
    pre_act = dot(normed_b, up_w)
    hidden_f, gelu_pull = jax.vjp(functools.partial(jax.nn.gelu, approximate=True), pre_act)
    hidden = hidden_f.astype(BF)
    result = (middle + dot(hidden, down_w)).astype(BF)
    down_grad = inner(hidden, grad_top)
    pre_grad = gelu_pull(outer(grad_top, down_w))[0].astype(BF)
    up_grad = inner(normed_b, pre_grad)
    middle_norm, norm_b_grad = norm_b_pull(outer(pre_grad, up_w))
    middle_grad = grad_top.astype(F32) + middle_norm
    branch_grad = middle_grad.astype(BF)
    out_grad = inner(mixed_in, branch_grad)
    mixed_grad = outer(branch_grad, out_w)
    gate_grad = lax.dot_general(
        mixed_grad * attended, widen, (((1,), (1,)), ((), ())), precision=lax.Precision.HIGHEST
    )
    logit_grad = gate_vals * (gate_grad - jnp.sum(gate_vals * gate_grad, axis=-1, keepdims=True))
    att_grad = (gates * mixed_grad).astype(BF)

    qa, doa, dot_t = attention_prepare(qt, ot, low, att_grad, head_count, head_width)
    both = core_sum([up_grad, down_grad, out_grad], lay, 512)
    both, qa, result = tie(both, qa, result)
    output = undeal(result, lay)
    pieces = swap_pieces(both, lay)

    cuts = (0, nb // 2, nb - nb // 5, nb)
    dq, dkv_sums, waiting = None, [], None
    for turn in range(3):
        parts = tuple(range(cuts[turn], cuts[turn + 1]))
        dq, dkv = attention_backward(
            useg, place, kaug, vt, qa, doa, qt, dot_t, dq, parts, head_count, head_width
        )
        if turn == 0:
            dq, dkv, output, pieces = tie(dq, dkv, output, pieces)
            total = add_pieces(pieces)
            near = spread(total[None], order_b, lay, 0, 1)
        elif turn == 1:
            dq, dkv, waiting, near = tie(dq, dkv, waiting, near)
            every = spread(near, order_b, lay, 1, 2)
        else:
            dq, dkv, waiting, every = tie(dq, dkv, waiting, every)
            every = spread(every, order_b, lay, 2)
        if waiting is not None:
            dkv_sums.append(add_pieces(waiting))
        waiting = swap_pieces(dkv, lay)
    query_grad = dq
    dkv_sums.append(add_pieces(waiting))
    keyval_grad = jnp.concatenate(dkv_sums, axis=0)
    up_sum, down_sum, out_sum = place_pieces(
        every, where_b, [w_up.shape, w_down.shape, w_out.shape], 512
    )

    logit_low = logit_grad.astype(BF)
    query_w_grad = inner(normed, query_grad)
    keyval_w_grad = inner(normed, keyval_grad)
    router_grad = inner(normed, logit_low)
    normed_grad = (
        outer(query_grad, query_w) + outer(keyval_grad, keyval_w) + outer(logit_low, router_w)
    )
    input_norm, norm_a_grad = norm_a_pull(normed_grad)
    input_grad = undeal((middle_grad + input_norm).astype(BF), lay).astype(F32)[None]

    query_both = core_sum([query_w_grad], lay, 128)
    query_every = spread(add_pieces(swap_pieces(query_both, lay))[None], order_b, lay)
    (query_sum,) = place_pieces(query_every, where_b, [w_query.shape], 128)
    small = jnp.concatenate(
        [keyval_w_grad, router_grad, norm_a_grad[:, None], norm_b_grad[:, None]], axis=1
    )
    small = jnp.pad(small, ((0, 0), (0, -small.shape[1] % 128))).astype(BF)
    small = small.reshape(2, width // 2, -1)
    core = lax.axis_index("w")
    keep = lax.dynamic_index_in_dim(small, core, 0, keepdims=False).astype(F32)
    other = exchange(lax.dynamic_index_in_dim(small, 1 - core, 0, keepdims=False), "w", 2, 1)
    small = sum_all((keep + other.astype(F32)).astype(BF), lay).astype(F32)
    kv_width = 2 * head_width
    keyval_sum, small_sum = small[:, :kv_width], small[:, kv_width:]
    return (
        output[None],
        input_grad,
        small_sum[:, head_count],
        query_sum,
        keyval_sum,
        small_sum[:, :head_count],
        out_sum,
        small_sum[:, head_count + 1],
        up_sum,
        down_sum,
    )


def solution(mesh):
    ctx_count, core_count = mesh.shape["ctx"], mesh.shape["wshard"]
    lay = Layout(ctx_count)
    grid = Mesh(mesh.devices.reshape(lay.sizes + (core_count,)), lay.axes + ("w",))
    ctx = lay.axes
    tokens = P("w", ctx, None)
    return jax.shard_map(
        functools.partial(on_device, lay),
        mesh=grid,
        in_specs=(
            tokens, tokens, P("w", ctx), tokens,
            P("w"), P("w", None), P("w", None), P("w", None), P("w", None),
            P("w"), P("w", None), P("w", None),
        ),
        out_specs=(
            tokens, tokens,
            P("w"), P("w", None), P("w", None), P("w", None), P("w", None),
            P("w"), P("w", None), P("w", None),
        ),
        check_vma=False,
    )
```

```python
import functools
import math

import jax
import jax.numpy as jnp
from jax import lax
from jax.experimental import pallas as pl
from jax.experimental.pallas import tpu as pltpu
from jax.sharding import Mesh, PartitionSpec as P

F32 = jnp.float32
BF = jnp.bfloat16
UNIT = 1024
TB = 64
INNER = UNIT // TB
RUN = 8
LOG2E = 1.4426950408889634
BIG = 2.0**100


def dot(lhs, rhs):
    return lax.dot_general(lhs, rhs, (((1,), (0,)), ((), ())), preferred_element_type=F32)


def inner(lhs, rhs):
    return lax.dot_general(lhs, rhs, (((0,), (0,)), ((), ())), preferred_element_type=F32)


def outer(lhs, rhs):
    return lax.dot_general(lhs, rhs, (((1,), (1,)), ((), ())), preferred_element_type=F32)


def split3(x):
    a = x.astype(BF)
    rest = x - a.astype(F32)
    b = rest.astype(BF)
    return a, b, (rest - b.astype(F32)).astype(BF)


def to_lanes(x, heads, hw):
    xt = x.T
    return jnp.concatenate([xt[h * hw : (h + 1) * hw] for h in range(heads)], axis=1)


def key_offsets(index, me):
    owner = jnp.bitwise_xor(index >> 6, me)
    rest = index & (TB - 1)
    return (rest >> 3) * (RUN * INNER) + owner * RUN + (rest & 7)


def query_offsets(index, me):
    rest = index & (TB - 1)
    return (rest >> 3) * (RUN * INNER) + me * RUN + (rest & 7)


def near_index(rest, sizes):
    digits = []
    for size in sizes[::-1]:
        digits.append(rest % size)
        rest = rest // size
    index = 0
    for digit, size in zip(digits, sizes[::-1]):
        index = index * size + digit
    return index


def piece_of(pieces, s, first, count, sizes, cut):
    near, near_x, near_y, far_a, far_b = pieces
    index = near_index(s // 4, sizes)
    ref = (near, near_x, near_y)[s % 4] if s % 4 < 3 else (far_a if first < cut else far_b)
    if s % 4 == 3 and first >= cut:
        first -= cut
    return ref[index, first : first + count, :]


def fwd_kernel(
    useg, place, near, near_x, near_y, far_a, far_b, q_ref, o_ref, ot_ref, l_ref, qt_ref, kaug, vt,
    qa, acc, ref_row, plist, rank, bad, *, nb, slots, heads, hw, sizes
):
    me, group = place[0], place[1]
    scale = LOG2E / math.sqrt(hw)
    lanes = heads * TB
    units = slots * nb

    def scan(u, n):
        rank[u] = n
        plist[n] = jnp.bitwise_xor(u // nb, group) * nb + u % nb
        return n + jnp.where(useg[u] == 0, 1, 0)

    prompt_units = lax.fori_loop(0, units, scan, jnp.int32(0))
    lane = lax.broadcasted_iota(jnp.int32, (UNIT, 2 * hw), 1)
    row = lax.broadcasted_iota(jnp.int32, (2 * hw, UNIT), 0)
    extra = jnp.where(lane < hw + 3, 1.0, 0.0).astype(BF)
    for slot in range(slots):
        for part in range(nb):
            rel = slot * nb + part
            tile = jnp.concatenate(
                [
                    piece_of(
                        (near, near_x, near_y, far_a, far_b),
                        slot * INNER + k, part * TB, TB, sizes, nb // 2 * TB,
                    )
                    for k in range(INNER)
                ],
                axis=0,
            )
            kaug[rel] = jnp.where(lane < hw, tile, extra)
            flip = tile.T
            vt[rel] = jnp.where(row < hw, jnp.ones_like(flip), flip)

    def block(i, carry):
        own = group * nb + i
        full_units = jnp.where(useg[own] != 0, prompt_units, rank[own])
        rows = pl.ds(pl.multiple_of(i * TB, TB), TB)
        qt = to_lanes(q_ref[rows, :], heads, hw)
        qt_ref[i] = qt
        qa[0:hw, :] = qt
        qa[hw:, :] = jnp.zeros((hw, lanes), BF)
        mask = key_offsets(
            lax.broadcasted_iota(jnp.int32, (UNIT, lanes), 0), me
        ) <= query_offsets(lax.broadcasted_iota(jnp.int32, (UNIT, lanes), 1), me)
        ref_row[...] = jnp.max(
            jnp.where(mask, dot(kaug[i], qa[...]), -1e30), axis=0, keepdims=True
        )
        bad[0] = 1

        def attempt(turn, carry):
            @pl.when(bad[0] != 0)
            def _():
                @pl.when(turn == 1)
                def _():
                    qa[hw:, :] = jnp.zeros((hw, lanes), BF)

                    def highest(k, carry):
                        ref_row[...] = jnp.maximum(
                            ref_row[...],
                            jnp.max(dot(kaug[plist[k]], qa[...]), axis=0, keepdims=True),
                        )
                        return carry

                    lax.fori_loop(0, full_units, highest, 0)

                a, b, c = split3(-ref_row[...])
                qa[hw:, :] = jnp.concatenate([a, b, c, jnp.zeros((hw - 3, lanes), BF)], axis=0)
                s = jnp.where(mask, dot(kaug[i], qa[...]) * scale, -1e30)
                acc[...] = dot(vt[i], jnp.exp2(s).astype(BF))

                def full(k, carry):
                    u = plist[k]
                    p = jnp.exp2(dot(kaug[u], qa[...]) * scale).astype(BF)
                    acc[...] += dot(vt[u], p)
                    return carry

                lax.fori_loop(0, full_units, full, 0)
                bad[0] = jnp.where(jnp.max(acc[0:1, :]) < BIG, 0, 1)

            return carry

        lax.fori_loop(0, 2, attempt, 0)
        ot = acc[hw:, :] / acc[0:hw, :]
        ot_ref[i] = ot
        l_ref[i] = ref_row[...] + jnp.log2(acc[0:1, :]) / scale
        on = jnp.concatenate([ot[:, h * TB : (h + 1) * TB] for h in range(heads)], axis=0)
        o_ref[rows, :] = on.T
        return carry

    lax.fori_loop(0, nb, block, 0)


def attention_forward(useg, place, pieces, q, heads, hw, sizes):
    rows = q.shape[0]
    nb = rows // TB
    slots = 4 * pieces[0].shape[0] // INNER
    lanes = heads * TB
    units = slots * nb
    vm = pl.BlockSpec(memory_space=pltpu.VMEM)
    sm = pl.BlockSpec(memory_space=pltpu.SMEM)
    return pl.pallas_call(
        functools.partial(fwd_kernel, nb=nb, slots=slots, heads=heads, hw=hw, sizes=sizes),
        out_shape=(
            jax.ShapeDtypeStruct((rows, heads * hw), F32),
            jax.ShapeDtypeStruct((nb, hw, lanes), F32),
            jax.ShapeDtypeStruct((nb, 1, lanes), F32),
            jax.ShapeDtypeStruct((nb, hw, lanes), BF),
            jax.ShapeDtypeStruct((units, UNIT, 2 * hw), BF),
            jax.ShapeDtypeStruct((units, 2 * hw, UNIT), BF),
        ),
        in_specs=[sm, sm] + [vm] * 6,
        out_specs=(vm,) * 6,
        scratch_shapes=[
            pltpu.VMEM((2 * hw, lanes), BF),
            pltpu.VMEM((2 * hw, lanes), F32),
            pltpu.VMEM((1, lanes), F32),
            pltpu.SMEM((units + 1,), jnp.int32),
            pltpu.SMEM((units + 1,), jnp.int32),
            pltpu.SMEM((1,), jnp.int32),
        ],
        compiler_params=pltpu.CompilerParams(vmem_limit_bytes=60 << 20),
        cost_estimate=pl.CostEstimate(
            flops=40 * 10**9, bytes_accessed=8 << 20, transcendentals=26 * 10**6
        ),
        name="attention_forward",
    )(useg, place, *pieces, q)


def prepare_kernel(qt_ref, ot_ref, l_ref, do_ref, qa_ref, doa_ref, dot_ref, *, nb, heads, hw):
    pad = jnp.zeros((hw - 3, heads * TB), BF)

    def prepare(i, carry):
        rows = pl.ds(pl.multiple_of(i * TB, TB), TB)
        a, b, c = split3(-l_ref[i])
        qa_ref[i] = jnp.concatenate([qt_ref[i], a, b, c, pad], axis=0).T
        dt = to_lanes(do_ref[rows, :], heads, hw)
        dot_ref[i] = dt
        total = jnp.sum(dt.astype(F32) * ot_ref[i], axis=0, keepdims=True)
        a, b, c = split3(-total)
        doa_ref[i] = jnp.concatenate([a, b, c, pad, dt], axis=0).T
        return carry

    lax.fori_loop(0, nb, prepare, 0)


def attention_prepare(qt, ot, low, do, heads, hw):
    nb, _, lanes = qt.shape
    vm = pl.BlockSpec(memory_space=pltpu.VMEM)
    return pl.pallas_call(
        functools.partial(prepare_kernel, nb=nb, heads=heads, hw=hw),
        out_shape=(
            jax.ShapeDtypeStruct((nb, lanes, 2 * hw), BF),
            jax.ShapeDtypeStruct((nb, lanes, 2 * hw), BF),
            jax.ShapeDtypeStruct((nb, hw, lanes), BF),
        ),
        in_specs=[vm] * 4,
        out_specs=(vm,) * 3,
        compiler_params=pltpu.CompilerParams(vmem_limit_bytes=40 << 20),
        cost_estimate=pl.CostEstimate(flops=10**9, bytes_accessed=8 << 20, transcendentals=0),
        name="attention_prepare",
    )(qt, ot, low, do)


def bwd_kernel(
    useg, place, kaug_ref, vt_ref, qa, doa, qt, dot_t, *rest, nb, parts, first, last, heads, hw
):
    if first:
        dqacc, dkv_ref, kt, dkvt = rest
    elif last:
        dqold, dq_ref, dkv_ref, dqacc, kt, dkvt = rest
    else:
        dqold, dqacc, dkv_ref, kt, dkvt = rest
    step_at = pl.program_id(0)
    me, group = place[0], place[1]
    slot, part = step_at // len(parts), step_at % len(parts) + parts[0]
    unit = jnp.bitwise_xor(slot, group) * nb + part
    scale = LOG2E / math.sqrt(hw)
    lanes = heads * TB

    @pl.when(step_at == 0)
    def _():
        dqacc[...] = jnp.zeros_like(dqacc) if first else dqold[...]

    kt[...] = kaug_ref[0].T
    dkvt[...] = jnp.zeros_like(dkvt)
    unit_seg = useg[unit]

    def block(i, carry):
        own = group * nb + i

        def step(masked):
            s = dot(qa[i], kt[...]) * scale
            if masked:
                mask = key_offsets(
                    lax.broadcasted_iota(jnp.int32, (lanes, UNIT), 1), me
                ) <= query_offsets(lax.broadcasted_iota(jnp.int32, (lanes, UNIT), 0), me)
                s = jnp.where(mask, s, -1e30)
            p = jnp.exp2(s)
            ds = (p * dot(doa[i], vt_ref[0])).astype(BF)
            dkvt[hw:, :] += dot(dot_t[i], p.astype(BF))
            dkvt[:hw, :] += dot(qt[i], ds)
            dqacc[i] += dot(ds, kaug_ref[0])

        @pl.when((unit_seg == 0) & (own != unit) & ((useg[own] != 0) | (own > unit)))
        def _():
            step(False)

        @pl.when(own == unit)
        def _():
            step(True)

        return carry

    lax.fori_loop(0, nb, block, 0)
    factor = jnp.where(
        lax.broadcasted_iota(jnp.int32, (2 * hw, 1), 0) < hw, 1 / math.sqrt(hw), 1.0
    )
    dkv = (dkvt[...] * factor).astype(BF).T
    for s in range(INNER):
        dkv_ref[jnp.bitwise_xor(me, s)] = dkv[s * TB : (s + 1) * TB, :]

    if last:
        @pl.when(step_at == pl.num_programs(0) - 1)
        def _():
            def finish(i, carry):
                rows = pl.ds(pl.multiple_of(i * TB, TB), TB)
                a = dqacc[i]
                dq_ref[rows, :] = (
                    jnp.concatenate([a[h * TB : (h + 1) * TB, :hw] for h in range(heads)], axis=1)
                    * (1 / math.sqrt(hw))
                ).astype(BF)
                return carry

            lax.fori_loop(0, nb, finish, 0)


def attention_backward(useg, place, kaug, vt, qa, doa, qt, dot_t, dqold, parts, heads, hw):
    nb, lanes, _ = qa.shape
    slots = kaug.shape[0] // nb
    first, last = dqold is None, parts[-1] == nb - 1
    vm = pl.BlockSpec(memory_space=pltpu.VMEM)
    acc_shape = jax.ShapeDtypeStruct((nb, lanes, 2 * hw), F32)
    count = len(parts)

    def at(u, seg, place):
        return (u // count * nb + u % count + parts[0], 0, 0)

    return pl.pallas_call(
        functools.partial(
            bwd_kernel, nb=nb, parts=parts, first=first, last=last, heads=heads, hw=hw
        ),
        out_shape=(
            jax.ShapeDtypeStruct((nb * TB, heads * hw), BF) if last else acc_shape,
            jax.ShapeDtypeStruct((slots * INNER, count * TB, 2 * hw), BF),
        ),
        grid_spec=pltpu.PrefetchScalarGridSpec(
            num_scalar_prefetch=2,
            grid=(slots * count,),
            in_specs=[
                pl.BlockSpec((1, UNIT, 2 * hw), at),
                pl.BlockSpec((1, 2 * hw, UNIT), at),
            ]
            + [vm] * (4 if first else 5),
            out_specs=(
                vm,
                pl.BlockSpec(
                    (INNER, TB, 2 * hw),
                    lambda u, seg, place: (jnp.bitwise_xor(u // count, place[1]), u % count, 0),
                ),
            ),
            scratch_shapes=([pltpu.VMEM(acc_shape.shape, F32)] if last and not first else [])
            + [
                pltpu.VMEM((2 * hw, UNIT), BF),
                pltpu.VMEM((2 * hw, UNIT), F32),
            ],
        ),
        compiler_params=pltpu.CompilerParams(vmem_limit_bytes=60 << 20),
        cost_estimate=pl.CostEstimate(
            flops=8 * 10**9 * count, bytes_accessed=12 << 20, transcendentals=2 * 10**6 * count
        ),
        name="attention_backward",
    )(useg, place, kaug, vt, qa, doa, qt, dot_t, *([] if first else [dqold]))


def exact_dot(x, ones):
    a, b, c = split3(x)
    return dot(a, ones) + dot(b, ones) + dot(c, ones)


def norm_parts(values):
    mean_val = jnp.mean(values, axis=-1, keepdims=True)
    centered = values - mean_val
    variance = jnp.mean(centered * centered, axis=-1, keepdims=True)
    inverse = lax.rsqrt(variance + 1e-05)
    return centered * inverse, inverse


def norm_back(grad, unit, inverse, gain):
    scaled = grad * gain
    shift = jnp.mean(scaled, axis=-1, keepdims=True)
    along = jnp.mean(scaled * unit, axis=-1, keepdims=True)
    return inverse * (scaled - shift - unit * along)


def put_pieces(grads_ref, core, value, first, rows, at, count):
    piece = rows // 2 // count
    value = value.astype(BF)
    for start in range(0, value.shape[0], piece):
        half, rest = divmod(first + start, rows // 2)
        grads_ref[jnp.bitwise_xor(core[0], half), rest // piece, at : at + piece, :] = value[
            start : start + piece
        ]


def middle_kernel(
    core, x_ref, att_ref, logit_ref, code_ref, cot_ref, norm_ref, out_w, up_w, down_w,
    result_ref, middle_grad_ref, att_grad_ref, logit_grad_ref, norm_grad_ref,
    grads_ref,
    mixed_s, normed_s, hidden_s, pre_s, branch_s, *, count, heads
):
    rows, width = x_ref.shape
    chunk = rows
    hw = width // heads
    gain = norm_ref[...].astype(F32)
    lane = lax.broadcasted_iota(jnp.int32, (chunk, 128), 1)
    head = lax.broadcasted_iota(jnp.int32, (128, width), 0)
    column = lax.broadcasted_iota(jnp.int32, (128, width), 1)
    widen = jnp.where(column // hw == head, 1.0, 0.0).astype(BF)
    narrow = jnp.where(
        lax.broadcasted_iota(jnp.int32, (width, 128), 0) // hw
        == lax.broadcasted_iota(jnp.int32, (width, 128), 1),
        1.0, 0.0,
    ).astype(BF)
    if True:
        at = slice(None)
        code = code_ref[at, :]
        chosen = ((code // heads == lane) | (code % heads == lane)) & (lane < heads)
        lifted = jnp.where(chosen, logit_ref[at, :], -1e30)
        raised = jnp.where(
            chosen, jnp.exp(lifted - jnp.max(lifted, axis=-1, keepdims=True)), 0.0
        )
        gate = raised / jnp.sum(raised, axis=-1, keepdims=True)
        gates = exact_dot(gate, widen)
        attended = att_ref[at, :]
        mixed = (gates * attended).astype(BF)
        mixed_s[at, :] = mixed
        middle = x_ref[at, :].astype(F32) + dot(mixed, out_w[...])
        unit, inverse = norm_parts(middle)
        normed = (unit * gain).astype(BF)
        normed_s[at, :] = normed
        cot = cot_ref[at, :]
        total = middle
        back = jnp.zeros((chunk, width), F32)
        step = 1024
        for c in range(0, up_w.shape[1], step):
            pre = dot(normed, up_w[:, c : c + step])
            inside = 0.7978845608028654 * (pre + 0.044715 * pre * pre * pre)
            t = jnp.tanh(inside)
            half = 0.5 * (1.0 + t)
            hidden = (pre * half).astype(BF)
            slope = half + 0.5 * pre * (1.0 - t * t) * (
                0.7978845608028654 * (1.0 + 3 * 0.044715 * pre * pre)
            )
            hidden_s[at, c : c + step] = hidden
            total = total + dot(hidden, down_w[c : c + step, :])
            pre_grad = (outer(cot, down_w[c : c + step, :]) * slope).astype(BF)
            pre_s[at, c : c + step] = pre_grad
            back = back + outer(pre_grad, up_w[:, c : c + step])
        result_ref[at, :] = total.astype(BF)
        norm_grad_ref[...] = jnp.sum(
            (back * unit).reshape(chunk // 8, 8, width), axis=0
        )
        middle_grad = cot.astype(F32) + norm_back(back, unit, inverse, gain)
        middle_grad_ref[at, :] = middle_grad
        branch = middle_grad.astype(BF)
        branch_s[at, :] = branch
        mixed_grad = outer(branch, out_w[...])
        gate_grad = exact_dot(mixed_grad * attended, narrow)
        logit_grad_ref[at, :] = (
            gate * (gate_grad - jnp.sum(gate * gate_grad, axis=-1, keepdims=True))
        ).astype(BF)
        att_grad_ref[at, :] = (gates * mixed_grad).astype(BF)
    ff = hidden_s.shape[1]
    across = width
    for c in range(0, ff, width):
        put_pieces(grads_ref, core, inner(hidden_s[:, c : c + width], cot), c, ff, 0, count)
    down_rows = ff // 2 // count
    for c in range(0, width, width // 2):
        at = slice(c, c + width // 2)
        up = inner(normed_s[:, at], pre_s[...])
        piece = width // 2 // count
        for k in range(ff // across):
            put_pieces(
                grads_ref, core, up[:, k * across : (k + 1) * across], c, width,
                down_rows + k * piece, count,
            )
        put_pieces(
            grads_ref, core, inner(mixed_s[:, at], branch_s[...]), c, width,
            down_rows + ff // across * piece, count,
        )


def middle_pass(core, x, attended, logits, code, cot, norm_b, out_w, up_w, down_w, heads, count):
    rows, width = x.shape
    ff = up_w.shape[1]
    piece_rows = (ff * width * 2 + width * width) // (2 * count * width)
    vm = pl.BlockSpec(memory_space=pltpu.VMEM)
    shape = jax.ShapeDtypeStruct
    return pl.pallas_call(
        functools.partial(middle_kernel, count=count, heads=heads),
        out_shape=(
            shape((rows, width), BF),
            shape((rows, width), F32),
            shape((rows, width), BF),
            shape((rows, 128), BF),
            shape((8, width), F32),
            shape((2, count, piece_rows, width), BF),
        ),
        in_specs=[pl.BlockSpec(memory_space=pltpu.SMEM)] + [vm] * 9,
        out_specs=(vm,) * 6,
        scratch_shapes=[
            pltpu.VMEM((rows, width), BF),
            pltpu.VMEM((rows, width), BF),
            pltpu.VMEM((rows, ff), BF),
            pltpu.VMEM((rows, ff), BF),
            pltpu.VMEM((rows, width), BF),
        ],
        compiler_params=pltpu.CompilerParams(vmem_limit_bytes=60 << 20),
        cost_estimate=pl.CostEstimate(
            flops=9 * 10**9, bytes_accessed=24 << 20, transcendentals=2 * 10**6
        ),
        name="middle_pass",
    )(core, x, attended, logits, code, cot, norm_b, out_w, up_w, down_w)


class Layout:
    def __init__(self, ctx_count):
        sizes = [4]
        while math.prod(sizes) < ctx_count:
            sizes.append(2)
        assert math.prod(sizes) == ctx_count
        self.sizes = tuple(sizes)
        self.axes = tuple(f"c{k}" for k in range(len(sizes)))
        cut = len(sizes)
        while math.prod(sizes[cut:]) < INNER:
            cut -= 1
        assert math.prod(sizes[cut:]) == INNER
        self.outer_axes, self.inner_axes = self.axes[:cut], self.axes[cut:]
        self.count = ctx_count


def exchange(x, axis, size, step):
    return lax.ppermute(x, axis, [(i, i ^ step) for i in range(size)])


def spread(x, order, lay, start=0, stop=None):
    for axis in order[start:stop]:
        size = lay.sizes[lay.axes.index(axis)]
        x = jnp.concatenate([x] + [exchange(x, axis, size, step) for step in range(1, size)])
    return x


def gather_near(x, lay):
    return spread(x[None], lay.axes[:-2], lay)


def gather_sides(near, lay):
    y_axis, x_axis = lay.axes[-2:]
    return exchange(near, x_axis, 2, 1), exchange(near, y_axis, 2, 1)


def gather_far(near_x, near_y, lay, cut):
    y_axis, x_axis = lay.axes[-2:]
    return exchange(near_x[:, :cut], y_axis, 2, 1), exchange(near_y[:, cut:], x_axis, 2, 1)


def deal(x, lay):
    rows, width = x.shape
    packed = x.reshape(rows // (RUN * INNER), INNER, RUN, width).transpose(1, 0, 2, 3)
    packed = packed.reshape(INNER, rows // INNER, width)
    return lax.all_to_all(packed, lay.inner_axes, 0, 0, tiled=True)


def undeal(x, lay):
    rows, width = x.shape
    return take_back(
        lax.all_to_all(x.reshape(INNER, rows // INNER, width), lay.inner_axes, 0, 0, tiled=True)
    )


def take_back(back):
    rows, width = back.shape[0] * back.shape[1], back.shape[2]
    back = back.reshape(INNER, rows // (RUN * INNER), RUN, width).transpose(1, 0, 2, 3)
    return back.reshape(rows, width)


def tie(*values):
    return lax.optimization_barrier(values)


def swap_pieces(both, lay):
    return lax.all_to_all(both, lay.axes, 0, 0, tiled=True)


def add_pieces(pieces):
    return jnp.sum(pieces.astype(F32), axis=0).astype(BF)


def place_kernel(mine, near, near_x, near_y, far_a, far_b, *outs, count, across, sizes):
    cut = far_a.shape[1]
    looped = all(out.shape[0] // count % 8 == 0 for out in outs)

    def one(c, carry):
        s = jnp.bitwise_xor(c, mine[0])
        index = near_index(s // 4, sizes)

        def put(ref, low, high, base):
            first = 0
            for out in outs:
                piece = out.shape[0] // count
                for k in range(out.shape[1] // across):
                    if low <= first < high:
                        rows = pl.ds(pl.multiple_of(c * piece, piece) if looped else c * piece, piece)
                        out[rows, k * across : (k + 1) * across] = ref[
                            index, first - base : first - base + piece, :
                        ].astype(F32)
                    first += piece

        everything = near.shape[1]
        for side, ref in enumerate((near, near_x, near_y)):
            @pl.when(s % 4 == side)
            def _(ref=ref):
                put(ref, 0, everything, 0)

        @pl.when(s % 4 == 3)
        def _():
            put(far_a, 0, cut, 0)
            put(far_b, cut, everything, cut)

        return carry

    if looped:
        lax.fori_loop(0, count, one, 0)
    else:
        for c in range(count):
            one(c, 0)


def place_pieces(pieces, mine, shapes, across, sizes):
    vm = pl.BlockSpec(memory_space=pltpu.VMEM)
    count = 4 * pieces[0].shape[0]
    return pl.pallas_call(
        functools.partial(place_kernel, count=count, across=across, sizes=sizes),
        out_shape=tuple(jax.ShapeDtypeStruct(shape, F32) for shape in shapes),
        in_specs=[pl.BlockSpec(memory_space=pltpu.SMEM)] + [vm] * 5,
        out_specs=(vm,) * len(shapes),
        compiler_params=pltpu.CompilerParams(vmem_limit_bytes=40 << 20),
        cost_estimate=pl.CostEstimate(
            flops=0, bytes_accessed=24 * pieces[0].size, transcendentals=0
        ),
        name="place_pieces",
    )(mine, *pieces)


def sum_all(x, lay):
    for axis, size in zip(lay.axes, lay.sizes):
        terms = [x.astype(F32)] + [
            exchange(x, axis, size, step).astype(F32) for step in range(1, size)
        ]
        while len(terms) > 1:
            terms = [terms[k] + terms[k + 1] for k in range(0, len(terms), 2)]
        x = terms[0].astype(BF)
    return x


def layer_norm(values, gain_vec):
    mean_val = jnp.mean(values, axis=-1, keepdims=True)
    centered = values - mean_val
    variance = jnp.mean(centered * centered, axis=-1, keepdims=True)
    return centered * lax.rsqrt(variance + 1e-05) * gain_vec


def on_device(
    lay, inputs, cotangent, segments, routes, norm_first, w_query, w_keyval, w_router, w_out,
    norm_second, w_up, w_down
):
    def whole(shard):
        return lax.all_gather(shard, "w", axis=0, tiled=True)

    rows, width = inputs.shape[1:]
    head_count = w_router.shape[1]
    head_width = w_keyval.shape[1] // 2
    nb = rows // TB
    group_count = lay.count // INNER
    me = lax.axis_index(lay.inner_axes)
    group = lax.axis_index(lay.outer_axes) if lay.outer_axes else jnp.int32(0)
    place = jnp.stack([me, group]).astype(jnp.int32)
    mine = (group * INNER + me).astype(jnp.int32)[None]

    core = lax.axis_index("w")
    near_sizes = lay.sizes[:-2]

    def whole_by_exchange(shard):
        other = exchange(shard, "w", 2, 1)
        return jnp.where(
            core == 0,
            jnp.concatenate([shard, other], axis=0),
            jnp.concatenate([other, shard], axis=0),
        )

    rows_low = deal(inputs[0], lay).reshape(rows, width)
    narrow = whole(
        jnp.concatenate([w_router, norm_first[:, None], norm_second[:, None]], axis=1)
    )
    router_w = jnp.pad(narrow[:, :head_count], ((0, 0), (0, 128 - head_count)))
    norm_a, norm_b = narrow[:, head_count], narrow[:, head_count + 1]
    query_w, keyval_w, out_w = whole(w_query), whole(w_keyval), whole(w_out)
    up_w, down_w = whole_by_exchange(w_up), whole_by_exchange(w_down)

    spans = rows // (RUN * INNER)
    span_seg = jnp.pad(segments[:, :: RUN * INNER], ((0, 0), (0, 128 - spans)))
    span_seg, rows_low = tie(span_seg, rows_low)
    all_seg = spread(span_seg, lay.axes[::-1], lay)
    source = jnp.bitwise_xor(jnp.arange(lay.count, dtype=jnp.int32), mine)
    at = source[:, None] * spans + jnp.arange(128, dtype=jnp.int32)[None]
    at = jnp.where(jnp.arange(128)[None] < spans, at, -1)
    first = jnp.arange(group_count * nb, dtype=jnp.int32) * (UNIT // (RUN * INNER))
    useg = jnp.sum(jnp.where(at[None] == first[:, None, None], all_seg[None], 0), axis=(1, 2))

    rows_in = rows_low.astype(F32)
    normed_f, norm_a_pull = jax.vjp(layer_norm, rows_in, norm_a.astype(F32))
    normed = normed_f.astype(BF)
    keyval = dot(normed, keyval_w).astype(BF)
    near = gather_near(keyval, lay)
    near_x, near_y = gather_sides(near, lay)
    far = gather_far(near_x, near_y, lay, (nb // 2) * TB)
    queries = dot(normed, query_w).astype(BF)
    logits = dot(normed, router_w)

    code = (routes[0, :, 0] * head_count + routes[0, :, 1]).astype(BF)
    slot_rows = rows // INNER
    code = code.reshape(rows // (RUN * INNER), INNER, RUN).transpose(1, 0, 2)
    code = jnp.pad(code.reshape(INNER, 1, slot_rows), ((0, 0), (0, RUN - 1), (0, width - slot_rows)))
    packed = cotangent[0].reshape(rows // (RUN * INNER), INNER, RUN, width).transpose(1, 0, 2, 3)
    packed = jnp.concatenate([packed.reshape(INNER, slot_rows, width), code], axis=1)
    packed, near_x, near_y = tie(packed, near_x, near_y)
    dealt = lax.all_to_all(packed, lay.inner_axes, 0, 0, tiled=True)
    attended, ot, low, qt, kaug, vt = attention_forward(
        useg, place, (near, near_x, near_y) + far, queries, head_count, head_width, near_sizes
    )
    attended, dealt = tie(attended, dealt)
    grad_top = dealt[:, :slot_rows].reshape(rows, width)
    code = dealt[:, slot_rows, :slot_rows].reshape(rows, 1).astype(jnp.int32)
    result, middle_grad, att_grad, logit_low, norm_b_part, grads = middle_pass(
        core.astype(jnp.int32)[None], rows_low, attended, logits, code, grad_top, norm_b[None],
        out_w, up_w, down_w, head_count, lay.count,
    )
    other = exchange(grads[1], "w", 2, 1)
    qa, doa, dot_t = attention_prepare(qt, ot, low, att_grad, head_count, head_width)
    both = (grads[0].astype(F32) + other.astype(F32)).astype(BF)
    piece_rows = both.shape[1]
    merged = lay.count == INNER
    if merged:
        both = jnp.concatenate([both, result.reshape(INNER, slot_rows, width)], axis=1)
    both, qa = tie(both, qa)
    pieces = swap_pieces(both, lay)

    cuts = (0, nb // 2, nb - nb // 5, nb)
    dq, dkv_sums, waiting = None, [], None
    for turn in range(3):
        parts = tuple(range(cuts[turn], cuts[turn + 1]))
        dq, dkv = attention_backward(
            useg, place, kaug, vt, qa, doa, qt, dot_t, dq, parts, head_count, head_width
        )
        if turn == 0:
            dq, dkv, pieces = tie(dq, dkv, pieces)
            total = add_pieces(pieces[:, :piece_rows])
            output = take_back(pieces[:, piece_rows:]) if merged else undeal(result, lay)
        elif turn == 1:
            dq, dkv, waiting, total = tie(dq, dkv, waiting, total)
            grad_near = gather_near(total, lay)
        else:
            dq, dkv, waiting, grad_near = tie(dq, dkv, waiting, grad_near)
        if waiting is not None:
            dkv_sums.append(add_pieces(waiting))
        if turn < 2:
            waiting = swap_pieces(dkv, lay)
    query_grad = dq
    query_w_grad = inner(normed, query_grad).astype(BF)
    piece = width // 2 // lay.count
    query_parts = query_w_grad.reshape(2, lay.count, piece, width // 128, 128)
    query_parts = query_parts.transpose(1, 0, 3, 2, 4).reshape(lay.count, -1, 128)
    dkv_rows = dkv.shape[1]
    last = add_pieces(swap_pieces(jnp.concatenate([dkv, query_parts], axis=1), lay))
    dkv_sums.append(last[:dkv_rows])
    query_halves = last[dkv_rows:].reshape(2, -1, 128)
    keyval_grad = jnp.concatenate(dkv_sums, axis=0)

    keyval_w_grad = inner(normed, keyval_grad)
    router_grad = inner(normed, logit_low)[:, :head_count]
    norm_b_grad = jnp.sum(norm_b_part, axis=0)
    normed_grad = (
        outer(query_grad, query_w) + outer(keyval_grad, keyval_w) + outer(logit_low, router_w)
    )
    input_norm, norm_a_grad = norm_a_pull(normed_grad)
    input_grad = undeal((middle_grad + input_norm).astype(BF), lay).astype(F32)[None]

    keep = lax.dynamic_index_in_dim(query_halves, core, 0, keepdims=False)
    other = exchange(
        lax.dynamic_index_in_dim(query_halves, 1 - core, 0, keepdims=False), "w", 2, 1
    )
    query_piece = (keep.astype(F32) + other.astype(F32)).astype(BF)

    def finish(near, cut, shapes, across):
        sides = gather_sides(near, lay)
        every = (near,) + sides + gather_far(*sides, lay, cut)
        return place_pieces(every, mine, shapes, across, near_sizes)

    down_sum, up_sum, out_sum = finish(
        grad_near, w_down.shape[0] // lay.count, [w_down.shape, w_up.shape, w_out.shape], width
    )
    (query_sum,) = finish(
        gather_near(query_piece, lay), query_piece.shape[0] // 2, [w_query.shape], 128
    )
    small = jnp.concatenate(
        [keyval_w_grad, router_grad, norm_a_grad[:, None], norm_b_grad[:, None]], axis=1
    )
    small = jnp.pad(small, ((0, 0), (0, -small.shape[1] % 128))).astype(BF)
    small = small.reshape(2, width // 2, -1)
    keep = lax.dynamic_index_in_dim(small, core, 0, keepdims=False).astype(F32)
    other = exchange(lax.dynamic_index_in_dim(small, 1 - core, 0, keepdims=False), "w", 2, 1)
    small = sum_all((keep + other.astype(F32)).astype(BF), lay).astype(F32)
    kv_width = 2 * head_width
    keyval_sum, small_sum = small[:, :kv_width], small[:, kv_width:]
    return (
        output[None],
        input_grad,
        small_sum[:, head_count],
        query_sum,
        keyval_sum,
        small_sum[:, :head_count],
        out_sum,
        small_sum[:, head_count + 1],
        up_sum,
        down_sum,
    )


def solution(mesh):
    ctx_count, core_count = mesh.shape["ctx"], mesh.shape["wshard"]
    lay = Layout(ctx_count)
    grid = Mesh(mesh.devices.reshape(lay.sizes + (core_count,)), lay.axes + ("w",))
    ctx = lay.axes
    tokens = P("w", ctx, None)
    return jax.shard_map(
        functools.partial(on_device, lay),
        mesh=grid,
        in_specs=(
            tokens, tokens, P("w", ctx), tokens,
            P("w"), P("w", None), P("w", None), P("w", None), P("w", None),
            P("w"), P("w", None), P("w", None),
        ),
        out_specs=(
            tokens, tokens,
            P("w"), P("w", None), P("w", None), P("w", None), P("w", None),
            P("w"), P("w", None), P("w", None),
        ),
        check_vma=False,
    )
```

```python
import functools
import math

import jax
import jax.numpy as jnp
from jax import lax
from jax.experimental import pallas as pl
from jax.experimental.pallas import tpu as pltpu
from jax.sharding import Mesh, PartitionSpec as P

F32 = jnp.float32
BF = jnp.bfloat16
UNIT = 1024
TB = 64
INNER = UNIT // TB
RUN = 8
LOG2E = 1.4426950408889634
BIG = 2.0**100


def dot(lhs, rhs):
    return lax.dot_general(lhs, rhs, (((1,), (0,)), ((), ())), preferred_element_type=F32)


def inner(lhs, rhs):
    return lax.dot_general(lhs, rhs, (((0,), (0,)), ((), ())), preferred_element_type=F32)


def outer(lhs, rhs):
    return lax.dot_general(lhs, rhs, (((1,), (1,)), ((), ())), preferred_element_type=F32)


def split3(x):
    a = x.astype(BF)
    rest = x - a.astype(F32)
    b = rest.astype(BF)
    return a, b, (rest - b.astype(F32)).astype(BF)


def to_lanes(x, heads, hw):
    xt = x.T
    return jnp.concatenate([xt[h * hw : (h + 1) * hw] for h in range(heads)], axis=1)


def query_offsets(index, me):
    rest = index & (TB - 1)
    return (rest >> 3) * (RUN * INNER) + me * RUN + (rest & 7)


def near_index(rest, sizes):
    digits = []
    for size in sizes[::-1]:
        digits.append(rest % size)
        rest = rest // size
    index = 0
    for digit, size in zip(digits, sizes[::-1]):
        index = index * size + digit
    return index


def fetch_pieces(pieces, count, sizes, mine, total, put):
    near, near_x, near_y, far_a, far_b = pieces
    cut = far_a.shape[1]

    def one(c, carry):
        s = jnp.bitwise_xor(c, mine)
        index = near_index(s // 4, sizes)
        for side, ref in enumerate((near, near_x, near_y)):
            @pl.when(s % 4 == side)
            def _(ref=ref):
                put(c, 0, ref[index, :total, :])

        @pl.when(s % 4 == 3)
        def _():
            put(c, 0, far_a[index])
            put(c, cut, far_b[index, : total - cut, :])

        return carry

    lax.fori_loop(0, count, one, 0)


def fwd_kernel(
    useg, place, near, near_x, near_y, far_a, far_b, q_ref, o_ref, ot_ref, l_ref, qt_ref, kaug, vt,
    qa, acc, ref_row, plist, rank, bad, *, nb, slots, heads, hw, sizes
):
    me, group = place[0], place[1]
    scale = LOG2E / math.sqrt(hw)
    lanes = heads * TB
    units = slots * nb

    def scan(u, n):
        rank[u] = n
        plist[n] = u
        return n + jnp.where(useg[u] == 0, 1, 0)

    prompt_units = lax.fori_loop(0, units, scan, jnp.int32(0))
    lane = lax.broadcasted_iota(jnp.int32, (UNIT, 2 * hw), 1)
    row = lax.broadcasted_iota(jnp.int32, (2 * hw, UNIT), 0)
    extra = jnp.where(lane < hw + 3, 1.0, 0.0).astype(BF)

    def put(c, first, rows):
        at = pl.multiple_of(c * nb * TB + first, TB)
        kaug[pl.ds(at, rows.shape[0]), :] = rows

    fetch_pieces(
        (near, near_x, near_y, far_a, far_b), slots * INNER, sizes, group * INNER + me, nb * TB, put
    )

    def split(u, carry):
        rows = pl.ds(pl.multiple_of(u * UNIT, UNIT), UNIT)
        tile = kaug[rows, :]
        kaug[rows, :] = jnp.where(lane < hw, tile, extra)
        flip = tile.T
        vt[u] = jnp.where(row < hw, jnp.ones_like(flip), flip)
        return carry

    lax.fori_loop(0, units, split, 0)

    def keys_of(u):
        return kaug[pl.ds(pl.multiple_of(u * UNIT, UNIT), UNIT), :]

    def block(i, carry):
        own = group * nb + i
        full_units = jnp.where(useg[own] != 0, prompt_units, rank[own])
        rows = pl.ds(pl.multiple_of(i * TB, TB), TB)
        qt = to_lanes(q_ref[rows, :], heads, hw)
        qt_ref[i] = qt
        qa[0:hw, :] = qt
        qa[hw:, :] = jnp.zeros((hw, lanes), BF)
        mask = lax.broadcasted_iota(jnp.int32, (UNIT, lanes), 0) <= query_offsets(lax.broadcasted_iota(jnp.int32, (UNIT, lanes), 1), me)
        ref_row[...] = jnp.max(
            jnp.where(mask, dot(keys_of(own), qa[...]), -1e30), axis=0, keepdims=True
        )
        bad[0] = 1

        def attempt(turn, carry):
            @pl.when(bad[0] != 0)
            def _():
                @pl.when(turn == 1)
                def _():
                    qa[hw:, :] = jnp.zeros((hw, lanes), BF)

                    def highest(k, carry):
                        ref_row[...] = jnp.maximum(
                            ref_row[...],
                            jnp.max(dot(keys_of(plist[k]), qa[...]), axis=0, keepdims=True),
                        )
                        return carry

                    lax.fori_loop(0, full_units, highest, 0)

                a, b, c = split3(-ref_row[...])
                qa[hw:, :] = jnp.concatenate([a, b, c, jnp.zeros((hw - 3, lanes), BF)], axis=0)
                s = jnp.where(mask, dot(keys_of(own), qa[...]) * scale, -1e30)
                acc[...] = dot(vt[own], jnp.exp2(s).astype(BF))

                def full(k, carry):
                    u = plist[k]
                    p = jnp.exp2(dot(keys_of(u), qa[...]) * scale).astype(BF)
                    acc[...] += dot(vt[u], p)
                    return carry

                lax.fori_loop(0, full_units, full, 0)
                bad[0] = jnp.where(jnp.max(acc[0:1, :]) < BIG, 0, 1)

            return carry

        lax.fori_loop(0, 2, attempt, 0)
        ot = acc[hw:, :] / acc[0:hw, :]
        ot_ref[i] = ot
        l_ref[i] = ref_row[...] + jnp.log2(acc[0:1, :]) / scale
        on = jnp.concatenate([ot[:, h * TB : (h + 1) * TB] for h in range(heads)], axis=0)
        o_ref[rows, :] = on.T
        return carry

    lax.fori_loop(0, nb, block, 0)


def attention_forward(useg, place, pieces, q, heads, hw, sizes):
    rows = q.shape[0]
    nb = rows // TB
    slots = 4 * pieces[0].shape[0] // INNER
    lanes = heads * TB
    units = slots * nb
    vm = pl.BlockSpec(memory_space=pltpu.VMEM)
    sm = pl.BlockSpec(memory_space=pltpu.SMEM)
    return pl.pallas_call(
        functools.partial(fwd_kernel, nb=nb, slots=slots, heads=heads, hw=hw, sizes=sizes),
        out_shape=(
            jax.ShapeDtypeStruct((rows, heads * hw), F32),
            jax.ShapeDtypeStruct((nb, hw, lanes), F32),
            jax.ShapeDtypeStruct((nb, 1, lanes), F32),
            jax.ShapeDtypeStruct((nb, hw, lanes), BF),
            jax.ShapeDtypeStruct((units * UNIT, 2 * hw), BF),
            jax.ShapeDtypeStruct((units, 2 * hw, UNIT), BF),
        ),
        in_specs=[sm, sm] + [vm] * 6,
        out_specs=(vm,) * 6,
        scratch_shapes=[
            pltpu.VMEM((2 * hw, lanes), BF),
            pltpu.VMEM((2 * hw, lanes), F32),
            pltpu.VMEM((1, lanes), F32),
            pltpu.SMEM((units + 1,), jnp.int32),
            pltpu.SMEM((units + 1,), jnp.int32),
            pltpu.SMEM((1,), jnp.int32),
        ],
        compiler_params=pltpu.CompilerParams(vmem_limit_bytes=60 << 20),
        cost_estimate=pl.CostEstimate(
            flops=40 * 10**9, bytes_accessed=8 << 20, transcendentals=26 * 10**6
        ),
        name="attention_forward",
    )(useg, place, *pieces, q)


def prepare_kernel(qt_ref, ot_ref, l_ref, do_ref, qa_ref, doa_ref, dot_ref, *, nb, heads, hw):
    pad = jnp.zeros((hw - 3, heads * TB), BF)

    def prepare(i, carry):
        rows = pl.ds(pl.multiple_of(i * TB, TB), TB)
        a, b, c = split3(-l_ref[i])
        qa_ref[i] = jnp.concatenate([qt_ref[i], a, b, c, pad], axis=0).T
        dt = to_lanes(do_ref[rows, :], heads, hw)
        dot_ref[i] = dt
        total = jnp.sum(dt.astype(F32) * ot_ref[i], axis=0, keepdims=True)
        a, b, c = split3(-total)
        doa_ref[i] = jnp.concatenate([a, b, c, pad, dt], axis=0).T
        return carry

    lax.fori_loop(0, nb, prepare, 0)


def bwd_kernel(
    useg, place, kaug_ref, vt_ref, qa, doa, qt, dot_t, *rest, nb, parts, first, last, dealt, heads, hw
):
    if first:
        dqacc, dkv_ref, kt, dkvt = rest
    elif last:
        dqold, normed, dq_ref, dkv_ref, dqacc, kt, dkvt = rest
    else:
        dqold, dqacc, dkv_ref, kt, dkvt = rest
    grid_at = pl.program_id(0)
    steps = pl.num_programs(0) - (2 if last and dealt else 0)
    step_at = jnp.minimum(grid_at, steps - 1)
    me, group = place[0], place[1]
    unit = step_at // len(parts) * nb + step_at % len(parts) + parts[0]
    scale = LOG2E / math.sqrt(hw)
    lanes = heads * TB

    @pl.when(grid_at == 0)
    def _():
        dqacc[...] = jnp.zeros_like(dqacc) if first else dqold[...]

    unit_seg = useg[unit]

    def block(i, carry):
        own = group * nb + i

        def step(masked):
            s = dot(qa[i], kt[...]) * scale
            if masked:
                mask = lax.broadcasted_iota(jnp.int32, (lanes, UNIT), 1) <= query_offsets(lax.broadcasted_iota(jnp.int32, (lanes, UNIT), 0), me)
                s = jnp.where(mask, s, -1e30)
            p = jnp.exp2(s)
            ds = (p * dot(doa[i], vt_ref[0])).astype(BF)
            dkvt[hw:, :] += dot(dot_t[i], p.astype(BF))
            dkvt[:hw, :] += dot(qt[i], ds)
            dqacc[i] += dot(ds, kaug_ref[...])

        @pl.when((unit_seg == 0) & (own != unit) & ((useg[own] != 0) | (own > unit)))
        def _():
            step(False)

        @pl.when(own == unit)
        def _():
            step(True)

        return carry

    def keys():
        kt[...] = kaug_ref[...].T
        dkvt[...] = jnp.zeros_like(dkvt)
        lax.fori_loop(0, nb, block, 0)
        factor = jnp.where(
            lax.broadcasted_iota(jnp.int32, (2 * hw, 1), 0) < hw, 1 / math.sqrt(hw), 1.0
        )
        dkv = (dkvt[...] * factor).T.reshape(TB // RUN, INNER, RUN, 2 * hw)
        for d in range(INNER):
            to = piece_at(d, me // 4, dealt)
            dkv_ref[to] = dkv[:, d].reshape(TB, 2 * hw).astype(BF)

    if last and dealt:
        pl.when(grid_at < steps)(keys)
    else:
        keys()

    if last:
        @pl.when(grid_at == steps - 1)
        def _():
            def finish(i, carry):
                rows = pl.ds(pl.multiple_of(i * TB, TB), TB)
                a = dqacc[i]
                dq_ref[rows, :] = (
                    jnp.concatenate([a[h * TB : (h + 1) * TB, :hw] for h in range(heads)], axis=1)
                    * (1 / math.sqrt(hw))
                ).astype(BF)
                return carry

            lax.fori_loop(0, nb, finish, 0)

    if last and dealt:
        @pl.when(grid_at >= steps)
        def _():
            width = dq_ref.shape[1]
            half = width // 2
            rows = pl.ds(pl.multiple_of((grid_at - steps) * half, half), half)
            grad = dot(normed[rows, :], dq_ref[...]).astype(BF)
            piece = half // INNER
            for c in range(INNER):
                to = piece_at(c, me // 4, dealt)
                for k in range(width // 128):
                    dkv_ref[to, k * piece : (k + 1) * piece, :] = grad[
                        c * piece : (c + 1) * piece, k * 128 : (k + 1) * 128
                    ]


def attention_backward(useg, place, kaug, vt, qa, doa, qt, dot_t, dqold, normed_t, parts, heads, hw):
    nb, lanes, _ = qa.shape
    slots = vt.shape[0] // nb
    first, last = dqold is None, parts[-1] == nb - 1
    dealt = slots == 1
    more = 2 if last and dealt else 0
    vm = pl.BlockSpec(memory_space=pltpu.VMEM)
    acc_shape = jax.ShapeDtypeStruct((nb, lanes, 2 * hw), F32)
    count = len(parts)

    def at(u, seg, place):
        u = jnp.minimum(u, slots * count - 1)
        return u // count * nb + u % count + parts[0]

    def to(u, seg, place):
        if dealt:
            return (0, u, 0)
        return (u // count, u % count, 0)

    return pl.pallas_call(
        functools.partial(
            bwd_kernel, nb=nb, parts=parts, first=first, last=last, dealt=dealt, heads=heads, hw=hw
        ),
        out_shape=(
            jax.ShapeDtypeStruct((nb * TB, heads * hw), BF) if last else acc_shape,
            jax.ShapeDtypeStruct((slots * INNER, (count + more) * TB, 2 * hw), BF),
        ),
        grid_spec=pltpu.PrefetchScalarGridSpec(
            num_scalar_prefetch=2,
            grid=(slots * count + more,),
            in_specs=[
                pl.BlockSpec((UNIT, 2 * hw), lambda *a: (at(*a), 0)),
                pl.BlockSpec((1, 2 * hw, UNIT), lambda *a: (at(*a), 0, 0)),
            ]
            + [vm] * (4 if first else 6 if last else 5),
            out_specs=(
                vm,
                pl.BlockSpec((INNER, TB, 2 * hw), to),
            ),
            scratch_shapes=([pltpu.VMEM(acc_shape.shape, F32)] if last and not first else [])
            + [
                pltpu.VMEM((2 * hw, UNIT), BF),
                pltpu.VMEM((2 * hw, UNIT), F32),
            ],
        ),
        compiler_params=pltpu.CompilerParams(vmem_limit_bytes=60 << 20),
        cost_estimate=pl.CostEstimate(
            flops=8 * 10**9 * count, bytes_accessed=12 << 20, transcendentals=2 * 10**6 * count
        ),
        name="attention_backward",
    )(useg, place, kaug, vt, qa, doa, qt, dot_t, *([] if first else [dqold, normed_t] if last else [dqold]))


def exact_dot(x, ones):
    a, b, c = split3(x)
    return dot(a, ones) + dot(b, ones) + dot(c, ones)


def norm_parts(values):
    mean_val = jnp.mean(values, axis=-1, keepdims=True)
    centered = values - mean_val
    variance = jnp.mean(centered * centered, axis=-1, keepdims=True)
    inverse = lax.rsqrt(variance + 1e-05)
    return centered * inverse, inverse


def norm_back(grad, unit, inverse, gain):
    scaled = grad * gain
    shift = jnp.mean(scaled, axis=-1, keepdims=True)
    along = jnp.mean(scaled * unit, axis=-1, keepdims=True)
    return inverse * (scaled - shift - unit * along)


def piece_at(c, my_rest, dealt):
    return c % 4 * (INNER // 4) + jnp.bitwise_xor(c // 4, my_rest) if dealt else c


def put_pieces(grads_ref, where, value, first, rows, at, count):
    piece = rows // 2 // count
    value = value.astype(BF)
    for start in range(0, value.shape[0], piece):
        half, rest = divmod(first + start, rows // 2)
        to = piece_at(rest // piece, where[1], count == INNER)
        grads_ref[to, half, at : at + piece, :] = value[start : start + piece]


def middle_kernel(
    core, x_ref, att_ref, logit_ref, code_ref, cot_ref, norm_ref, out_w, up_w, down_w,
    qt_ref, ot_ref, low_ref,
    result_ref, middle_grad_ref, logit_grad_ref, norm_grad_ref, grads_ref, qa_ref, doa_ref, dot_ref,
    att_grad_s, mixed_s, normed_s, hidden_s, pre_s, branch_s, *, count, heads
):
    rows, width = x_ref.shape
    chunk = rows
    hw = width // heads
    gain = norm_ref[...].astype(F32)
    lane = lax.broadcasted_iota(jnp.int32, (chunk, 128), 1)
    head = lax.broadcasted_iota(jnp.int32, (128, width), 0)
    column = lax.broadcasted_iota(jnp.int32, (128, width), 1)
    widen = jnp.where(column // hw == head, 1.0, 0.0).astype(BF)
    narrow = jnp.where(
        lax.broadcasted_iota(jnp.int32, (width, 128), 0) // hw
        == lax.broadcasted_iota(jnp.int32, (width, 128), 1),
        1.0, 0.0,
    ).astype(BF)
    if True:
        at = slice(None)
        code = code_ref[at, :]
        chosen = ((code // heads == lane) | (code % heads == lane)) & (lane < heads)
        lifted = jnp.where(chosen, logit_ref[at, :], -1e30)
        raised = jnp.where(
            chosen, jnp.exp(lifted - jnp.max(lifted, axis=-1, keepdims=True)), 0.0
        )
        gate = raised / jnp.sum(raised, axis=-1, keepdims=True)
        gates = exact_dot(gate, widen)
        attended = att_ref[at, :]
        mixed = (gates * attended).astype(BF)
        mixed_s[at, :] = mixed
        middle = x_ref[at, :].astype(F32) + dot(mixed, out_w[...])
        unit, inverse = norm_parts(middle)
        normed = (unit * gain).astype(BF)
        normed_s[at, :] = normed
        cot = cot_ref[at, :]
        total = middle
        back = jnp.zeros((chunk, width), F32)
        step = 1024
        for c in range(0, up_w.shape[1], step):
            pre = dot(normed, up_w[:, c : c + step])
            inside = 0.7978845608028654 * (pre + 0.044715 * pre * pre * pre)
            t = jnp.tanh(inside)
            half = 0.5 * (1.0 + t)
            hidden = (pre * half).astype(BF)
            slope = half + 0.5 * pre * (1.0 - t * t) * (
                0.7978845608028654 * (1.0 + 3 * 0.044715 * pre * pre)
            )
            hidden_s[at, c : c + step] = hidden
            total = total + dot(hidden, down_w[c : c + step, :])
            pre_grad = (outer(cot, down_w[c : c + step, :]) * slope).astype(BF)
            pre_s[at, c : c + step] = pre_grad
            back = back + outer(pre_grad, up_w[:, c : c + step])
        result_ref[at, :] = total.astype(BF)
        norm_grad_ref[...] = jnp.sum(
            (back * unit).reshape(chunk // 8, 8, width), axis=0
        )
        middle_grad = cot.astype(F32) + norm_back(back, unit, inverse, gain)
        middle_grad_ref[at, :] = middle_grad
        branch = middle_grad.astype(BF)
        branch_s[at, :] = branch
        mixed_grad = outer(branch, out_w[...])
        gate_grad = exact_dot(mixed_grad * attended, narrow)
        logit_grad_ref[at, :] = (
            gate * (gate_grad - jnp.sum(gate * gate_grad, axis=-1, keepdims=True))
        ).astype(BF)
        att_grad_s[at, :] = (gates * mixed_grad).astype(BF)
    prepare_kernel(
        qt_ref, ot_ref, low_ref, att_grad_s, qa_ref, doa_ref, dot_ref,
        nb=qt_ref.shape[0], heads=heads, hw=hw,
    )
    ff = hidden_s.shape[1]
    across = width
    for c in range(0, ff, width):
        put_pieces(grads_ref, core, inner(hidden_s[:, c : c + width], cot), c, ff, 0, count)
    down_rows = ff // 2 // count
    for c in range(0, width, width // 2):
        at = slice(c, c + width // 2)
        up = inner(normed_s[:, at], pre_s[...])
        piece = width // 2 // count
        for k in range(ff // across):
            put_pieces(
                grads_ref, core, up[:, k * across : (k + 1) * across], c, width,
                down_rows + k * piece, count,
            )
        put_pieces(
            grads_ref, core, inner(mixed_s[:, at], branch_s[...]), c, width,
            down_rows + ff // across * piece, count,
        )


def middle_pass(core, x, attended, logits, code, cot, norm_b, out_w, up_w, down_w, kept, heads, count):
    rows, width = x.shape
    nb, hw, lanes = kept[0].shape
    ff = up_w.shape[1]
    piece_rows = (ff * 2 + width) // (2 * count)
    vm = pl.BlockSpec(memory_space=pltpu.VMEM)
    shape = jax.ShapeDtypeStruct
    return pl.pallas_call(
        functools.partial(middle_kernel, count=count, heads=heads),
        out_shape=(
            shape((rows, width), BF),
            shape((rows, width), F32),
            shape((rows, 128), BF),
            shape((8, width), F32),
            shape((count, 2, piece_rows, width), BF),
            shape((nb, lanes, 2 * hw), BF),
            shape((nb, lanes, 2 * hw), BF),
            shape((nb, hw, lanes), BF),
        ),
        in_specs=[pl.BlockSpec(memory_space=pltpu.SMEM)] + [vm] * 12,
        out_specs=(vm,) * 8,
        scratch_shapes=[
            pltpu.VMEM((rows, width), BF),
            pltpu.VMEM((rows, width), BF),
            pltpu.VMEM((rows, width), BF),
            pltpu.VMEM((rows, ff), BF),
            pltpu.VMEM((rows, ff), BF),
            pltpu.VMEM((rows, width), BF),
        ],
        compiler_params=pltpu.CompilerParams(vmem_limit_bytes=60 << 20),
        cost_estimate=pl.CostEstimate(
            flops=9 * 10**9, bytes_accessed=24 << 20, transcendentals=2 * 10**6
        ),
        name="middle_pass",
    )(core, x, attended, logits, code, cot, norm_b, out_w, up_w, down_w, *kept)


class Layout:
    def __init__(self, ctx_count):
        sizes = [4]
        while math.prod(sizes) < ctx_count:
            sizes.append(2)
        assert math.prod(sizes) == ctx_count
        self.sizes = tuple(sizes)
        self.axes = tuple(f"c{k}" for k in range(len(sizes)))
        cut = len(sizes)
        while math.prod(sizes[cut:]) < INNER:
            cut -= 1
        assert math.prod(sizes[cut:]) == INNER
        self.outer_axes, self.inner_axes = self.axes[:cut], self.axes[cut:]
        self.count = ctx_count


def exchange(x, axis, size, step):
    return lax.ppermute(x, axis, [(i, i ^ step) for i in range(size)])


def spread(x, order, lay, start=0, stop=None):
    for axis in order[start:stop]:
        size = lay.sizes[lay.axes.index(axis)]
        x = jnp.concatenate([x] + [exchange(x, axis, size, step) for step in range(1, size)])
    return x


def gather_near(x, lay):
    return spread(x[None], lay.axes[:-2], lay)


def gather_sides(near, lay):
    y_axis, x_axis = lay.axes[-2:]
    return exchange(near, x_axis, 2, 1), exchange(near, y_axis, 2, 1)


def gather_far(near_x, near_y, lay, cut):
    y_axis, x_axis = lay.axes[-2:]
    return exchange(near_x[:, :cut], y_axis, 2, 1), exchange(near_y[:, cut:], x_axis, 2, 1)


def deal(x, lay):
    rows, width = x.shape
    packed = x.reshape(rows // (RUN * INNER), INNER, RUN, width).transpose(1, 0, 2, 3)
    packed = packed.reshape(INNER, rows // INNER, width)
    return lax.all_to_all(packed, lay.inner_axes, 0, 0, tiled=True)


def move_back(x, lay):
    rows, width = x.shape
    return lax.all_to_all(x.reshape(INNER, rows // INNER, width), lay.inner_axes, 0, 0, tiled=True)


def take_back(back):
    rows, width = back.shape[0] * back.shape[1], back.shape[2]
    back = back.reshape(INNER, rows // (RUN * INNER), RUN, width).transpose(1, 0, 2, 3)
    return back.reshape(rows, width)


def tie(*values):
    return lax.optimization_barrier(values)


def order_pieces(pieces, mine, lay):
    if lay.count == INNER:
        return pieces
    index = jnp.arange(lay.count, dtype=jnp.int32)
    quarter = lay.count // 4
    rest = jnp.bitwise_xor(index % quarter, mine // 4)
    return jnp.take(pieces, rest * 4 + index // quarter, axis=0)


def plane_swap(pieces, lay):
    return lax.all_to_all(pieces, lay.axes[-2:], 0, 0, tiled=True)


def plane_sum(pieces):
    return add_pieces(pieces.reshape((4, -1) + pieces.shape[1:]))


def rest_terms(pieces, lay):
    axes = list(zip(lay.axes, lay.sizes))[:-2]
    for k, (axis, size) in enumerate(axes):
        pieces = pieces.reshape((size, -1) + pieces.shape[1:])
        terms = [pieces[0]] + [exchange(pieces[step], axis, size, step) for step in range(1, size)]
        if k < len(axes) - 1:
            pieces = sum(term.astype(F32) for term in terms).astype(BF)
    return [term[0] for term in terms]


def add_pieces(pieces):
    return jnp.sum(pieces.astype(F32), axis=0).astype(BF)


def add_terms(refs):
    total = refs[0][...].astype(F32)
    for ref in refs[1:]:
        total = total + ref[...].astype(F32)
    return total.astype(BF)


def last_kernel(
    core, x_ref, base_ref, middle_grad_ref, logit_ref, norm_b_ref, gain_ref, keyval_w, *rest, heads
):
    first, *terms, grad_ref, small_ref = rest
    rows, width = x_ref.shape
    gain = gain_ref[...].astype(F32)
    unit, inverse = norm_parts(x_ref[...].astype(F32))
    normed = (unit * gain).astype(BF)
    early, late = first[...], add_terms(terms)
    late_rows = rows - early.shape[0]
    keyval_grad = jnp.concatenate([early, late[:late_rows]], axis=0)
    grad = base_ref[...] + outer(keyval_grad, keyval_w[...])
    grad_ref[...] = (middle_grad_ref[...] + norm_back(grad, unit, inverse, gain)).astype(BF)
    keyval_sum = inner(normed, keyval_grad).astype(BF)
    thin = jnp.concatenate(
        [
            inner(logit_ref[...], normed)[:heads],
            jnp.sum(grad * unit, axis=0, keepdims=True),
            jnp.sum(norm_b_ref[...], axis=0, keepdims=True),
            jnp.zeros((-(heads + 2) % 16, width), F32),
        ],
        axis=0,
    ).astype(BF)
    half, query_half = width // 2, (late.shape[0] - late_rows) // 2
    for side in range(2):
        to = jnp.bitwise_xor(core[0], side)
        small_ref[to, :half, :] = keyval_sum[side * half : (side + 1) * half]
        first = half
        for c in range(side * half, (side + 1) * half, 128):
            small_ref[to, first : first + thin.shape[0], :] = thin[:, c : c + 128]
            first += thin.shape[0]
        small_ref[to, first:, :] = late[late_rows + side * query_half :][:query_half]


def last_pass(core, x, base, middle_grad, logit_low, norm_b_part, gain, keyval_w, early, late, heads):
    rows, width = x.shape
    query_half = (late[0].shape[0] + early[0].shape[0] - rows) // 2
    thin_rows = (heads + 2 + -(heads + 2) % 16) * (width // 2) // 128
    sums = width // 2 + thin_rows
    arrays = (x, base, middle_grad, logit_low, norm_b_part, gain, keyval_w, *early, *late)
    vm = pl.BlockSpec(memory_space=pltpu.VMEM)
    grad, small = pl.pallas_call(
        functools.partial(last_kernel, heads=heads),
        out_shape=(
            jax.ShapeDtypeStruct((rows, width), BF),
            jax.ShapeDtypeStruct((2, sums + query_half, 128), BF),
        ),
        grid=(1,),
        in_specs=[pl.BlockSpec(memory_space=pltpu.SMEM)]
        + [pl.BlockSpec(a.shape, lambda g: (0, 0)) for a in arrays],
        out_specs=(vm,) * 2,
        compiler_params=pltpu.CompilerParams(vmem_limit_bytes=40 << 20),
        cost_estimate=pl.CostEstimate(flops=10**9, bytes_accessed=6 << 20, transcendentals=0),
        name="last_pass",
    )(core, *arrays)
    return grad, small, sums


def sum_and_gather(both, sums, lay, beside):
    total, rest = both[:sums], both[sums:][None]
    height = rest.shape[1]
    for axis, size in zip(lay.axes[::-1], lay.sizes[::-1]):
        send = jnp.concatenate([total, rest.reshape(-1, 128)], axis=0)
        got = [exchange(send, axis, size, step) for step in range(1, size)]
        terms = [total.astype(F32)] + [other[:sums].astype(F32) for other in got]
        while len(terms) > 1:
            terms = [terms[k] + terms[k + 1] for k in range(0, len(terms), 2)]
        total = terms[0].astype(BF)
        rest = jnp.concatenate(
            [rest] + [other[sums:].reshape(-1, height, 128) for other in got], axis=0
        )
        if axis == lay.axes[1]:
            total, rest, *arrived = tie(total, rest, *beside)
    return total, rest, arrived


def query_kernel(mine, rest_ref, out_ref, *, count):
    piece = out_ref.shape[0] // count
    for c in range(count):
        at = jnp.bitwise_xor(c, mine[0])
        for k in range(out_ref.shape[1] // 128):
            out_ref[c * piece : (c + 1) * piece, k * 128 : (k + 1) * 128] = rest_ref[
                at, k * piece : (k + 1) * piece, :
            ].astype(F32)


def place_query(mine, rest, shape, lay):
    vm = pl.BlockSpec(memory_space=pltpu.VMEM)
    return pl.pallas_call(
        functools.partial(query_kernel, count=lay.count),
        out_shape=jax.ShapeDtypeStruct(shape, F32),
        in_specs=[pl.BlockSpec(memory_space=pltpu.SMEM), vm],
        out_specs=vm,
        name="place_query",
    )(mine, rest)


def place_kernel(mine, near, near_x, near_y, far_a, far_b, *outs, count, across, sizes):
    cut = far_a.shape[1]
    looped = all(out.shape[0] // count % 8 == 0 for out in outs)

    def one(c, carry):
        s = jnp.bitwise_xor(c, mine[0])
        index = near_index(s // 4, sizes)

        def put(ref, low, high, base):
            first = 0
            for out in outs:
                piece = out.shape[0] // count
                for k in range(out.shape[1] // across):
                    if low <= first < high:
                        rows = pl.ds(pl.multiple_of(c * piece, piece) if looped else c * piece, piece)
                        out[rows, k * across : (k + 1) * across] = ref[
                            index, first - base : first - base + piece, :
                        ].astype(F32)
                    first += piece

        everything = near.shape[1]
        for side, ref in enumerate((near, near_x, near_y)):
            @pl.when(s % 4 == side)
            def _(ref=ref):
                put(ref, 0, everything, 0)

        @pl.when(s % 4 == 3)
        def _():
            put(far_a, 0, cut, 0)
            put(far_b, cut, everything, cut)

        return carry

    if looped:
        lax.fori_loop(0, count, one, 0)
    else:
        for c in range(count):
            one(c, 0)


def place_pieces(pieces, mine, shapes, across, sizes):
    vm = pl.BlockSpec(memory_space=pltpu.VMEM)
    count = 4 * pieces[0].shape[0]
    return pl.pallas_call(
        functools.partial(place_kernel, count=count, across=across, sizes=sizes),
        out_shape=tuple(jax.ShapeDtypeStruct(shape, F32) for shape in shapes),
        in_specs=[pl.BlockSpec(memory_space=pltpu.SMEM)] + [vm] * 5,
        out_specs=(vm,) * len(shapes),
        compiler_params=pltpu.CompilerParams(vmem_limit_bytes=40 << 20),
        cost_estimate=pl.CostEstimate(
            flops=0, bytes_accessed=24 * pieces[0].size, transcendentals=0
        ),
        name="place_pieces",
    )(mine, *pieces)


def layer_norm(values, gain_vec):
    mean_val = jnp.mean(values, axis=-1, keepdims=True)
    centered = values - mean_val
    variance = jnp.mean(centered * centered, axis=-1, keepdims=True)
    return centered * lax.rsqrt(variance + 1e-05) * gain_vec


def on_device(
    lay, inputs, cotangent, segments, routes, norm_first, w_query, w_keyval, w_router, w_out,
    norm_second, w_up, w_down
):
    def whole(shard):
        return lax.all_gather(shard, "w", axis=0, tiled=True)

    rows, width = inputs.shape[1:]
    head_count = w_router.shape[1]
    head_width = w_keyval.shape[1] // 2
    nb = rows // TB
    group_count = lay.count // INNER
    me = lax.axis_index(lay.inner_axes)
    group = lax.axis_index(lay.outer_axes) if lay.outer_axes else jnp.int32(0)
    place = jnp.stack([me, group]).astype(jnp.int32)
    mine = (group * INNER + me).astype(jnp.int32)[None]

    core = lax.axis_index("w")
    near_sizes = lay.sizes[:-2]

    def whole_by_exchange(shard):
        other = exchange(shard, "w", 2, 1)
        return jnp.where(
            core == 0,
            jnp.concatenate([shard, other], axis=0),
            jnp.concatenate([other, shard], axis=0),
        )

    narrow = whole(
        jnp.concatenate([w_keyval, w_router, norm_first[:, None], norm_second[:, None]], axis=1)
    )
    keyval_w = narrow[:, : 2 * head_width]
    narrow = narrow[:, 2 * head_width :]
    router_w = jnp.pad(narrow[:, :head_count], ((0, 0), (0, 128 - head_count)))
    norm_a, norm_b = narrow[:, head_count], narrow[:, head_count + 1]
    own_normed = layer_norm(inputs[0].astype(F32), norm_a.astype(F32)).astype(BF)
    spans = rows // (RUN * INNER)
    own_seg = segments[:, :: RUN * INNER].astype(BF)
    own_seg = jnp.pad(own_seg, ((0, 7), (0, 2 * head_width - spans)))
    near = gather_near(
        jnp.concatenate([dot(own_normed, keyval_w).astype(BF), own_seg], axis=0), lay
    )
    near_x, near_y = gather_sides(near, lay)
    rows_low = deal(inputs[0], lay).reshape(rows, width)
    near_x, near_y, rows_low = tie(near_x, near_y, rows_low)
    far = gather_far(near_x, near_y, lay, (nb // 2) * TB)
    query_w, out_w = whole(w_query), whole(w_out)
    up_w, down_w = whole_by_exchange(w_up), whole_by_exchange(w_down)

    quarter = lay.count // 4
    entry = [near_index(rest, near_sizes) for rest in range(quarter)]
    source = [entry.index(k) * 4 + side for side in range(4) for k in range(quarter)]
    source = jnp.bitwise_xor(jnp.array(source, jnp.int32), mine)
    far_rows = rows - (nb // 2) * TB
    all_seg = jnp.concatenate(
        [near[:, rows], near_x[:, rows], near_y[:, rows], far[1][:, far_rows]], axis=0
    ).astype(jnp.int32)
    at = source[:, None] * spans + jnp.arange(128, dtype=jnp.int32)[None]
    at = jnp.where(jnp.arange(128)[None] < spans, at, -1)
    first = jnp.arange(group_count * nb, dtype=jnp.int32) * (UNIT // (RUN * INNER))
    useg = jnp.sum(jnp.where(at[None] == first[:, None, None], all_seg[None], 0), axis=(1, 2))

    rows_in = rows_low.astype(F32)
    normed = layer_norm(rows_in, norm_a.astype(F32)).astype(BF)
    queries = dot(normed, query_w).astype(BF)
    logits = dot(normed, router_w)

    code = (routes[0, :, 0] * head_count + routes[0, :, 1]).astype(BF)
    slot_rows = rows // INNER
    code = code.reshape(rows // (RUN * INNER), INNER, RUN).transpose(1, 0, 2)
    code = jnp.pad(code.reshape(INNER, 1, slot_rows), ((0, 0), (0, RUN - 1), (0, width - slot_rows)))
    packed = cotangent[0].reshape(rows // (RUN * INNER), INNER, RUN, width).transpose(1, 0, 2, 3)
    packed = jnp.concatenate([packed.reshape(INNER, slot_rows, width), code], axis=1)
    packed, near_x, near_y = tie(packed, near_x, near_y)
    dealt = lax.all_to_all(packed, lay.inner_axes, 0, 0, tiled=True)
    attended, ot, low, qt, kaug, vt = attention_forward(
        useg, place, (near, near_x, near_y) + far, queries, head_count, head_width, near_sizes
    )
    attended, dealt = tie(attended, dealt)
    grad_top = dealt[:, :slot_rows].reshape(rows, width)
    code = dealt[:, slot_rows, :slot_rows].reshape(rows, 1).astype(jnp.int32)
    core_at = jnp.stack([core, me // 4]).astype(jnp.int32)
    result, middle_grad, logit_low, norm_b_part, grads, qa, doa, dot_t = middle_pass(
        core_at, rows_low, attended, logits, code, grad_top, norm_b[None], out_w, up_w, down_w,
        (qt, ot, low), head_count, lay.count,
    )
    grads = grads.reshape(lay.count, -1, width)
    grads, qa = tie(grads, qa)
    swapped = plane_swap(order_pieces(grads, mine, lay), lay)
    normed_t = normed.T

    def backward(first, stop, dq):
        return attention_backward(
            useg, place, kaug, vt, qa, doa, qt, dot_t, dq, normed_t, tuple(range(first, stop)),
            head_count, head_width,
        )

    one, two = 4 * nb // 10, 7 * nb // 10
    dq, dkv_a = backward(0, one, None)
    dq, dkv_a, swapped = tie(dq, dkv_a, swapped)
    halves = plane_sum(swapped)
    halves = halves.reshape(halves.shape[0], 2, -1, width)
    weights_own = lax.dynamic_index_in_dim(halves, core, 1, keepdims=False)
    weights_other = exchange(
        lax.dynamic_index_in_dim(halves, 1 - core, 1, keepdims=False), "w", 2, 1
    )
    back = move_back(result, lay)
    dq, dkv_b = backward(one, two, dq)
    dq, dkv_b, back, weights_other = tie(dq, dkv_b, back, weights_other)
    output = take_back(back)
    weight_terms = rest_terms(
        (weights_own.astype(F32) + weights_other.astype(F32)).astype(BF), lay
    )
    swapped = plane_swap(
        order_pieces(jnp.concatenate([dkv_a, dkv_b], axis=1), mine, lay), lay
    )
    dq, late = backward(two, nb, dq)
    dq, late, swapped, *weight_terms = tie(dq, late, swapped, *weight_terms)
    early = rest_terms(plane_sum(swapped), lay)
    weights_near = gather_near(sum(term.astype(F32) for term in weight_terms).astype(BF), lay)
    if lay.count != INNER:
        query_w_grad = inner(normed, dq).astype(BF)
        piece = width // 2 // lay.count
        query_parts = query_w_grad.reshape(2, lay.count, piece, width // 128, 128)
        query_parts = query_parts.transpose(1, 0, 3, 2, 4).reshape(lay.count, -1, 128)
        late = order_pieces(jnp.concatenate([late, query_parts], axis=1), mine, lay)
    swapped = plane_swap(late, lay)
    base = outer(dq, query_w) + outer(logit_low, router_w)
    early = sum(term.astype(F32) for term in early).astype(BF)
    swapped, base, early = tie(swapped, base, early)
    late = rest_terms(plane_sum(swapped), lay)
    base, weights_near, *late = tie(base, weights_near, *late)
    grad_rows, small, sums = last_pass(
        core_at, rows_low, base, middle_grad, logit_low, norm_b_part, norm_a[None], keyval_w,
        [early], late, head_count,
    )
    back = move_back(grad_rows, lay)
    other = exchange(small[1], "w", 2, 1)
    weights_x, weights_y = gather_sides(weights_near, lay)
    both = (small[0].astype(F32) + other.astype(F32)).astype(BF)
    total, rest, (back, weights_x, weights_y) = sum_and_gather(
        both, sums, lay, (back, weights_x, weights_y)
    )
    weights_far = gather_far(weights_x, weights_y, lay, w_down.shape[0] // lay.count)
    input_grad = take_back(back).astype(F32)[None]
    query_sum = place_query(mine, rest, w_query.shape, lay)
    half = width // 2
    keyval_sum = total[:half].astype(F32)
    thin = total[half:].reshape(half // 128, -1, 128).transpose(1, 0, 2).reshape(-1, half)
    thin = thin.astype(F32)
    down_sum, up_sum, out_sum = place_pieces(
        (weights_near, weights_x, weights_y, *weights_far), mine,
        [w_down.shape, w_up.shape, w_out.shape], width, near_sizes,
    )
    return (
        output[None],
        input_grad,
        thin[head_count],
        query_sum,
        keyval_sum,
        thin[:head_count].T,
        out_sum,
        thin[head_count + 1],
        up_sum,
        down_sum,
    )


def solution(mesh):
    ctx_count, core_count = mesh.shape["ctx"], mesh.shape["wshard"]
    lay = Layout(ctx_count)
    grid = Mesh(mesh.devices.reshape(lay.sizes + (core_count,)), lay.axes + ("w",))
    ctx = lay.axes
    tokens = P("w", ctx, None)
    return jax.shard_map(
        functools.partial(on_device, lay),
        mesh=grid,
        in_specs=(
            tokens, tokens, P("w", ctx), tokens,
            P("w"), P("w", None), P("w", None), P("w", None), P("w", None),
            P("w"), P("w", None), P("w", None),
        ),
        out_specs=(
            tokens, tokens,
            P("w"), P("w", None), P("w", None), P("w", None), P("w", None),
            P("w"), P("w", None), P("w", None),
        ),
        check_vma=False,
    )
```

```python
import functools
import math

import jax
import jax.numpy as jnp
from jax import lax
from jax.experimental import pallas as pl
from jax.experimental.pallas import tpu as pltpu
from jax.sharding import Mesh, PartitionSpec as P

F32 = jnp.float32
BF = jnp.bfloat16
UNIT = 1024
TB = 64
INNER = UNIT // TB
RUN = 8
LOG2E = 1.4426950408889634
BIG = 2.0**100


def dot(lhs, rhs):
    return lax.dot_general(lhs, rhs, (((1,), (0,)), ((), ())), preferred_element_type=F32)


def inner(lhs, rhs):
    return lax.dot_general(lhs, rhs, (((0,), (0,)), ((), ())), preferred_element_type=F32)


def outer(lhs, rhs):
    return lax.dot_general(lhs, rhs, (((1,), (1,)), ((), ())), preferred_element_type=F32)


def split3(x):
    a = x.astype(BF)
    rest = x - a.astype(F32)
    b = rest.astype(BF)
    return a, b, (rest - b.astype(F32)).astype(BF)


def to_lanes(x, heads, hw):
    xt = x.T
    return jnp.concatenate([xt[h * hw : (h + 1) * hw] for h in range(heads)], axis=1)


def query_offsets(index, me):
    rest = index & (TB - 1)
    return (rest >> 3) * (RUN * INNER) + me * RUN + (rest & 7)


def near_index(rest, sizes):
    digits = []
    for size in sizes[::-1]:
        digits.append(rest % size)
        rest = rest // size
    index = 0
    for digit, size in zip(digits, sizes[::-1]):
        index = index * size + digit
    return index


def fetch_pieces(pieces, count, sizes, mine, total, put):
    near, near_x, near_y, far_a, far_b = pieces
    cut = far_a.shape[1]

    def one(c, carry):
        s = jnp.bitwise_xor(c, mine)
        index = near_index(s // 4, sizes)
        for side, ref in enumerate((near, near_x, near_y)):
            @pl.when(s % 4 == side)
            def _(ref=ref):
                put(c, 0, ref[index, :total, :])

        @pl.when(s % 4 == 3)
        def _():
            put(c, 0, far_a[index])
            put(c, cut, far_b[index, : total - cut, :])

        return carry

    lax.fori_loop(0, count, one, 0)


def fwd_kernel(
    useg, place, near, near_x, near_y, far_a, far_b, q_ref, o_ref, ot_ref, l_ref, qt_ref, kaug, vt, order,
    qa, acc, ref_row, plist, rank, ranked, bad, *, nb, slots, heads, hw, sizes, turns
):
    me, group = place[0], place[1]
    scale = LOG2E / math.sqrt(hw)
    lanes = heads * TB
    units = slots * nb

    def scan(u, n):
        rank[u] = n
        plist[n] = u
        return n + jnp.where(useg[u] == 0, 1, 0)

    prompt_units = lax.fori_loop(0, units, scan, jnp.int32(0))

    def settle(u, after):
        others = u - rank[u]
        ranked[jnp.where(useg[u] == 0, rank[u], prompt_units + others)] = u
        return after

    lax.fori_loop(0, units, settle, 0)
    for k in range(units):
        order[k] = ranked[turns[k]] if slots == 1 else k
    lane = lax.broadcasted_iota(jnp.int32, (UNIT, 2 * hw), 1)
    row = lax.broadcasted_iota(jnp.int32, (2 * hw, UNIT), 0)
    extra = jnp.where(lane < hw + 3, 1.0, 0.0).astype(BF)

    def put(c, first, rows):
        at = pl.multiple_of(c * nb * TB + first, TB)
        kaug[pl.ds(at, rows.shape[0]), :] = rows

    fetch_pieces(
        (near, near_x, near_y, far_a, far_b), slots * INNER, sizes, group * INNER + me, nb * TB, put
    )

    def split(u, carry):
        rows = pl.ds(pl.multiple_of(u * UNIT, UNIT), UNIT)
        tile = kaug[rows, :]
        kaug[rows, :] = jnp.where(lane < hw, tile, extra)
        flip = tile.T
        vt[u] = jnp.where(row < hw, jnp.ones_like(flip), flip)
        return carry

    lax.fori_loop(0, units, split, 0)

    def keys_of(u):
        return kaug[pl.ds(pl.multiple_of(u * UNIT, UNIT), UNIT), :]

    def block(i, carry):
        own = group * nb + i
        full_units = jnp.where(useg[own] != 0, prompt_units, rank[own])
        rows = pl.ds(pl.multiple_of(i * TB, TB), TB)
        qt = to_lanes(q_ref[rows, :], heads, hw)
        qt_ref[i] = qt
        qa[0:hw, :] = qt
        qa[hw:, :] = jnp.zeros((hw, lanes), BF)
        mask = lax.broadcasted_iota(jnp.int32, (UNIT, lanes), 0) <= query_offsets(
            lax.broadcasted_iota(jnp.int32, (UNIT, lanes), 1), me
        )
        few = UNIT // 4
        keys = kaug[pl.ds(pl.multiple_of(own * UNIT, UNIT), few), :]
        ref_row[...] = jnp.max(
            jnp.where(mask[:few], dot(keys, qa[...]), -1e30), axis=0, keepdims=True
        )
        bad[0] = 1

        def attempt(turn, carry):
            @pl.when(bad[0] != 0)
            def _():
                @pl.when(turn == 1)
                def _():
                    qa[hw:, :] = jnp.zeros((hw, lanes), BF)

                    def highest(k, carry):
                        u = jnp.where(k // 4 < full_units, plist[k // 4], own)
                        first = k % 4 * few
                        keys = kaug[pl.ds(pl.multiple_of(u * UNIT + first, few), few), :]
                        usable = first + lax.broadcasted_iota(
                            jnp.int32, (few, lanes), 0
                        ) <= query_offsets(lax.broadcasted_iota(jnp.int32, (few, lanes), 1), me)
                        ref_row[...] = jnp.maximum(
                            ref_row[...],
                            jnp.max(
                                jnp.where(usable | (u != own), dot(keys, qa[...]), -1e30),
                                axis=0, keepdims=True,
                            ),
                        )
                        return carry

                    lax.fori_loop(0, 4 * full_units + 4, highest, 0)

                a, b, c = split3(-ref_row[...])
                qa[hw:, :] = jnp.concatenate([a, b, c, jnp.zeros((hw - 3, lanes), BF)], axis=0)
                s = jnp.where(mask, dot(keys_of(own), qa[...]) * scale, -1e30)
                acc[...] = dot(vt[own], jnp.exp2(s).astype(BF))

                def full(k, carry):
                    u = plist[k]
                    p = jnp.exp2(dot(keys_of(u), qa[...]) * scale).astype(BF)
                    acc[...] += dot(vt[u], p)
                    return carry

                lax.fori_loop(0, full_units, full, 0)
                bad[0] = jnp.where(jnp.max(acc[0:1, :]) < BIG, 0, 1)

            return carry

        lax.fori_loop(0, 2, attempt, 0)
        ot = acc[hw:, :] / acc[0:hw, :]
        ot_ref[i] = ot
        l_ref[i] = ref_row[...] + jnp.log2(acc[0:1, :]) / scale
        on = jnp.concatenate([ot[:, h * TB : (h + 1) * TB] for h in range(heads)], axis=0)
        o_ref[rows, :] = on.T
        return carry

    lax.fori_loop(0, nb, block, 0)


def attention_forward(useg, place, pieces, q, heads, hw, sizes, turns):
    rows = q.shape[0]
    nb = rows // TB
    slots = 4 * pieces[0].shape[0] // INNER
    lanes = heads * TB
    units = slots * nb
    vm = pl.BlockSpec(memory_space=pltpu.VMEM)
    sm = pl.BlockSpec(memory_space=pltpu.SMEM)
    return pl.pallas_call(
        functools.partial(fwd_kernel, nb=nb, slots=slots, heads=heads, hw=hw, sizes=sizes, turns=turns),
        out_shape=(
            jax.ShapeDtypeStruct((rows, heads * hw), F32),
            jax.ShapeDtypeStruct((nb, hw, lanes), F32),
            jax.ShapeDtypeStruct((nb, 1, lanes), F32),
            jax.ShapeDtypeStruct((nb, hw, lanes), BF),
            jax.ShapeDtypeStruct((units * UNIT, 2 * hw), BF),
            jax.ShapeDtypeStruct((units, 2 * hw, UNIT), BF),
            jax.ShapeDtypeStruct((units,), jnp.int32),
        ),
        in_specs=[sm, sm] + [vm] * 6,
        out_specs=(vm,) * 6 + (sm,),
        scratch_shapes=[
            pltpu.VMEM((2 * hw, lanes), BF),
            pltpu.VMEM((2 * hw, lanes), F32),
            pltpu.VMEM((1, lanes), F32),
            pltpu.SMEM((units + 1,), jnp.int32),
            pltpu.SMEM((units + 1,), jnp.int32),
            pltpu.SMEM((units + 1,), jnp.int32),
            pltpu.SMEM((1,), jnp.int32),
        ],
        compiler_params=pltpu.CompilerParams(vmem_limit_bytes=60 << 20),
        cost_estimate=pl.CostEstimate(
            flops=40 * 10**9, bytes_accessed=8 << 20, transcendentals=26 * 10**6
        ),
        name="attention_forward",
    )(useg, place, *pieces, q)


def prepare_kernel(qt_ref, ot_ref, l_ref, do_ref, qa_ref, doa_ref, dot_ref, *, nb, heads, hw):
    pad = jnp.zeros((hw - 3, heads * TB), BF)

    def prepare(i, carry):
        rows = pl.ds(pl.multiple_of(i * TB, TB), TB)
        a, b, c = split3(-l_ref[i])
        qa_ref[i] = jnp.concatenate([qt_ref[i], a, b, c, pad], axis=0).T
        dt = to_lanes(do_ref[rows, :], heads, hw)
        dot_ref[i] = dt
        total = jnp.sum(dt.astype(F32) * ot_ref[i], axis=0, keepdims=True)
        a, b, c = split3(-total)
        doa_ref[i] = jnp.concatenate([a, b, c, pad, dt], axis=0).T
        return carry

    lax.fori_loop(0, nb, prepare, 0)


def bwd_kernel(
    useg, place, order, kaug_ref, vt_ref, qa, doa, qt, dot_t, *rest,
    nb, parts, first, last, dealt, heads, hw
):
    if first:
        dqacc, dkv_ref, kt, dkvt = rest
    elif last:
        dqold, normed, dq_ref, dkv_ref, dqacc, kt, dkvt = rest
    else:
        dqold, _, dqacc, dkv_ref, kt, dkvt = rest
    grid_at = pl.program_id(0)
    steps = pl.num_programs(0) - (2 if last and dealt else 0)
    step_at = jnp.minimum(grid_at, steps - 1)
    me, group = place[0], place[1]
    unit = order[step_at // len(parts) * nb + step_at % len(parts) + parts[0]]
    scale = LOG2E / math.sqrt(hw)
    lanes = heads * TB

    @pl.when(grid_at == 0)
    def _():
        dqacc[...] = jnp.zeros_like(dqacc) if first else dqold[...]

    unit_seg = useg[unit]

    def block(i, carry):
        own = group * nb + i

        def step(first, size, masked):
            keys = pl.ds(first, size)
            s = dot(qa[i], kt[:, keys]) * scale
            if masked:
                mask = first + lax.broadcasted_iota(
                    jnp.int32, (lanes, size), 1
                ) <= query_offsets(lax.broadcasted_iota(jnp.int32, (lanes, size), 0), me)
                s = jnp.where(mask, s, -1e30)
            p = jnp.exp2(s)
            ds = (p * dot(doa[i], vt_ref[0, :, keys])).astype(BF)
            dkvt[hw:, keys] += dot(dot_t[i], p.astype(BF))
            dkvt[:hw, keys] += dot(qt[i], ds)
            dqacc[i] += dot(ds, kaug_ref[keys, :])

        @pl.when((unit_seg == 0) & (own != unit) & ((useg[own] != 0) | (own > unit)))
        def _():
            step(0, UNIT, False)

        @pl.when(own == unit)
        def _():
            def part_of_own(k, carry):
                step(pl.multiple_of(k * (UNIT // 2), UNIT // 2), UNIT // 2, True)
                return carry

            lax.fori_loop(0, 2, part_of_own, 0)

        return carry

    def keys():
        kt[...] = kaug_ref[...].T
        dkvt[...] = jnp.zeros_like(dkvt)
        lax.fori_loop(0, nb, block, 0)
        factor = jnp.where(
            lax.broadcasted_iota(jnp.int32, (2 * hw, 1), 0) < hw, 1 / math.sqrt(hw), 1.0
        )
        dkv = (dkvt[...] * factor).T.reshape(TB // RUN, INNER, RUN, 2 * hw)
        for d in range(INNER):
            to = piece_at(d, me // 4, dealt)
            dkv_ref[to] = dkv[:, d].reshape(TB, 2 * hw).astype(BF)

    if last and dealt:
        pl.when(grid_at < steps)(keys)
    else:
        keys()

    if last:
        @pl.when(grid_at == steps - 1)
        def _():
            def finish(i, carry):
                rows = pl.ds(pl.multiple_of(i * TB, TB), TB)
                a = dqacc[i]
                dq_ref[rows, :] = (
                    jnp.concatenate([a[h * TB : (h + 1) * TB, :hw] for h in range(heads)], axis=1)
                    * (1 / math.sqrt(hw))
                ).astype(BF)
                return carry

            lax.fori_loop(0, nb, finish, 0)

    if last and dealt:
        @pl.when(grid_at >= steps)
        def _():
            width = dq_ref.shape[1]
            half = width // 2
            rows = pl.ds(pl.multiple_of((grid_at - steps) * half, half), half)
            grad = dot(normed[rows, :], dq_ref[...]).astype(BF)
            piece = half // INNER
            for c in range(INNER):
                to = piece_at(c, me // 4, dealt)
                for k in range(width // 128):
                    dkv_ref[to, k * piece : (k + 1) * piece, :] = grad[
                        c * piece : (c + 1) * piece, k * 128 : (k + 1) * 128
                    ]


def attention_backward(
    useg, place, order, kaug, vt, qa, doa, qt, dot_t, dqold, more_in, parts, joint, heads, hw
):
    nb, lanes, _ = qa.shape
    slots = vt.shape[0] // nb
    first, last = dqold is None, parts[-1] == nb - 1
    dealt = slots == 1
    more = 2 if last and dealt else 0
    turns_out = len(parts) + more if last else joint
    base = 0 if last else parts[0]
    vm = pl.BlockSpec(memory_space=pltpu.VMEM)
    acc_shape = jax.ShapeDtypeStruct((nb, lanes, 2 * hw), F32)
    count = len(parts)

    def at(u, seg, place, order):
        u = jnp.minimum(u, slots * count - 1)
        return order[u // count * nb + u % count + parts[0]]

    def to(u, seg, place, order):
        if dealt:
            return (0, u + base, 0)
        return (u // count, u % count + base, 0)

    return pl.pallas_call(
        functools.partial(
            bwd_kernel, nb=nb, parts=parts, first=first, last=last, dealt=dealt, heads=heads, hw=hw
        ),
        out_shape=(
            jax.ShapeDtypeStruct((nb * TB, heads * hw), BF) if last else acc_shape,
            jax.ShapeDtypeStruct((slots * INNER, turns_out * TB, 2 * hw), BF),
        ),
        grid_spec=pltpu.PrefetchScalarGridSpec(
            num_scalar_prefetch=3,
            grid=(slots * count + more,),
            in_specs=[
                pl.BlockSpec((UNIT, 2 * hw), lambda *a: (at(*a), 0)),
                pl.BlockSpec((1, 2 * hw, UNIT), lambda *a: (at(*a), 0, 0)),
            ]
            + [vm] * (4 if first else 6 if last else 5)
            + ([] if first or last else [pl.BlockSpec(memory_space=pl.ANY)]),
            out_specs=(
                vm,
                pl.BlockSpec((INNER, TB, 2 * hw), to),
            ),
            scratch_shapes=([pltpu.VMEM(acc_shape.shape, F32)] if last and not first else [])
            + [
                pltpu.VMEM((2 * hw, UNIT), BF),
                pltpu.VMEM((2 * hw, UNIT), F32),
            ],
        ),
        compiler_params=pltpu.CompilerParams(vmem_limit_bytes=60 << 20),
        cost_estimate=pl.CostEstimate(
            flops=8 * 10**9 * count, bytes_accessed=12 << 20, transcendentals=2 * 10**6 * count
        ),
        input_output_aliases={} if first or last else {10: 1},
        name="attention_backward",
    )(useg, place, order, kaug, vt, qa, doa, qt, dot_t, *([] if first else [dqold, more_in]))


def exact_dot(x, ones):
    a, b, c = split3(x)
    return dot(a, ones) + dot(b, ones) + dot(c, ones)


def norm_parts(values):
    mean_val = jnp.mean(values, axis=-1, keepdims=True)
    centered = values - mean_val
    variance = jnp.mean(centered * centered, axis=-1, keepdims=True)
    inverse = lax.rsqrt(variance + 1e-05)
    return centered * inverse, inverse


def norm_back(grad, unit, inverse, gain):
    scaled = grad * gain
    shift = jnp.mean(scaled, axis=-1, keepdims=True)
    along = jnp.mean(scaled * unit, axis=-1, keepdims=True)
    return inverse * (scaled - shift - unit * along)


def piece_at(c, my_rest, dealt):
    return c % 4 * (INNER // 4) + jnp.bitwise_xor(c // 4, my_rest) if dealt else c


def put_pieces(grads_ref, where, value, first, rows, at, count, step):
    piece = rows // 2 // count
    value = value.astype(BF)
    half = first // (rows // 2)
    device = (first - half * (rows // 2)) // piece
    for k in range(step // piece):
        to = piece_at(device + k, where[1], count == INNER)
        grads_ref[to, half, at : at + piece, :] = value[k * piece : (k + 1) * piece]


def middle_kernel(
    where, x_ref, att_ref, logit_ref, code_ref, cot_ref, norm_ref, out_w, up_w, down_w,
    qt_ref, ot_ref, low_ref,
    result_ref, middle_grad_ref, logit_grad_ref, norm_grad_ref, grads_ref, qa_ref, doa_ref, dot_ref,
    att_grad_s, mixed_s, normed_s, hidden_s, pre_s, branch_s, *, count, heads
):
    rows, width = x_ref.shape
    chunk = rows
    hw = width // heads
    gain = norm_ref[...].astype(F32)
    lane = lax.broadcasted_iota(jnp.int32, (chunk, 128), 1)
    head = lax.broadcasted_iota(jnp.int32, (128, width), 0)
    column = lax.broadcasted_iota(jnp.int32, (128, width), 1)
    widen = jnp.where(column // hw == head, 1.0, 0.0).astype(BF)
    narrow = jnp.where(
        lax.broadcasted_iota(jnp.int32, (width, 128), 0) // hw
        == lax.broadcasted_iota(jnp.int32, (width, 128), 1),
        1.0, 0.0,
    ).astype(BF)
    if True:
        at = slice(None)
        code = code_ref[at, :]
        chosen = ((code // heads == lane) | (code % heads == lane)) & (lane < heads)
        lifted = jnp.where(chosen, logit_ref[at, :], -1e30)
        raised = jnp.where(
            chosen, jnp.exp(lifted - jnp.max(lifted, axis=-1, keepdims=True)), 0.0
        )
        gate = raised / jnp.sum(raised, axis=-1, keepdims=True)
        gates = exact_dot(gate, widen)
        attended = att_ref[at, :]
        mixed = (gates * attended).astype(BF)
        mixed_s[at, :] = mixed
        middle = x_ref[at, :].astype(F32) + dot(mixed, out_w[...])
        unit, inverse = norm_parts(middle)
        normed = (unit * gain).astype(BF)
        normed_s[at, :] = normed
        cot = cot_ref[at, :]
        back = jnp.zeros((chunk, width), F32)
        step = 512

        def hidden_block(k, sums):
            total, back = sums
            to = pl.ds(pl.multiple_of(k * step, step), step)
            pre = dot(normed, up_w[:, to])
            inside = 0.7978845608028654 * (pre + 0.044715 * pre * pre * pre)
            t = jnp.tanh(inside)
            half = 0.5 * (1.0 + t)
            hidden = (pre * half).astype(BF)
            slope = half + 0.5 * pre * (1.0 - t * t) * (
                0.7978845608028654 * (1.0 + 3 * 0.044715 * pre * pre)
            )
            hidden_s[:, to] = hidden
            pre_grad = (outer(cot, down_w[to, :]) * slope).astype(BF)
            pre_s[:, to] = pre_grad
            return total + dot(hidden, down_w[to, :]), back + outer(pre_grad, up_w[:, to])

        total, back = lax.fori_loop(0, up_w.shape[1] // step, hidden_block, (middle, back))
        result_ref[at, :] = total.astype(BF)
        norm_grad_ref[...] = jnp.sum(
            (back * unit).reshape(chunk // 8, 8, width), axis=0
        )
        middle_grad = cot.astype(F32) + norm_back(back, unit, inverse, gain)
        middle_grad_ref[at, :] = middle_grad
        branch = middle_grad.astype(BF)
        branch_s[at, :] = branch
        mixed_grad = outer(branch, out_w[...])
        gate_grad = exact_dot(mixed_grad * attended, narrow)
        logit_grad_ref[at, :] = (
            gate * (gate_grad - jnp.sum(gate * gate_grad, axis=-1, keepdims=True))
        ).astype(BF)
        att_grad_s[at, :] = (gates * mixed_grad).astype(BF)
    prepare_kernel(
        qt_ref, ot_ref, low_ref, att_grad_s, qa_ref, doa_ref, dot_ref,
        nb=qt_ref.shape[0], heads=heads, hw=hw,
    )
    ff = hidden_s.shape[1]
    across = width
    half, down_rows = width // 2, ff // 2 // count

    def down_block(k, carry):
        at = pl.ds(pl.multiple_of(k * width, width), width)
        put_pieces(grads_ref, where, inner(hidden_s[:, at], cot), k * width, ff, 0, count, width)
        return carry

    lax.fori_loop(0, ff // width, down_block, 0)

    def up_block(k, carry):
        at = pl.ds(pl.multiple_of(k * half, half), half)
        up = inner(normed_s[:, at], pre_s[...])
        piece = half // count
        for c in range(ff // width):
            put_pieces(
                grads_ref, where, up[:, c * width : (c + 1) * width], k * half, width,
                down_rows + c * piece, count, half,
            )
        put_pieces(
            grads_ref, where, inner(mixed_s[:, at], branch_s[...]), k * half, width,
            down_rows + ff // width * piece, count, half,
        )
        return carry

    lax.fori_loop(0, 2, up_block, 0)


def middle_pass(core, x, attended, logits, code, cot, norm_b, out_w, up_w, down_w, kept, heads, count):
    rows, width = x.shape
    nb, hw, lanes = kept[0].shape
    ff = up_w.shape[1]
    piece_rows = (ff * 2 + width) // (2 * count)
    vm = pl.BlockSpec(memory_space=pltpu.VMEM)
    shape = jax.ShapeDtypeStruct
    return pl.pallas_call(
        functools.partial(middle_kernel, count=count, heads=heads),
        out_shape=(
            shape((rows, width), BF),
            shape((rows, width), F32),
            shape((rows, 128), BF),
            shape((8, width), F32),
            shape((count, 2, piece_rows, width), BF),
            shape((nb, lanes, 2 * hw), BF),
            shape((nb, lanes, 2 * hw), BF),
            shape((nb, hw, lanes), BF),
        ),
        in_specs=[pl.BlockSpec(memory_space=pltpu.SMEM)] + [vm] * 12,
        out_specs=(vm,) * 8,
        scratch_shapes=[
            pltpu.VMEM((rows, width), BF),
            pltpu.VMEM((rows, width), BF),
            pltpu.VMEM((rows, width), BF),
            pltpu.VMEM((rows, ff), BF),
            pltpu.VMEM((rows, ff), BF),
            pltpu.VMEM((rows, width), BF),
        ],
        compiler_params=pltpu.CompilerParams(vmem_limit_bytes=60 << 20),
        cost_estimate=pl.CostEstimate(
            flops=9 * 10**9, bytes_accessed=24 << 20, transcendentals=2 * 10**6
        ),
        name="middle_pass",
    )(core, x, attended, logits, code, cot, norm_b, out_w, up_w, down_w, *kept)


class Layout:
    def __init__(self, ctx_count):
        sizes = [4]
        while math.prod(sizes) < ctx_count:
            sizes.append(2)
        assert math.prod(sizes) == ctx_count
        self.sizes = tuple(sizes)
        self.axes = tuple(f"c{k}" for k in range(len(sizes)))
        cut = len(sizes)
        while math.prod(sizes[cut:]) < INNER:
            cut -= 1
        assert math.prod(sizes[cut:]) == INNER
        self.outer_axes, self.inner_axes = self.axes[:cut], self.axes[cut:]
        self.count = ctx_count


def exchange(x, axis, size, step):
    return lax.ppermute(x, axis, [(i, i ^ step) for i in range(size)])


def spread(x, order, lay, start=0, stop=None):
    for axis in order[start:stop]:
        size = lay.sizes[lay.axes.index(axis)]
        x = jnp.concatenate([x] + [exchange(x, axis, size, step) for step in range(1, size)])
    return x


def gather_near(x, lay):
    return spread(x[None], lay.axes[:-2], lay)


def gather_sides(near, lay):
    y_axis, x_axis = lay.axes[-2:]
    return exchange(near, x_axis, 2, 1), exchange(near, y_axis, 2, 1)


def gather_far(near_x, near_y, lay, cut):
    y_axis, x_axis = lay.axes[-2:]
    return exchange(near_x[:, :cut], y_axis, 2, 1), exchange(near_y[:, cut:], x_axis, 2, 1)


def deal(x, lay):
    rows, width = x.shape
    packed = x.reshape(rows // (RUN * INNER), INNER, RUN, width).transpose(1, 0, 2, 3)
    packed = packed.reshape(INNER, rows // INNER, width)
    return lax.all_to_all(packed, lay.inner_axes, 0, 0, tiled=True)


def move_back(x, lay):
    rows, width = x.shape
    return lax.all_to_all(x.reshape(INNER, rows // INNER, width), lay.inner_axes, 0, 0, tiled=True)


def take_back(back):
    rows, width = back.shape[0] * back.shape[1], back.shape[2]
    back = back.reshape(INNER, rows // (RUN * INNER), RUN, width).transpose(1, 0, 2, 3)
    return back.reshape(rows, width)


def tie(*values):
    return lax.optimization_barrier(values)


def order_pieces(pieces, mine, lay):
    if lay.count == INNER:
        return pieces
    index = jnp.arange(lay.count, dtype=jnp.int32)
    quarter = lay.count // 4
    rest = jnp.bitwise_xor(index % quarter, mine // 4)
    return jnp.take(pieces, rest * 4 + index // quarter, axis=0)


def plane_swap(pieces, lay):
    return lax.all_to_all(pieces, lay.axes[-2:], 0, 0, tiled=True)


def plane_sum(pieces):
    return add_pieces(pieces.reshape((4, -1) + pieces.shape[1:]))


def rest_terms(pieces, lay):
    axes = list(zip(lay.axes, lay.sizes))[:-2]
    for k, (axis, size) in enumerate(axes):
        pieces = pieces.reshape((size, -1) + pieces.shape[1:])
        terms = [pieces[0]] + [exchange(pieces[step], axis, size, step) for step in range(1, size)]
        if k < len(axes) - 1:
            pieces = sum(term.astype(F32) for term in terms).astype(BF)
    return [term[0] for term in terms]


def add_pieces(pieces):
    return jnp.sum(pieces.astype(F32), axis=0).astype(BF)


def add_terms(refs):
    total = refs[0][...].astype(F32)
    for ref in refs[1:]:
        total = total + ref[...].astype(F32)
    return total.astype(BF)


def last_kernel(
    core, order, x_ref, base_ref, middle_grad_ref, logit_ref, norm_b_ref, gain_ref, keyval_w, *rest,
    heads, dealt
):
    first, *terms, grad_ref, small_ref, keyval_s = rest
    rows, width = x_ref.shape
    gain = gain_ref[...].astype(F32)
    unit, inverse = norm_parts(x_ref[...].astype(F32))
    normed = (unit * gain).astype(BF)
    early, late = first[...], add_terms(terms)
    late_rows = rows - early.shape[0]
    turned = jnp.concatenate([early, late[:late_rows]], axis=0)
    for k in range(rows // TB):
        to = pl.multiple_of((order[k] if dealt else k) * TB, TB)
        keyval_s[pl.ds(to, TB), :] = turned[k * TB : (k + 1) * TB]
    keyval_grad = keyval_s[...]
    grad = base_ref[...] + outer(keyval_grad, keyval_w[...])
    grad_ref[...] = (middle_grad_ref[...] + norm_back(grad, unit, inverse, gain)).astype(BF)
    keyval_sum = inner(normed, keyval_grad).astype(BF)
    thin = jnp.concatenate(
        [
            inner(logit_ref[...], normed)[:heads],
            jnp.sum(grad * unit, axis=0, keepdims=True),
            jnp.sum(norm_b_ref[...], axis=0, keepdims=True),
            jnp.zeros((-(heads + 2) % 16, width), F32),
        ],
        axis=0,
    ).astype(BF)
    half, query_half = width // 2, (late.shape[0] - late_rows) // 2
    for side in range(2):
        to = jnp.bitwise_xor(core[0], side)
        small_ref[to, :half, :] = keyval_sum[side * half : (side + 1) * half]
        first = half
        for c in range(side * half, (side + 1) * half, 128):
            small_ref[to, first : first + thin.shape[0], :] = thin[:, c : c + 128]
            first += thin.shape[0]
        small_ref[to, first:, :] = late[late_rows + side * query_half :][:query_half]


def last_pass(core, order, dealt, x, base, middle_grad, logit_low, norm_b_part, gain, keyval_w, early, late, heads):
    rows, width = x.shape
    query_half = (late[0].shape[0] + early[0].shape[0] - rows) // 2
    thin_rows = (heads + 2 + -(heads + 2) % 16) * (width // 2) // 128
    sums = width // 2 + thin_rows
    arrays = (x, base, middle_grad, logit_low, norm_b_part, gain, keyval_w, *early, *late)
    vm = pl.BlockSpec(memory_space=pltpu.VMEM)
    grad, small = pl.pallas_call(
        functools.partial(last_kernel, heads=heads, dealt=dealt),
        out_shape=(
            jax.ShapeDtypeStruct((rows, width), BF),
            jax.ShapeDtypeStruct((2, sums + query_half, 128), BF),
        ),
        grid=(1,),
        in_specs=[pl.BlockSpec(memory_space=pltpu.SMEM)] * 2
        + [pl.BlockSpec(a.shape, lambda g: (0, 0)) for a in arrays],
        out_specs=(vm,) * 2,
        scratch_shapes=[pltpu.VMEM((rows, keyval_w.shape[1]), BF)],
        compiler_params=pltpu.CompilerParams(vmem_limit_bytes=40 << 20),
        cost_estimate=pl.CostEstimate(flops=10**9, bytes_accessed=6 << 20, transcendentals=0),
        name="last_pass",
    )(core, order, *arrays)
    return grad, small, sums


def sum_and_gather(total, rest, axis, lay):
    sums, height = total.shape[0], rest.shape[1]
    size = lay.sizes[lay.axes.index(axis)]
    send = jnp.concatenate([total, rest.reshape(-1, 128)], axis=0)
    got = [exchange(send, axis, size, step) for step in range(1, size)]
    terms = [total.astype(F32)] + [other[:sums].astype(F32) for other in got]
    while len(terms) > 1:
        terms = [terms[k] + terms[k + 1] for k in range(0, len(terms), 2)]
    rest = jnp.concatenate(
        [rest] + [other[sums:].reshape(-1, height, 128) for other in got], axis=0
    )
    return terms[0].astype(BF), rest


def query_kernel(mine, rest_ref, out_ref, *, count):
    piece = out_ref.shape[0] // count
    for c in range(count):
        at = jnp.bitwise_xor(c, mine[0])
        for k in range(out_ref.shape[1] // 128):
            out_ref[c * piece : (c + 1) * piece, k * 128 : (k + 1) * 128] = rest_ref[
                at, k * piece : (k + 1) * piece, :
            ].astype(F32)


def place_query(mine, rest, shape, lay):
    vm = pl.BlockSpec(memory_space=pltpu.VMEM)
    return pl.pallas_call(
        functools.partial(query_kernel, count=lay.count),
        out_shape=jax.ShapeDtypeStruct(shape, F32),
        in_specs=[pl.BlockSpec(memory_space=pltpu.SMEM), vm],
        out_specs=vm,
        name="place_query",
    )(mine, rest)


def place_kernel(mine, near, near_x, near_y, far_a, far_b, *outs, count, across, sizes):
    cut = far_a.shape[1]
    looped = all(out.shape[0] // count % 8 == 0 for out in outs)

    def one(c, carry):
        s = jnp.bitwise_xor(c, mine[0])
        index = near_index(s // 4, sizes)

        def put(ref, low, high, base):
            first = 0
            for out in outs:
                piece = out.shape[0] // count
                for k in range(out.shape[1] // across):
                    if low <= first < high:
                        rows = pl.ds(pl.multiple_of(c * piece, piece) if looped else c * piece, piece)
                        out[rows, k * across : (k + 1) * across] = ref[
                            index, first - base : first - base + piece, :
                        ].astype(F32)
                    first += piece

        everything = near.shape[1]
        for side, ref in enumerate((near, near_x, near_y)):
            @pl.when(s % 4 == side)
            def _(ref=ref):
                put(ref, 0, everything, 0)

        @pl.when(s % 4 == 3)
        def _():
            put(far_a, 0, cut, 0)
            put(far_b, cut, everything, cut)

        return carry

    if looped:
        lax.fori_loop(0, count, one, 0)
    else:
        for c in range(count):
            one(c, 0)


def place_pieces(pieces, mine, shapes, across, sizes):
    vm = pl.BlockSpec(memory_space=pltpu.VMEM)
    count = 4 * pieces[0].shape[0]
    return pl.pallas_call(
        functools.partial(place_kernel, count=count, across=across, sizes=sizes),
        out_shape=tuple(jax.ShapeDtypeStruct(shape, F32) for shape in shapes),
        in_specs=[pl.BlockSpec(memory_space=pltpu.SMEM)] + [vm] * 5,
        out_specs=(vm,) * len(shapes),
        compiler_params=pltpu.CompilerParams(vmem_limit_bytes=40 << 20),
        cost_estimate=pl.CostEstimate(
            flops=0, bytes_accessed=24 * pieces[0].size, transcendentals=0
        ),
        name="place_pieces",
    )(mine, *pieces)


def layer_norm(values, gain_vec):
    mean_val = jnp.mean(values, axis=-1, keepdims=True)
    centered = values - mean_val
    variance = jnp.mean(centered * centered, axis=-1, keepdims=True)
    return centered * lax.rsqrt(variance + 1e-05) * gain_vec


def on_device(
    lay, inputs, cotangent, segments, routes, norm_first, w_query, w_keyval, w_router, w_out,
    norm_second, w_up, w_down
):
    def whole(shard):
        return lax.all_gather(shard, "w", axis=0, tiled=True)

    rows, width = inputs.shape[1:]
    head_count = w_router.shape[1]
    head_width = w_keyval.shape[1] // 2
    nb = rows // TB
    group_count = lay.count // INNER
    me = lax.axis_index(lay.inner_axes)
    group = lax.axis_index(lay.outer_axes) if lay.outer_axes else jnp.int32(0)
    place = jnp.stack([me, group]).astype(jnp.int32)
    mine = (group * INNER + me).astype(jnp.int32)[None]

    core = lax.axis_index("w")
    near_sizes = lay.sizes[:-2]

    def whole_by_exchange(shard):
        other = exchange(shard, "w", 2, 1)
        return jnp.where(
            core == 0,
            jnp.concatenate([shard, other], axis=0),
            jnp.concatenate([other, shard], axis=0),
        )

    narrow = whole(
        jnp.concatenate([w_keyval, w_router, norm_first[:, None], norm_second[:, None]], axis=1)
    )
    keyval_w = narrow[:, : 2 * head_width]
    narrow = narrow[:, 2 * head_width :]
    router_w = jnp.pad(narrow[:, :head_count], ((0, 0), (0, 128 - head_count)))
    norm_a, norm_b = narrow[:, head_count], narrow[:, head_count + 1]
    own_normed = layer_norm(inputs[0].astype(F32), norm_a.astype(F32)).astype(BF)
    spans = rows // (RUN * INNER)
    own_seg = segments[:, :: RUN * INNER].astype(BF)
    own_seg = jnp.pad(own_seg, ((0, 7), (0, 2 * head_width - spans)))
    near = gather_near(
        jnp.concatenate([dot(own_normed, keyval_w).astype(BF), own_seg], axis=0), lay
    )
    near_x, near_y = gather_sides(near, lay)
    rows_low = deal(inputs[0], lay).reshape(rows, width)
    near_x, near_y, rows_low = tie(near_x, near_y, rows_low)
    far = gather_far(near_x, near_y, lay, (nb // 2) * TB)
    query_w, out_w = whole(w_query), whole(w_out)
    up_w, down_w = whole_by_exchange(w_up), whole_by_exchange(w_down)

    quarter = lay.count // 4
    entry = [near_index(rest, near_sizes) for rest in range(quarter)]
    source = [entry.index(k) * 4 + side for side in range(4) for k in range(quarter)]
    source = jnp.bitwise_xor(jnp.array(source, jnp.int32), mine)
    far_rows = rows - (nb // 2) * TB
    all_seg = jnp.concatenate(
        [near[:, rows], near_x[:, rows], near_y[:, rows], far[1][:, far_rows]], axis=0
    ).astype(jnp.int32)
    at = source[:, None] * spans + jnp.arange(128, dtype=jnp.int32)[None]
    at = jnp.where(jnp.arange(128)[None] < spans, at, -1)
    first = jnp.arange(group_count * nb, dtype=jnp.int32) * (UNIT // (RUN * INNER))
    useg = jnp.sum(jnp.where(at[None] == first[:, None, None], all_seg[None], 0), axis=(1, 2))

    rows_in = rows_low.astype(F32)
    normed = layer_norm(rows_in, norm_a.astype(F32)).astype(BF)
    queries = dot(normed, query_w).astype(BF)
    logits = dot(normed, router_w)

    code = (routes[0, :, 0] * head_count + routes[0, :, 1]).astype(BF)
    slot_rows = rows // INNER
    code = code.reshape(rows // (RUN * INNER), INNER, RUN).transpose(1, 0, 2)
    code = jnp.pad(code.reshape(INNER, 1, slot_rows), ((0, 0), (0, RUN - 1), (0, width - slot_rows)))
    packed = cotangent[0].reshape(rows // (RUN * INNER), INNER, RUN, width).transpose(1, 0, 2, 3)
    packed = jnp.concatenate([packed.reshape(INNER, slot_rows, width), code], axis=1)
    packed, near_x, near_y = tie(packed, near_x, near_y)
    dealt = lax.all_to_all(packed, lay.inner_axes, 0, 0, tiled=True)
    if nb == 10:
        turns, one, two = (0, 1, 2, 5, 6, 7, 8, 9, 3, 4), 3, 8
    else:
        turns, one, two = tuple(range(group_count * nb)), nb // 3, nb - nb // 3
    attended, ot, low, qt, kaug, vt, order = attention_forward(
        useg, place, (near, near_x, near_y) + far, queries, head_count, head_width, near_sizes,
        turns,
    )
    attended, dealt = tie(attended, dealt)
    grad_top = dealt[:, :slot_rows].reshape(rows, width)
    code = dealt[:, slot_rows, :slot_rows].reshape(rows, 1).astype(jnp.int32)
    core_at = jnp.stack([core, me // 4]).astype(jnp.int32)
    result, middle_grad, logit_low, norm_b_part, grads, qa, doa, dot_t = middle_pass(
        core_at, rows_low, attended, logits, code, grad_top, norm_b[None], out_w, up_w, down_w,
        (qt, ot, low), head_count, lay.count,
    )
    grads = grads.reshape(lay.count, -1, width)
    grads, qa = tie(grads, qa)
    swapped = plane_swap(order_pieces(grads, mine, lay), lay)
    normed_t = normed.T

    def backward(first, stop, dq, more_in):
        return attention_backward(
            useg, place, order, kaug, vt, qa, doa, qt, dot_t, dq, more_in,
            tuple(range(first, stop)), two, head_count, head_width,
        )

    dq, dkv = backward(0, one, None, None)
    dq, dkv, swapped = tie(dq, dkv, swapped)
    halves = plane_sum(swapped)
    halves = halves.reshape(halves.shape[0], 2, -1, width)
    weights_own = lax.dynamic_index_in_dim(halves, core, 1, keepdims=False)
    weights_other = exchange(
        lax.dynamic_index_in_dim(halves, 1 - core, 1, keepdims=False), "w", 2, 1
    )
    weight_terms = rest_terms(
        (weights_own.astype(F32) + weights_other.astype(F32)).astype(BF), lay
    )
    back = move_back(result, lay)
    dq, dkv = backward(one, two, dq, dkv)
    dq, dkv, back, *weight_terms = tie(dq, dkv, back, *weight_terms)
    output = take_back(back)
    weights_near = gather_near(sum(term.astype(F32) for term in weight_terms).astype(BF), lay)
    swapped = plane_swap(order_pieces(dkv, mine, lay), lay)
    dq, late = backward(two, nb, dq, normed_t)
    dq, late, swapped, weights_near = tie(dq, late, swapped, weights_near)
    early = rest_terms(plane_sum(swapped), lay)
    if lay.count != INNER:
        query_w_grad = inner(normed, dq).astype(BF)
        piece = width // 2 // lay.count
        query_parts = query_w_grad.reshape(2, lay.count, piece, width // 128, 128)
        query_parts = query_parts.transpose(1, 0, 3, 2, 4).reshape(lay.count, -1, 128)
        late = order_pieces(jnp.concatenate([late, query_parts], axis=1), mine, lay)
    swapped = plane_swap(late, lay)
    base = outer(dq, query_w) + outer(logit_low, router_w)
    early = sum(term.astype(F32) for term in early).astype(BF)
    swapped, base, weights_near = tie(swapped, base, weights_near)
    weights_x, weights_y = gather_sides(weights_near, lay)
    late = plane_sum(swapped)
    late, early = tie(late, early)
    late = rest_terms(late, lay)
    grad_rows, small, sums = last_pass(
        core_at, order, lay.count == INNER, rows_low, base, middle_grad, logit_low, norm_b_part, norm_a[None], keyval_w,
        [early], late, head_count,
    )
    grad_rows, small, weights_x, weights_y = tie(grad_rows, small, weights_x, weights_y)
    weights_far = gather_far(weights_x, weights_y, lay, w_down.shape[0] // lay.count)
    back = move_back(grad_rows, lay)
    other = exchange(small[1], "w", 2, 1)
    both = (small[0].astype(F32) + other.astype(F32)).astype(BF)
    total, rest = both[:sums], both[sums:][None]
    for axis in lay.axes[::-1]:
        total, rest = sum_and_gather(total, rest, axis, lay)
        if axis == lay.axes[1]:
            total, rest, back = tie(total, rest, back)
    total, rest, *weights_far = tie(total, rest, *weights_far)
    input_grad = take_back(back).astype(F32)[None]
    query_sum = place_query(mine, rest, w_query.shape, lay)
    half = width // 2
    keyval_sum = total[:half].astype(F32)
    thin = total[half:].reshape(half // 128, -1, 128).transpose(1, 0, 2).reshape(-1, half)
    thin = thin.astype(F32)
    down_sum, up_sum, out_sum = place_pieces(
        (weights_near, weights_x, weights_y, *weights_far), mine,
        [w_down.shape, w_up.shape, w_out.shape], width, near_sizes,
    )
    return (
        output[None],
        input_grad,
        thin[head_count],
        query_sum,
        keyval_sum,
        thin[:head_count].T,
        out_sum,
        thin[head_count + 1],
        up_sum,
        down_sum,
    )


def solution(mesh):
    ctx_count, core_count = mesh.shape["ctx"], mesh.shape["wshard"]
    lay = Layout(ctx_count)
    grid = Mesh(mesh.devices.reshape(lay.sizes + (core_count,)), lay.axes + ("w",))
    ctx = lay.axes
    tokens = P("w", ctx, None)
    return jax.shard_map(
        functools.partial(on_device, lay),
        mesh=grid,
        in_specs=(
            tokens, tokens, P("w", ctx), tokens,
            P("w"), P("w", None), P("w", None), P("w", None), P("w", None),
            P("w"), P("w", None), P("w", None),
        ),
        out_specs=(
            tokens, tokens,
            P("w"), P("w", None), P("w", None), P("w", None), P("w", None),
            P("w"), P("w", None), P("w", None),
        ),
        check_vma=False,
    )
```

```python
import functools
import math

import jax
import jax.numpy as jnp
from jax import lax
from jax.experimental import pallas as pl
from jax.experimental.pallas import tpu as pltpu
from jax.sharding import Mesh, PartitionSpec as P

F32 = jnp.float32
BF = jnp.bfloat16
UNIT = 1024
TB = 64
INNER = UNIT // TB
RUN = 8
LOG2E = 1.4426950408889634
BIG = 2.0**100


def dot(lhs, rhs):
    return lax.dot_general(lhs, rhs, (((1,), (0,)), ((), ())), preferred_element_type=F32)


def inner(lhs, rhs):
    return lax.dot_general(lhs, rhs, (((0,), (0,)), ((), ())), preferred_element_type=F32)


def outer(lhs, rhs):
    return lax.dot_general(lhs, rhs, (((1,), (1,)), ((), ())), preferred_element_type=F32)


def split3(x):
    a = x.astype(BF)
    rest = x - a.astype(F32)
    b = rest.astype(BF)
    return a, b, (rest - b.astype(F32)).astype(BF)


def to_lanes(x, heads, hw):
    xt = x.T
    return jnp.concatenate([xt[h * hw : (h + 1) * hw] for h in range(heads)], axis=1)


def query_offsets(index, me):
    rest = index & (TB - 1)
    return (rest >> 3) * (RUN * INNER) + me * RUN + (rest & 7)


def near_index(rest, sizes):
    digits = []
    for size in sizes[::-1]:
        digits.append(rest % size)
        rest = rest // size
    index = 0
    for digit, size in zip(digits, sizes[::-1]):
        index = index * size + digit
    return index


def fetch_pieces(pieces, count, sizes, mine, total, put):
    near, near_x, near_y, far_a, far_b = pieces
    cut = far_a.shape[1]

    def one(c, carry):
        s = jnp.bitwise_xor(c, mine)
        index = near_index(s // 4, sizes)
        for side, ref in enumerate((near, near_x, near_y)):
            @pl.when(s % 4 == side)
            def _(ref=ref):
                put(c, 0, ref[index, :total, :])

        @pl.when(s % 4 == 3)
        def _():
            put(c, 0, far_a[index])
            put(c, cut, far_b[index, : total - cut, :])

        return carry

    lax.fori_loop(0, count, one, 0)


def fwd_kernel(
    useg, place, near, near_x, near_y, far_a, far_b, q_ref, o_ref, ot_ref, l_ref, qt_ref, kaug, vt, order,
    qa, acc, ref_row, plist, rank, ranked, bad, *, nb, slots, heads, hw, sizes, turns
):
    me, group = place[0], place[1]
    scale = LOG2E / math.sqrt(hw)
    lanes = heads * TB
    units = slots * nb

    def scan(u, n):
        rank[u] = n
        plist[n] = u
        return n + jnp.where(useg[u] == 0, 1, 0)

    prompt_units = lax.fori_loop(0, units, scan, jnp.int32(0))

    def settle(u, after):
        others = u - rank[u]
        ranked[jnp.where(useg[u] == 0, rank[u], prompt_units + others)] = u
        return after

    lax.fori_loop(0, units, settle, 0)
    for k in range(units):
        order[k] = ranked[turns[k]] if slots == 1 else k
    lane = lax.broadcasted_iota(jnp.int32, (UNIT, 2 * hw), 1)
    row = lax.broadcasted_iota(jnp.int32, (2 * hw, UNIT), 0)
    extra = jnp.where(lane < hw + 3, 1.0, 0.0).astype(BF)

    def put(c, first, rows):
        at = pl.multiple_of(c * nb * TB + first, TB)
        kaug[pl.ds(at, rows.shape[0]), :] = rows

    fetch_pieces(
        (near, near_x, near_y, far_a, far_b), slots * INNER, sizes, group * INNER + me, nb * TB, put
    )

    def split(u, carry):
        rows = pl.ds(pl.multiple_of(u * UNIT, UNIT), UNIT)
        tile = kaug[rows, :]
        kaug[rows, :] = jnp.where(lane < hw, tile, extra)
        flip = tile.T
        vt[u] = jnp.where(row < hw, jnp.ones_like(flip), flip)
        return carry

    lax.fori_loop(0, units, split, 0)

    def keys_of(u):
        return kaug[pl.ds(pl.multiple_of(u * UNIT, UNIT), UNIT), :]

    def block(i, carry):
        own = group * nb + i
        full_units = jnp.where(useg[own] != 0, prompt_units, rank[own])
        rows = pl.ds(pl.multiple_of(i * TB, TB), TB)
        qt = to_lanes(q_ref[rows, :], heads, hw)
        qt_ref[i] = qt
        qa[0:hw, :] = qt
        qa[hw:, :] = jnp.zeros((hw, lanes), BF)
        mask = lax.broadcasted_iota(jnp.int32, (UNIT, lanes), 0) <= query_offsets(
            lax.broadcasted_iota(jnp.int32, (UNIT, lanes), 1), me
        )
        few = UNIT // 4
        keys = kaug[pl.ds(pl.multiple_of(own * UNIT, UNIT), few), :]
        ref_row[...] = jnp.max(
            jnp.where(mask[:few], dot(keys, qa[...]), -1e30), axis=0, keepdims=True
        )
        bad[0] = 1

        def attempt(turn, carry):
            @pl.when(bad[0] != 0)
            def _():
                @pl.when(turn == 1)
                def _():
                    qa[hw:, :] = jnp.zeros((hw, lanes), BF)

                    def highest(k, carry):
                        u = jnp.where(k // 4 < full_units, plist[k // 4], own)
                        first = k % 4 * few
                        keys = kaug[pl.ds(pl.multiple_of(u * UNIT + first, few), few), :]
                        usable = first + lax.broadcasted_iota(
                            jnp.int32, (few, lanes), 0
                        ) <= query_offsets(lax.broadcasted_iota(jnp.int32, (few, lanes), 1), me)
                        ref_row[...] = jnp.maximum(
                            ref_row[...],
                            jnp.max(
                                jnp.where(usable | (u != own), dot(keys, qa[...]), -1e30),
                                axis=0, keepdims=True,
                            ),
                        )
                        return carry

                    lax.fori_loop(0, 4 * full_units + 4, highest, 0)

                a, b, c = split3(-ref_row[...])
                qa[hw:, :] = jnp.concatenate([a, b, c, jnp.zeros((hw - 3, lanes), BF)], axis=0)
                s = jnp.where(mask, dot(keys_of(own), qa[...]) * scale, -1e30)
                acc[...] = dot(vt[own], jnp.exp2(s).astype(BF))

                def full(k, carry):
                    u = plist[k]
                    p = jnp.exp2(dot(keys_of(u), qa[...]) * scale).astype(BF)
                    acc[...] += dot(vt[u], p)
                    return carry

                lax.fori_loop(0, full_units, full, 0)
                bad[0] = jnp.where(jnp.max(acc[0:1, :]) < BIG, 0, 1)

            return carry

        lax.fori_loop(0, 2, attempt, 0)
        ot = acc[hw:, :] / acc[0:hw, :]
        ot_ref[i] = ot
        l_ref[i] = ref_row[...] + jnp.log2(acc[0:1, :]) / scale
        on = jnp.concatenate([ot[:, h * TB : (h + 1) * TB] for h in range(heads)], axis=0)
        o_ref[rows, :] = on.T
        return carry

    lax.fori_loop(0, nb, block, 0)


def attention_forward(useg, place, pieces, q, heads, hw, sizes, turns):
    rows = q.shape[0]
    nb = rows // TB
    slots = 4 * pieces[0].shape[0] // INNER
    lanes = heads * TB
    units = slots * nb
    vm = pl.BlockSpec(memory_space=pltpu.VMEM)
    sm = pl.BlockSpec(memory_space=pltpu.SMEM)
    return pl.pallas_call(
        functools.partial(fwd_kernel, nb=nb, slots=slots, heads=heads, hw=hw, sizes=sizes, turns=turns),
        out_shape=(
            jax.ShapeDtypeStruct((rows, heads * hw), F32),
            jax.ShapeDtypeStruct((nb, hw, lanes), F32),
            jax.ShapeDtypeStruct((nb, 1, lanes), F32),
            jax.ShapeDtypeStruct((nb, hw, lanes), BF),
            jax.ShapeDtypeStruct((units * UNIT, 2 * hw), BF),
            jax.ShapeDtypeStruct((units, 2 * hw, UNIT), BF),
            jax.ShapeDtypeStruct((units,), jnp.int32),
        ),
        in_specs=[sm, sm] + [vm] * 6,
        out_specs=(vm,) * 6 + (sm,),
        scratch_shapes=[
            pltpu.VMEM((2 * hw, lanes), BF),
            pltpu.VMEM((2 * hw, lanes), F32),
            pltpu.VMEM((1, lanes), F32),
            pltpu.SMEM((units + 1,), jnp.int32),
            pltpu.SMEM((units + 1,), jnp.int32),
            pltpu.SMEM((units + 1,), jnp.int32),
            pltpu.SMEM((1,), jnp.int32),
        ],
        compiler_params=pltpu.CompilerParams(vmem_limit_bytes=60 << 20),
        cost_estimate=pl.CostEstimate(
            flops=40 * 10**9, bytes_accessed=8 << 20, transcendentals=26 * 10**6
        ),
        name="attention_forward",
    )(useg, place, *pieces, q)


def prepare_kernel(qt_ref, ot_ref, l_ref, do_ref, qa_ref, doa_ref, dot_ref, *, nb, heads, hw):
    pad = jnp.zeros((hw - 3, heads * TB), BF)

    def prepare(i, carry):
        rows = pl.ds(pl.multiple_of(i * TB, TB), TB)
        a, b, c = split3(-l_ref[i])
        qa_ref[i] = jnp.concatenate([qt_ref[i], a, b, c, pad], axis=0).T
        dt = to_lanes(do_ref[rows, :], heads, hw)
        dot_ref[i] = dt
        total = jnp.sum(dt.astype(F32) * ot_ref[i], axis=0, keepdims=True)
        a, b, c = split3(-total)
        doa_ref[i] = jnp.concatenate([a, b, c, pad, dt], axis=0).T
        return carry

    lax.fori_loop(0, nb, prepare, 0)


def bwd_kernel(
    useg, place, order, kaug_ref, vt_ref, qa, doa, qt, dot_t, *rest,
    nb, parts, first, last, dealt, heads, hw
):
    if first:
        dqacc, dkv_ref, kt, dkvt = rest
    elif last:
        dqold, normed, dq_ref, dkv_ref, dqacc, kt, dkvt = rest
    else:
        dqold, _, dqacc, dkv_ref, kt, dkvt = rest
    grid_at = pl.program_id(0)
    steps = pl.num_programs(0) - (2 if last and dealt else 0)
    step_at = jnp.minimum(grid_at, steps - 1)
    me, group = place[0], place[1]
    unit = order[step_at // len(parts) * nb + step_at % len(parts) + parts[0]]
    scale = LOG2E / math.sqrt(hw)
    lanes = heads * TB

    @pl.when(grid_at == 0)
    def _():
        dqacc[...] = jnp.zeros_like(dqacc) if first else dqold[...]

    unit_seg = useg[unit]

    def block(i, carry):
        own = group * nb + i

        def step(first, size, masked):
            keys = pl.ds(first, size)
            s = dot(qa[i], kt[:, keys]) * scale
            if masked:
                mask = first + lax.broadcasted_iota(
                    jnp.int32, (lanes, size), 1
                ) <= query_offsets(lax.broadcasted_iota(jnp.int32, (lanes, size), 0), me)
                s = jnp.where(mask, s, -1e30)
            p = jnp.exp2(s)
            ds = (p * dot(doa[i], vt_ref[0, :, keys])).astype(BF)
            dkvt[hw:, keys] += dot(dot_t[i], p.astype(BF))
            dkvt[:hw, keys] += dot(qt[i], ds)
            dqacc[i] += dot(ds, kaug_ref[keys, :])

        @pl.when((unit_seg == 0) & (own != unit) & ((useg[own] != 0) | (own > unit)))
        def _():
            step(0, UNIT, False)

        @pl.when(own == unit)
        def _():
            def part_of_own(k, carry):
                step(pl.multiple_of(k * (UNIT // 2), UNIT // 2), UNIT // 2, True)
                return carry

            lax.fori_loop(0, 2, part_of_own, 0)

        return carry

    def keys():
        kt[...] = kaug_ref[...].T
        dkvt[...] = jnp.zeros_like(dkvt)
        lax.fori_loop(0, nb, block, 0)
        factor = jnp.where(
            lax.broadcasted_iota(jnp.int32, (2 * hw, 1), 0) < hw, 1 / math.sqrt(hw), 1.0
        )
        dkv = (dkvt[...] * factor).T.reshape(TB // RUN, INNER, RUN, 2 * hw)
        for d in range(INNER):
            to = piece_at(d, me // 4, dealt)
            dkv_ref[to] = dkv[:, d].reshape(TB, 2 * hw).astype(BF)

    if last and dealt:
        pl.when(grid_at < steps)(keys)
    else:
        keys()

    if last:
        @pl.when(grid_at == steps - 1)
        def _():
            def finish(i, carry):
                rows = pl.ds(pl.multiple_of(i * TB, TB), TB)
                a = dqacc[i]
                dq_ref[rows, :] = (
                    jnp.concatenate([a[h * TB : (h + 1) * TB, :hw] for h in range(heads)], axis=1)
                    * (1 / math.sqrt(hw))
                ).astype(BF)
                return carry

            lax.fori_loop(0, nb, finish, 0)

    if last and dealt:
        @pl.when(grid_at >= steps)
        def _():
            width = dq_ref.shape[1]
            half = width // 2
            rows = pl.ds(pl.multiple_of((grid_at - steps) * half, half), half)
            grad = dot(normed[rows, :], dq_ref[...]).astype(BF)
            piece = half // INNER
            for c in range(INNER):
                to = piece_at(c, me // 4, dealt)
                for k in range(width // 128):
                    dkv_ref[to, k * piece : (k + 1) * piece, :] = grad[
                        c * piece : (c + 1) * piece, k * 128 : (k + 1) * 128
                    ]


def attention_backward(
    useg, place, order, kaug, vt, qa, doa, qt, dot_t, dqold, more_in, parts, joint, heads, hw
):
    nb, lanes, _ = qa.shape
    slots = vt.shape[0] // nb
    first, last = dqold is None, parts[-1] == nb - 1
    dealt = slots == 1
    more = 2 if last and dealt else 0
    turns_out = len(parts) + more if last else joint
    base = 0 if last else parts[0]
    vm = pl.BlockSpec(memory_space=pltpu.VMEM)
    acc_shape = jax.ShapeDtypeStruct((nb, lanes, 2 * hw), F32)
    count = len(parts)

    def at(u, seg, place, order):
        u = jnp.minimum(u, slots * count - 1)
        return order[u // count * nb + u % count + parts[0]]

    def to(u, seg, place, order):
        if dealt:
            return (0, u + base, 0)
        return (u // count, u % count + base, 0)

    return pl.pallas_call(
        functools.partial(
            bwd_kernel, nb=nb, parts=parts, first=first, last=last, dealt=dealt, heads=heads, hw=hw
        ),
        out_shape=(
            jax.ShapeDtypeStruct((nb * TB, heads * hw), BF) if last else acc_shape,
            jax.ShapeDtypeStruct((slots * INNER, turns_out * TB, 2 * hw), BF),
        ),
        grid_spec=pltpu.PrefetchScalarGridSpec(
            num_scalar_prefetch=3,
            grid=(slots * count + more,),
            in_specs=[
                pl.BlockSpec((UNIT, 2 * hw), lambda *a: (at(*a), 0)),
                pl.BlockSpec((1, 2 * hw, UNIT), lambda *a: (at(*a), 0, 0)),
            ]
            + [vm] * (4 if first else 6 if last else 5)
            + ([] if first or last else [pl.BlockSpec(memory_space=pl.ANY)]),
            out_specs=(
                vm,
                pl.BlockSpec((INNER, TB, 2 * hw), to),
            ),
            scratch_shapes=([pltpu.VMEM(acc_shape.shape, F32)] if last and not first else [])
            + [
                pltpu.VMEM((2 * hw, UNIT), BF),
                pltpu.VMEM((2 * hw, UNIT), F32),
            ],
        ),
        compiler_params=pltpu.CompilerParams(vmem_limit_bytes=60 << 20),
        cost_estimate=pl.CostEstimate(
            flops=8 * 10**9 * count, bytes_accessed=12 << 20, transcendentals=2 * 10**6 * count
        ),
        input_output_aliases={} if first or last else {10: 1},
        name="attention_backward",
    )(useg, place, order, kaug, vt, qa, doa, qt, dot_t, *([] if first else [dqold, more_in]))


def exact_dot(x, ones):
    a, b, c = split3(x)
    return dot(a, ones) + dot(b, ones) + dot(c, ones)


def norm_parts(values):
    mean_val = jnp.mean(values, axis=-1, keepdims=True)
    centered = values - mean_val
    variance = jnp.mean(centered * centered, axis=-1, keepdims=True)
    inverse = lax.rsqrt(variance + 1e-05)
    return centered * inverse, inverse


def norm_back(grad, unit, inverse, gain):
    scaled = grad * gain
    shift = jnp.mean(scaled, axis=-1, keepdims=True)
    along = jnp.mean(scaled * unit, axis=-1, keepdims=True)
    return inverse * (scaled - shift - unit * along)


def piece_at(c, my_rest, dealt):
    return c % 4 * (INNER // 4) + jnp.bitwise_xor(c // 4, my_rest) if dealt else c


def put_pieces(grads_ref, where, value, first, rows, at, count, step):
    piece = rows // 2 // count
    value = value.astype(BF)
    half = first // (rows // 2)
    device = (first - half * (rows // 2)) // piece
    for k in range(step // piece):
        to = piece_at(device + k, where[1], count == INNER)
        grads_ref[to, half, at : at + piece, :] = value[k * piece : (k + 1) * piece]


def middle_kernel(
    where, x_ref, att_ref, logit_ref, code_ref, cot_ref, norm_ref, out_w, up_w, down_w,
    qt_ref, ot_ref, low_ref,
    result_ref, middle_grad_ref, logit_grad_ref, norm_grad_ref, grads_ref, qa_ref, doa_ref, dot_ref,
    att_grad_s, mixed_s, normed_s, hidden_s, pre_s, branch_s, *, count, heads
):
    rows, width = x_ref.shape
    chunk = rows
    hw = width // heads
    gain = norm_ref[...].astype(F32)
    lane = lax.broadcasted_iota(jnp.int32, (chunk, 128), 1)
    head = lax.broadcasted_iota(jnp.int32, (128, width), 0)
    column = lax.broadcasted_iota(jnp.int32, (128, width), 1)
    widen = jnp.where(column // hw == head, 1.0, 0.0).astype(BF)
    narrow = jnp.where(
        lax.broadcasted_iota(jnp.int32, (width, 128), 0) // hw
        == lax.broadcasted_iota(jnp.int32, (width, 128), 1),
        1.0, 0.0,
    ).astype(BF)
    if True:
        at = slice(None)
        code = code_ref[at, :]
        chosen = ((code // heads == lane) | (code % heads == lane)) & (lane < heads)
        lifted = jnp.where(chosen, logit_ref[at, :], -1e30)
        raised = jnp.where(
            chosen, jnp.exp(lifted - jnp.max(lifted, axis=-1, keepdims=True)), 0.0
        )
        gate = raised / jnp.sum(raised, axis=-1, keepdims=True)
        gates = exact_dot(gate, widen)
        attended = att_ref[at, :]
        mixed = (gates * attended).astype(BF)
        mixed_s[at, :] = mixed
        middle = x_ref[at, :].astype(F32) + dot(mixed, out_w[...])
        unit, inverse = norm_parts(middle)
        normed = (unit * gain).astype(BF)
        normed_s[at, :] = normed
        cot = cot_ref[at, :]
        back = jnp.zeros((chunk, width), F32)
        step = 512

        def hidden_block(k, sums):
            total, back = sums
            to = pl.ds(pl.multiple_of(k * step, step), step)
            pre = dot(normed, up_w[:, to])
            inside = 0.7978845608028654 * (pre + 0.044715 * pre * pre * pre)
            t = jnp.tanh(inside)
            half = 0.5 * (1.0 + t)
            hidden = (pre * half).astype(BF)
            slope = half + 0.5 * pre * (1.0 - t * t) * (
                0.7978845608028654 * (1.0 + 3 * 0.044715 * pre * pre)
            )
            hidden_s[:, to] = hidden
            pre_grad = (outer(cot, down_w[to, :]) * slope).astype(BF)
            pre_s[:, to] = pre_grad
            return total + dot(hidden, down_w[to, :]), back + outer(pre_grad, up_w[:, to])

        total, back = lax.fori_loop(0, up_w.shape[1] // step, hidden_block, (middle, back))
        result_ref[at, :] = total.astype(BF)
        norm_grad_ref[...] = jnp.sum(
            (back * unit).reshape(chunk // 8, 8, width), axis=0
        )
        middle_grad = cot.astype(F32) + norm_back(back, unit, inverse, gain)
        middle_grad_ref[at, :] = middle_grad
        branch = middle_grad.astype(BF)
        branch_s[at, :] = branch
        mixed_grad = outer(branch, out_w[...])
        gate_grad = exact_dot(mixed_grad * attended, narrow)
        logit_grad_ref[at, :] = (
            gate * (gate_grad - jnp.sum(gate * gate_grad, axis=-1, keepdims=True))
        ).astype(BF)
        att_grad_s[at, :] = (gates * mixed_grad).astype(BF)
    prepare_kernel(
        qt_ref, ot_ref, low_ref, att_grad_s, qa_ref, doa_ref, dot_ref,
        nb=qt_ref.shape[0], heads=heads, hw=hw,
    )
    ff = hidden_s.shape[1]
    across = width
    half, down_rows = width // 2, ff // 2 // count

    def down_block(k, carry):
        at = pl.ds(pl.multiple_of(k * width, width), width)
        put_pieces(grads_ref, where, inner(hidden_s[:, at], cot), k * width, ff, 0, count, width)
        return carry

    lax.fori_loop(0, ff // width, down_block, 0)

    def up_block(k, carry):
        at = pl.ds(pl.multiple_of(k * half, half), half)
        up = inner(normed_s[:, at], pre_s[...])
        piece = half // count
        for c in range(ff // width):
            put_pieces(
                grads_ref, where, up[:, c * width : (c + 1) * width], k * half, width,
                down_rows + c * piece, count, half,
            )
        put_pieces(
            grads_ref, where, inner(mixed_s[:, at], branch_s[...]), k * half, width,
            down_rows + ff // width * piece, count, half,
        )
        return carry

    lax.fori_loop(0, 2, up_block, 0)


def middle_pass(core, x, attended, logits, code, cot, norm_b, out_w, up_w, down_w, kept, heads, count):
    rows, width = x.shape
    nb, hw, lanes = kept[0].shape
    ff = up_w.shape[1]
    piece_rows = (ff * 2 + width) // (2 * count)
    vm = pl.BlockSpec(memory_space=pltpu.VMEM)
    shape = jax.ShapeDtypeStruct
    return pl.pallas_call(
        functools.partial(middle_kernel, count=count, heads=heads),
        out_shape=(
            shape((rows, width), BF),
            shape((rows, width), F32),
            shape((rows, 128), BF),
            shape((8, width), F32),
            shape((count, 2, piece_rows, width), BF),
            shape((nb, lanes, 2 * hw), BF),
            shape((nb, lanes, 2 * hw), BF),
            shape((nb, hw, lanes), BF),
        ),
        in_specs=[pl.BlockSpec(memory_space=pltpu.SMEM)] + [vm] * 12,
        out_specs=(vm,) * 8,
        scratch_shapes=[
            pltpu.VMEM((rows, width), BF),
            pltpu.VMEM((rows, width), BF),
            pltpu.VMEM((rows, width), BF),
            pltpu.VMEM((rows, ff), BF),
            pltpu.VMEM((rows, ff), BF),
            pltpu.VMEM((rows, width), BF),
        ],
        compiler_params=pltpu.CompilerParams(vmem_limit_bytes=60 << 20),
        cost_estimate=pl.CostEstimate(
            flops=9 * 10**9, bytes_accessed=24 << 20, transcendentals=2 * 10**6
        ),
        name="middle_pass",
    )(core, x, attended, logits, code, cot, norm_b, out_w, up_w, down_w, *kept)


class Layout:
    def __init__(self, ctx_count):
        sizes = [4]
        while math.prod(sizes) < ctx_count:
            sizes.append(2)
        assert math.prod(sizes) == ctx_count
        self.sizes = tuple(sizes)
        self.axes = tuple(f"c{k}" for k in range(len(sizes)))
        cut = len(sizes)
        while math.prod(sizes[cut:]) < INNER:
            cut -= 1
        assert math.prod(sizes[cut:]) == INNER
        self.outer_axes, self.inner_axes = self.axes[:cut], self.axes[cut:]
        self.count = ctx_count


def exchange(x, axis, size, step):
    return lax.ppermute(x, axis, [(i, i ^ step) for i in range(size)])


def spread(x, order, lay, start=0, stop=None):
    for axis in order[start:stop]:
        size = lay.sizes[lay.axes.index(axis)]
        x = jnp.concatenate([x] + [exchange(x, axis, size, step) for step in range(1, size)])
    return x


def gather_near(x, lay):
    return spread(x[None], lay.axes[:-2], lay)


def gather_sides(near, lay):
    y_axis, x_axis = lay.axes[-2:]
    return exchange(near, x_axis, 2, 1), exchange(near, y_axis, 2, 1)


def gather_far(near_x, near_y, lay, cut):
    y_axis, x_axis = lay.axes[-2:]
    return exchange(near_x[:, :cut], y_axis, 2, 1), exchange(near_y[:, cut:], x_axis, 2, 1)


def deal(x, lay):
    rows, width = x.shape
    packed = x.reshape(rows // (RUN * INNER), INNER, RUN, width).transpose(1, 0, 2, 3)
    packed = packed.reshape(INNER, rows // INNER, width)
    return lax.all_to_all(packed, lay.inner_axes, 0, 0, tiled=True)


def move_back(x, lay):
    rows, width = x.shape
    return lax.all_to_all(x.reshape(INNER, rows // INNER, width), lay.inner_axes, 0, 0, tiled=True)


def take_back(back):
    rows, width = back.shape[0] * back.shape[1], back.shape[2]
    back = back.reshape(INNER, rows // (RUN * INNER), RUN, width).transpose(1, 0, 2, 3)
    return back.reshape(rows, width)


def tie(*values):
    return lax.optimization_barrier(values)


def order_pieces(pieces, mine, lay):
    if lay.count == INNER:
        return pieces
    index = jnp.arange(lay.count, dtype=jnp.int32)
    quarter = lay.count // 4
    rest = jnp.bitwise_xor(index % quarter, mine // 4)
    return jnp.take(pieces, rest * 4 + index // quarter, axis=0)


def plane_swap(pieces, lay):
    return lax.all_to_all(pieces, lay.axes[-2:], 0, 0, tiled=True)


def plane_sum(pieces):
    return add_pieces(pieces.reshape((4, -1) + pieces.shape[1:]))


def rest_terms(pieces, lay):
    axes = list(zip(lay.axes, lay.sizes))[:-2]
    for k, (axis, size) in enumerate(axes):
        pieces = pieces.reshape((size, -1) + pieces.shape[1:])
        terms = [pieces[0]] + [exchange(pieces[step], axis, size, step) for step in range(1, size)]
        if k < len(axes) - 1:
            pieces = sum(term.astype(F32) for term in terms).astype(BF)
    return [term[0] for term in terms]


def add_pieces(pieces):
    return jnp.sum(pieces.astype(F32), axis=0).astype(BF)


def add_terms(refs):
    total = refs[0][...].astype(F32)
    for ref in refs[1:]:
        total = total + ref[...].astype(F32)
    return total.astype(BF)


def last_kernel(
    core, order, x_ref, base_ref, middle_grad_ref, logit_ref, norm_b_ref, gain_ref, keyval_w, *rest,
    heads, dealt
):
    first, *terms, grad_ref, small_ref, keyval_s = rest
    rows, width = x_ref.shape
    gain = gain_ref[...].astype(F32)
    unit, inverse = norm_parts(x_ref[...].astype(F32))
    normed = (unit * gain).astype(BF)
    early, late = first[...], add_terms(terms)
    late_rows = rows - early.shape[0]
    turned = jnp.concatenate([early, late[:late_rows]], axis=0)
    for k in range(rows // TB):
        to = pl.multiple_of((order[k] if dealt else k) * TB, TB)
        keyval_s[pl.ds(to, TB), :] = turned[k * TB : (k + 1) * TB]
    keyval_grad = keyval_s[...]
    grad = base_ref[...] + outer(keyval_grad, keyval_w[...])
    grad_ref[...] = (middle_grad_ref[...] + norm_back(grad, unit, inverse, gain)).astype(BF)
    keyval_sum = inner(normed, keyval_grad).astype(BF)
    thin = jnp.concatenate(
        [
            inner(logit_ref[...], normed)[:heads],
            jnp.sum(grad * unit, axis=0, keepdims=True),
            jnp.sum(norm_b_ref[...], axis=0, keepdims=True),
            jnp.zeros((-(heads + 2) % 16, width), F32),
        ],
        axis=0,
    ).astype(BF)
    half, query_half = width // 2, (late.shape[0] - late_rows) // 2
    for side in range(2):
        to = jnp.bitwise_xor(core[0], side)
        small_ref[to, :half, :] = keyval_sum[side * half : (side + 1) * half]
        first = half
        for c in range(side * half, (side + 1) * half, 128):
            small_ref[to, first : first + thin.shape[0], :] = thin[:, c : c + 128]
            first += thin.shape[0]
        small_ref[to, first:, :] = late[late_rows + side * query_half :][:query_half]


def last_pass(core, order, dealt, x, base, middle_grad, logit_low, norm_b_part, gain, keyval_w, early, late, heads):
    rows, width = x.shape
    query_half = (late[0].shape[0] + early[0].shape[0] - rows) // 2
    thin_rows = (heads + 2 + -(heads + 2) % 16) * (width // 2) // 128
    sums = width // 2 + thin_rows
    arrays = (x, base, middle_grad, logit_low, norm_b_part, gain, keyval_w, *early, *late)
    vm = pl.BlockSpec(memory_space=pltpu.VMEM)
    grad, small = pl.pallas_call(
        functools.partial(last_kernel, heads=heads, dealt=dealt),
        out_shape=(
            jax.ShapeDtypeStruct((rows, width), BF),
            jax.ShapeDtypeStruct((2, sums + query_half, 128), BF),
        ),
        grid=(1,),
        in_specs=[pl.BlockSpec(memory_space=pltpu.SMEM)] * 2
        + [pl.BlockSpec(a.shape, lambda g: (0, 0)) for a in arrays],
        out_specs=(vm,) * 2,
        scratch_shapes=[pltpu.VMEM((rows, keyval_w.shape[1]), BF)],
        compiler_params=pltpu.CompilerParams(vmem_limit_bytes=40 << 20),
        cost_estimate=pl.CostEstimate(flops=10**9, bytes_accessed=6 << 20, transcendentals=0),
        name="last_pass",
    )(core, order, *arrays)
    return grad, small, sums


def sum_and_gather(total, rest, axis, lay):
    sums, height = total.shape[0], rest.shape[1]
    size = lay.sizes[lay.axes.index(axis)]
    send = jnp.concatenate([total, rest.reshape(-1, 128)], axis=0)
    got = [exchange(send, axis, size, step) for step in range(1, size)]
    terms = [total.astype(F32)] + [other[:sums].astype(F32) for other in got]
    while len(terms) > 1:
        terms = [terms[k] + terms[k + 1] for k in range(0, len(terms), 2)]
    rest = jnp.concatenate(
        [rest] + [other[sums:].reshape(-1, height, 128) for other in got], axis=0
    )
    return terms[0].astype(BF), rest


def query_kernel(mine, rest_ref, out_ref, *, count):
    piece = out_ref.shape[0] // count
    for c in range(count):
        at = jnp.bitwise_xor(c, mine[0])
        for k in range(out_ref.shape[1] // 128):
            out_ref[c * piece : (c + 1) * piece, k * 128 : (k + 1) * 128] = rest_ref[
                at, k * piece : (k + 1) * piece, :
            ].astype(F32)


def place_query(mine, rest, shape, lay):
    vm = pl.BlockSpec(memory_space=pltpu.VMEM)
    return pl.pallas_call(
        functools.partial(query_kernel, count=lay.count),
        out_shape=jax.ShapeDtypeStruct(shape, F32),
        in_specs=[pl.BlockSpec(memory_space=pltpu.SMEM), vm],
        out_specs=vm,
        name="place_query",
    )(mine, rest)


def place_kernel(mine, near, near_x, near_y, far_a, far_b, *outs, count, across, sizes):
    cut = far_a.shape[1]
    looped = all(out.shape[0] // count % 8 == 0 for out in outs)

    def one(c, carry):
        s = jnp.bitwise_xor(c, mine[0])
        index = near_index(s // 4, sizes)

        def put(ref, low, high, base):
            first = 0
            for out in outs:
                piece = out.shape[0] // count
                for k in range(out.shape[1] // across):
                    if low <= first < high:
                        rows = pl.ds(pl.multiple_of(c * piece, piece) if looped else c * piece, piece)
                        out[rows, k * across : (k + 1) * across] = ref[
                            index, first - base : first - base + piece, :
                        ].astype(F32)
                    first += piece

        everything = near.shape[1]
        for side, ref in enumerate((near, near_x, near_y)):
            @pl.when(s % 4 == side)
            def _(ref=ref):
                put(ref, 0, everything, 0)

        @pl.when(s % 4 == 3)
        def _():
            put(far_a, 0, cut, 0)
            put(far_b, cut, everything, cut)

        return carry

    if looped:
        lax.fori_loop(0, count, one, 0)
    else:
        for c in range(count):
            one(c, 0)


def place_pieces(pieces, mine, shapes, across, sizes):
    vm = pl.BlockSpec(memory_space=pltpu.VMEM)
    count = 4 * pieces[0].shape[0]
    return pl.pallas_call(
        functools.partial(place_kernel, count=count, across=across, sizes=sizes),
        out_shape=tuple(jax.ShapeDtypeStruct(shape, F32) for shape in shapes),
        in_specs=[pl.BlockSpec(memory_space=pltpu.SMEM)] + [vm] * 5,
        out_specs=(vm,) * len(shapes),
        compiler_params=pltpu.CompilerParams(vmem_limit_bytes=40 << 20),
        cost_estimate=pl.CostEstimate(
            flops=0, bytes_accessed=24 * pieces[0].size, transcendentals=0
        ),
        name="place_pieces",
    )(mine, *pieces)


def layer_norm(values, gain_vec):
    mean_val = jnp.mean(values, axis=-1, keepdims=True)
    centered = values - mean_val
    variance = jnp.mean(centered * centered, axis=-1, keepdims=True)
    return centered * lax.rsqrt(variance + 1e-05) * gain_vec


def on_device(
    lay, inputs, cotangent, segments, routes, norm_first, w_query, w_keyval, w_router, w_out,
    norm_second, w_up, w_down
):
    def whole(shard):
        return lax.all_gather(shard, "w", axis=0, tiled=True)

    rows, width = inputs.shape[1:]
    head_count = w_router.shape[1]
    head_width = w_keyval.shape[1] // 2
    nb = rows // TB
    group_count = lay.count // INNER
    me = lax.axis_index(lay.inner_axes)
    group = lax.axis_index(lay.outer_axes) if lay.outer_axes else jnp.int32(0)
    place = jnp.stack([me, group]).astype(jnp.int32)
    mine = (group * INNER + me).astype(jnp.int32)[None]

    core = lax.axis_index("w")
    near_sizes = lay.sizes[:-2]

    def whole_by_exchange(shard):
        other = exchange(shard, "w", 2, 1)
        return jnp.where(
            core == 0,
            jnp.concatenate([shard, other], axis=0),
            jnp.concatenate([other, shard], axis=0),
        )

    narrow = whole(
        jnp.concatenate([w_keyval, w_router, norm_first[:, None], norm_second[:, None]], axis=1)
    )
    keyval_w = narrow[:, : 2 * head_width]
    narrow = narrow[:, 2 * head_width :]
    router_w = jnp.pad(narrow[:, :head_count], ((0, 0), (0, 128 - head_count)))
    norm_a, norm_b = narrow[:, head_count], narrow[:, head_count + 1]
    own_normed = layer_norm(inputs[0].astype(F32), norm_a.astype(F32)).astype(BF)
    spans = rows // (RUN * INNER)
    own_seg = segments[:, :: RUN * INNER].astype(BF)
    own_seg = jnp.pad(own_seg, ((0, 7), (0, 2 * head_width - spans)))
    near = gather_near(
        jnp.concatenate([dot(own_normed, keyval_w).astype(BF), own_seg], axis=0), lay
    )
    near_x, near_y = gather_sides(near, lay)
    rows_low = deal(inputs[0], lay).reshape(rows, width)
    near_x, near_y, rows_low = tie(near_x, near_y, rows_low)
    far = gather_far(near_x, near_y, lay, (nb // 2) * TB)
    query_w, out_w = whole(w_query), whole(w_out)
    up_w, down_w = whole_by_exchange(w_up), whole_by_exchange(w_down)

    quarter = lay.count // 4
    entry = [near_index(rest, near_sizes) for rest in range(quarter)]
    source = [entry.index(k) * 4 + side for side in range(4) for k in range(quarter)]
    source = jnp.bitwise_xor(jnp.array(source, jnp.int32), mine)
    far_rows = rows - (nb // 2) * TB
    all_seg = jnp.concatenate(
        [near[:, rows], near_x[:, rows], near_y[:, rows], far[1][:, far_rows]], axis=0
    ).astype(jnp.int32)
    at = source[:, None] * spans + jnp.arange(128, dtype=jnp.int32)[None]
    at = jnp.where(jnp.arange(128)[None] < spans, at, -1)
    first = jnp.arange(group_count * nb, dtype=jnp.int32) * (UNIT // (RUN * INNER))
    useg = jnp.sum(jnp.where(at[None] == first[:, None, None], all_seg[None], 0), axis=(1, 2))

    rows_in = rows_low.astype(F32)
    normed = layer_norm(rows_in, norm_a.astype(F32)).astype(BF)
    queries = dot(normed, query_w).astype(BF)
    logits = dot(normed, router_w)

    code = (routes[0, :, 0] * head_count + routes[0, :, 1]).astype(BF)
    slot_rows = rows // INNER
    code = code.reshape(rows // (RUN * INNER), INNER, RUN).transpose(1, 0, 2)
    code = jnp.pad(code.reshape(INNER, 1, slot_rows), ((0, 0), (0, RUN - 1), (0, width - slot_rows)))
    packed = cotangent[0].reshape(rows // (RUN * INNER), INNER, RUN, width).transpose(1, 0, 2, 3)
    packed = jnp.concatenate([packed.reshape(INNER, slot_rows, width), code], axis=1)
    packed, near_x, near_y = tie(packed, near_x, near_y)
    dealt = lax.all_to_all(packed, lay.inner_axes, 0, 0, tiled=True)
    if nb == 10:
        turns, one, two = (0, 1, 2, 5, 6, 7, 8, 9, 3, 4), 3, 8
    else:
        turns, one, two = tuple(range(group_count * nb)), nb // 3, nb - nb // 3
    attended, ot, low, qt, kaug, vt, order = attention_forward(
        useg, place, (near, near_x, near_y) + far, queries, head_count, head_width, near_sizes,
        turns,
    )
    attended, dealt = tie(attended, dealt)
    grad_top = dealt[:, :slot_rows].reshape(rows, width)
    code = dealt[:, slot_rows, :slot_rows].reshape(rows, 1).astype(jnp.int32)
    core_at = jnp.stack([core, me // 4]).astype(jnp.int32)
    result, middle_grad, logit_low, norm_b_part, grads, qa, doa, dot_t = middle_pass(
        core_at, rows_low, attended, logits, code, grad_top, norm_b[None], out_w, up_w, down_w,
        (qt, ot, low), head_count, lay.count,
    )
    grads = grads.reshape(lay.count, -1, width)
    grads, qa = tie(grads, qa)
    swapped = plane_swap(order_pieces(grads, mine, lay), lay)
    normed_t = normed.T

    def backward(first, stop, dq, more_in):
        return attention_backward(
            useg, place, order, kaug, vt, qa, doa, qt, dot_t, dq, more_in,
            tuple(range(first, stop)), two, head_count, head_width,
        )

    dq, dkv = backward(0, one, None, None)
    dq, dkv, swapped = tie(dq, dkv, swapped)
    halves = plane_sum(swapped)
    halves = halves.reshape(halves.shape[0], 2, -1, width)
    weights_own = lax.dynamic_index_in_dim(halves, core, 1, keepdims=False)
    weights_other = exchange(
        lax.dynamic_index_in_dim(halves, 1 - core, 1, keepdims=False), "w", 2, 1
    )
    weight_terms = rest_terms(
        (weights_own.astype(F32) + weights_other.astype(F32)).astype(BF), lay
    )
    back = move_back(result, lay)
    dq, dkv = backward(one, two, dq, dkv)
    dq, dkv, back, *weight_terms = tie(dq, dkv, back, *weight_terms)
    output = take_back(back)
    weights_near = gather_near(sum(term.astype(F32) for term in weight_terms).astype(BF), lay)
    swapped = plane_swap(order_pieces(dkv, mine, lay), lay)
    dq, late = backward(two, nb, dq, normed_t)
    dq, late, swapped, weights_near = tie(dq, late, swapped, weights_near)
    early = rest_terms(plane_sum(swapped), lay)
    if lay.count != INNER:
        query_w_grad = inner(normed, dq).astype(BF)
        piece = width // 2 // lay.count
        query_parts = query_w_grad.reshape(2, lay.count, piece, width // 128, 128)
        query_parts = query_parts.transpose(1, 0, 3, 2, 4).reshape(lay.count, -1, 128)
        late = order_pieces(jnp.concatenate([late, query_parts], axis=1), mine, lay)
    swapped = plane_swap(late, lay)
    base = outer(dq, query_w) + outer(logit_low, router_w)
    early = sum(term.astype(F32) for term in early).astype(BF)
    swapped, base, weights_near = tie(swapped, base, weights_near)
    weights_x, weights_y = gather_sides(weights_near, lay)
    late = plane_sum(swapped)
    late, early = tie(late, early)
    late = rest_terms(late, lay)
    grad_rows, small, sums = last_pass(
        core_at, order, lay.count == INNER, rows_low, base, middle_grad, logit_low, norm_b_part, norm_a[None], keyval_w,
        [early], late, head_count,
    )
    grad_rows, small, weights_x, weights_y = tie(grad_rows, small, weights_x, weights_y)
    weights_far = gather_far(weights_x, weights_y, lay, w_down.shape[0] // lay.count)
    back = move_back(grad_rows, lay)
    other = exchange(small[1], "w", 2, 1)
    both = (small[0].astype(F32) + other.astype(F32)).astype(BF)
    total, rest = both[:sums], both[sums:][None]
    for axis in lay.axes[::-1]:
        total, rest = sum_and_gather(total, rest, axis, lay)
        if axis == lay.axes[1]:
            total, rest, back = tie(total, rest, back)
        elif axis == lay.axes[-1]:
            total, rest, *weights_far = tie(total, rest, *weights_far)
    input_grad = take_back(back).astype(F32)[None]
    query_sum = place_query(mine, rest, w_query.shape, lay)
    half = width // 2
    keyval_sum = total[:half].astype(F32)
    thin = total[half:].reshape(half // 128, -1, 128).transpose(1, 0, 2).reshape(-1, half)
    thin = thin.astype(F32)
    down_sum, up_sum, out_sum = place_pieces(
        (weights_near, weights_x, weights_y, *weights_far), mine,
        [w_down.shape, w_up.shape, w_out.shape], width, near_sizes,
    )
    return (
        output[None],
        input_grad,
        thin[head_count],
        query_sum,
        keyval_sum,
        thin[:head_count].T,
        out_sum,
        thin[head_count + 1],
        up_sum,
        down_sum,
    )


def solution(mesh):
    ctx_count, core_count = mesh.shape["ctx"], mesh.shape["wshard"]
    lay = Layout(ctx_count)
    grid = Mesh(mesh.devices.reshape(lay.sizes + (core_count,)), lay.axes + ("w",))
    ctx = lay.axes
    tokens = P("w", ctx, None)
    return jax.shard_map(
        functools.partial(on_device, lay),
        mesh=grid,
        in_specs=(
            tokens, tokens, P("w", ctx), tokens,
            P("w"), P("w", None), P("w", None), P("w", None), P("w", None),
            P("w"), P("w", None), P("w", None),
        ),
        out_specs=(
            tokens, tokens,
            P("w"), P("w", None), P("w", None), P("w", None), P("w", None),
            P("w"), P("w", None), P("w", None),
        ),
        check_vma=False,
    )
```

```python
import functools
import math

import jax
import jax.numpy as jnp
from jax import lax
from jax.experimental import pallas as pl
from jax.experimental.pallas import tpu as pltpu
from jax.sharding import Mesh, PartitionSpec as P

F32 = jnp.float32
BF = jnp.bfloat16
UNIT = 1024
TB = 64
INNER = UNIT // TB
RUN = 8
LOG2E = 1.4426950408889634
BIG = 2.0**100


def dot(lhs, rhs):
    return lax.dot_general(lhs, rhs, (((1,), (0,)), ((), ())), preferred_element_type=F32)


def inner(lhs, rhs):
    return lax.dot_general(lhs, rhs, (((0,), (0,)), ((), ())), preferred_element_type=F32)


def outer(lhs, rhs):
    return lax.dot_general(lhs, rhs, (((1,), (1,)), ((), ())), preferred_element_type=F32)


def split3(x):
    a = x.astype(BF)
    rest = x - a.astype(F32)
    b = rest.astype(BF)
    return a, b, (rest - b.astype(F32)).astype(BF)


def to_lanes(x, heads, hw):
    xt = x.T
    return jnp.concatenate([xt[h * hw : (h + 1) * hw] for h in range(heads)], axis=1)


def query_offsets(index, me):
    rest = index & (TB - 1)
    return (rest >> 3) * (RUN * INNER) + me * RUN + (rest & 7)


def near_index(rest, sizes):
    digits = []
    for size in sizes[::-1]:
        digits.append(rest % size)
        rest = rest // size
    index = 0
    for digit, size in zip(digits, sizes[::-1]):
        index = index * size + digit
    return index


def fetch_pieces(pieces, count, sizes, mine, total, put):
    near, near_x, near_y, far_a, far_b = pieces
    cut = far_a.shape[1]

    def one(c, carry):
        s = jnp.bitwise_xor(c, mine)
        index = near_index(s // 4, sizes)
        for side, ref in enumerate((near, near_x, near_y)):
            @pl.when(s % 4 == side)
            def _(ref=ref):
                put(c, 0, ref[index, :total, :])

        @pl.when(s % 4 == 3)
        def _():
            put(c, 0, far_a[index])
            put(c, cut, far_b[index, : total - cut, :])

        return carry

    lax.fori_loop(0, count, one, 0)


def fwd_kernel(
    useg, place, near, near_x, near_y, far_a, far_b, q_ref, o_ref, ot_ref, l_ref, qt_ref, kaug, vt, order,
    qa, acc, ref_row, plist, rank, ranked, bad, *, nb, slots, heads, hw, sizes, turns
):
    me, group = place[0], place[1]
    scale = LOG2E / math.sqrt(hw)
    lanes = heads * TB
    units = slots * nb

    def scan(u, n):
        rank[u] = n
        plist[n] = u
        return n + jnp.where(useg[u] == 0, 1, 0)

    prompt_units = lax.fori_loop(0, units, scan, jnp.int32(0))

    def settle(u, after):
        others = u - rank[u]
        ranked[jnp.where(useg[u] == 0, rank[u], prompt_units + others)] = u
        return after

    lax.fori_loop(0, units, settle, 0)
    for k in range(units):
        order[k] = ranked[turns[k]] if slots == 1 else k
    lane = lax.broadcasted_iota(jnp.int32, (UNIT, 2 * hw), 1)
    row = lax.broadcasted_iota(jnp.int32, (2 * hw, UNIT), 0)
    extra = jnp.where(lane < hw + 3, 1.0, 0.0).astype(BF)

    def put(c, first, rows):
        at = pl.multiple_of(c * nb * TB + first, TB)
        kaug[pl.ds(at, rows.shape[0]), :] = rows

    fetch_pieces(
        (near, near_x, near_y, far_a, far_b), slots * INNER, sizes, group * INNER + me, nb * TB, put
    )

    def split(u, carry):
        rows = pl.ds(pl.multiple_of(u * UNIT, UNIT), UNIT)
        tile = kaug[rows, :]
        kaug[rows, :] = jnp.where(lane < hw, tile, extra)
        flip = tile.T
        vt[u] = jnp.where(row < hw, jnp.ones_like(flip), flip)
        return carry

    lax.fori_loop(0, units, split, 0)

    def keys_of(u):
        return kaug[pl.ds(pl.multiple_of(u * UNIT, UNIT), UNIT), :]

    def block(i, carry):
        own = group * nb + i
        full_units = jnp.where(useg[own] != 0, prompt_units, rank[own])
        rows = pl.ds(pl.multiple_of(i * TB, TB), TB)
        qt = to_lanes(q_ref[rows, :], heads, hw)
        qt_ref[i] = qt
        qa[0:hw, :] = qt
        qa[hw:, :] = jnp.zeros((hw, lanes), BF)
        mask = lax.broadcasted_iota(jnp.int32, (UNIT, lanes), 0) <= query_offsets(
            lax.broadcasted_iota(jnp.int32, (UNIT, lanes), 1), me
        )
        few = UNIT // 4
        keys = kaug[pl.ds(pl.multiple_of(own * UNIT, UNIT), few), :]
        ref_row[...] = jnp.max(
            jnp.where(mask[:few], dot(keys, qa[...]), -1e30), axis=0, keepdims=True
        )
        bad[0] = 1

        def attempt(turn, carry):
            @pl.when(bad[0] != 0)
            def _():
                @pl.when(turn == 1)
                def _():
                    qa[hw:, :] = jnp.zeros((hw, lanes), BF)

                    def highest(k, carry):
                        u = jnp.where(k // 4 < full_units, plist[k // 4], own)
                        first = k % 4 * few
                        keys = kaug[pl.ds(pl.multiple_of(u * UNIT + first, few), few), :]
                        usable = first + lax.broadcasted_iota(
                            jnp.int32, (few, lanes), 0
                        ) <= query_offsets(lax.broadcasted_iota(jnp.int32, (few, lanes), 1), me)
                        ref_row[...] = jnp.maximum(
                            ref_row[...],
                            jnp.max(
                                jnp.where(usable | (u != own), dot(keys, qa[...]), -1e30),
                                axis=0, keepdims=True,
                            ),
                        )
                        return carry

                    lax.fori_loop(0, 4 * full_units + 4, highest, 0)

                a, b, c = split3(-ref_row[...])
                qa[hw:, :] = jnp.concatenate([a, b, c, jnp.zeros((hw - 3, lanes), BF)], axis=0)
                s = jnp.where(mask, dot(keys_of(own), qa[...]) * scale, -1e30)
                acc[...] = dot(vt[own], jnp.exp2(s).astype(BF))

                def full(k, carry):
                    u = plist[k]
                    p = jnp.exp2(dot(keys_of(u), qa[...]) * scale).astype(BF)
                    acc[...] += dot(vt[u], p)
                    return carry

                lax.fori_loop(0, full_units, full, 0)
                bad[0] = jnp.where(jnp.max(acc[0:1, :]) < BIG, 0, 1)

            return carry

        lax.fori_loop(0, 2, attempt, 0)
        ot = acc[hw:, :] / acc[0:hw, :]
        ot_ref[i] = ot
        l_ref[i] = ref_row[...] + jnp.log2(acc[0:1, :]) / scale
        on = jnp.concatenate([ot[:, h * TB : (h + 1) * TB] for h in range(heads)], axis=0)
        o_ref[rows, :] = on.T
        return carry

    lax.fori_loop(0, nb, block, 0)


def attention_forward(useg, place, pieces, q, heads, hw, sizes, turns):
    rows = q.shape[0]
    nb = rows // TB
    slots = 4 * pieces[0].shape[0] // INNER
    lanes = heads * TB
    units = slots * nb
    vm = pl.BlockSpec(memory_space=pltpu.VMEM)
    sm = pl.BlockSpec(memory_space=pltpu.SMEM)
    return pl.pallas_call(
        functools.partial(fwd_kernel, nb=nb, slots=slots, heads=heads, hw=hw, sizes=sizes, turns=turns),
        out_shape=(
            jax.ShapeDtypeStruct((rows, heads * hw), F32),
            jax.ShapeDtypeStruct((nb, hw, lanes), F32),
            jax.ShapeDtypeStruct((nb, 1, lanes), F32),
            jax.ShapeDtypeStruct((nb, hw, lanes), BF),
            jax.ShapeDtypeStruct((units * UNIT, 2 * hw), BF),
            jax.ShapeDtypeStruct((units, 2 * hw, UNIT), BF),
            jax.ShapeDtypeStruct((units,), jnp.int32),
        ),
        in_specs=[sm, sm] + [vm] * 6,
        out_specs=(vm,) * 6 + (sm,),
        scratch_shapes=[
            pltpu.VMEM((2 * hw, lanes), BF),
            pltpu.VMEM((2 * hw, lanes), F32),
            pltpu.VMEM((1, lanes), F32),
            pltpu.SMEM((units + 1,), jnp.int32),
            pltpu.SMEM((units + 1,), jnp.int32),
            pltpu.SMEM((units + 1,), jnp.int32),
            pltpu.SMEM((1,), jnp.int32),
        ],
        compiler_params=pltpu.CompilerParams(vmem_limit_bytes=60 << 20),
        cost_estimate=pl.CostEstimate(
            flops=40 * 10**9, bytes_accessed=8 << 20, transcendentals=26 * 10**6
        ),
        name="attention_forward",
    )(useg, place, *pieces, q)


def prepare_kernel(qt_ref, ot_ref, l_ref, do_ref, qa_ref, doa_ref, dot_ref, *, nb, heads, hw):
    pad = jnp.zeros((hw - 3, heads * TB), BF)

    def prepare(i, carry):
        rows = pl.ds(pl.multiple_of(i * TB, TB), TB)
        a, b, c = split3(-l_ref[i])
        qa_ref[i] = jnp.concatenate([qt_ref[i], a, b, c, pad], axis=0).T
        dt = to_lanes(do_ref[rows, :], heads, hw)
        dot_ref[i] = dt
        total = jnp.sum(dt.astype(F32) * ot_ref[i], axis=0, keepdims=True)
        a, b, c = split3(-total)
        doa_ref[i] = jnp.concatenate([a, b, c, pad, dt], axis=0).T
        return carry

    lax.fori_loop(0, nb, prepare, 0)


def bwd_kernel(
    useg, place, order, kaug_ref, vt_ref, qa, doa, qt, dot_t, *rest,
    nb, parts, first, last, dealt, heads, hw
):
    if first:
        dqacc, dkv_ref, kt, dkvt = rest
    elif last:
        dqold, normed, dq_ref, dkv_ref, dqacc, kt, dkvt = rest
    else:
        dqold, _, dqacc, dkv_ref, kt, dkvt = rest
    grid_at = pl.program_id(0)
    steps = pl.num_programs(0) - (2 if last and dealt else 0)
    step_at = jnp.minimum(grid_at, steps - 1)
    me, group = place[0], place[1]
    unit = order[step_at // len(parts) * nb + step_at % len(parts) + parts[0]]
    scale = LOG2E / math.sqrt(hw)
    lanes = heads * TB

    @pl.when(grid_at == 0)
    def _():
        dqacc[...] = jnp.zeros_like(dqacc) if first else dqold[...]

    unit_seg = useg[unit]

    def block(i, carry):
        own = group * nb + i

        def step(first, size, masked):
            keys = pl.ds(first, size)
            s = dot(qa[i], kt[:, keys]) * scale
            if masked:
                mask = first + lax.broadcasted_iota(
                    jnp.int32, (lanes, size), 1
                ) <= query_offsets(lax.broadcasted_iota(jnp.int32, (lanes, size), 0), me)
                s = jnp.where(mask, s, -1e30)
            p = jnp.exp2(s)
            ds = (p * dot(doa[i], vt_ref[0, :, keys])).astype(BF)
            dkvt[hw:, keys] += dot(dot_t[i], p.astype(BF))
            dkvt[:hw, keys] += dot(qt[i], ds)
            dqacc[i] += dot(ds, kaug_ref[keys, :])

        @pl.when((unit_seg == 0) & (own != unit) & ((useg[own] != 0) | (own > unit)))
        def _():
            step(0, UNIT, False)

        @pl.when(own == unit)
        def _():
            def part_of_own(k, carry):
                step(pl.multiple_of(k * (UNIT // 2), UNIT // 2), UNIT // 2, True)
                return carry

            lax.fori_loop(0, 2, part_of_own, 0)

        return carry

    def keys():
        kt[...] = kaug_ref[...].T
        dkvt[...] = jnp.zeros_like(dkvt)
        lax.fori_loop(0, nb, block, 0)
        factor = jnp.where(
            lax.broadcasted_iota(jnp.int32, (2 * hw, 1), 0) < hw, 1 / math.sqrt(hw), 1.0
        )
        dkv = (dkvt[...] * factor).T.reshape(TB // RUN, INNER, RUN, 2 * hw)
        for d in range(INNER):
            to = piece_at(d, me // 4, dealt)
            dkv_ref[to] = dkv[:, d].reshape(TB, 2 * hw).astype(BF)

    if last and dealt:
        pl.when(grid_at < steps)(keys)
    else:
        keys()

    if last:
        @pl.when(grid_at == steps - 1)
        def _():
            def finish(i, carry):
                rows = pl.ds(pl.multiple_of(i * TB, TB), TB)
                a = dqacc[i]
                dq_ref[rows, :] = (
                    jnp.concatenate([a[h * TB : (h + 1) * TB, :hw] for h in range(heads)], axis=1)
                    * (1 / math.sqrt(hw))
                ).astype(BF)
                return carry

            lax.fori_loop(0, nb, finish, 0)

    if last and dealt:
        @pl.when(grid_at >= steps)
        def _():
            width = dq_ref.shape[1]
            half = width // 2
            rows = pl.ds(pl.multiple_of((grid_at - steps) * half, half), half)
            grad = dot(normed[rows, :], dq_ref[...]).astype(BF)
            piece = half // INNER
            for c in range(INNER):
                to = piece_at(c, me // 4, dealt)
                for k in range(width // 128):
                    dkv_ref[to, k * piece : (k + 1) * piece, :] = grad[
                        c * piece : (c + 1) * piece, k * 128 : (k + 1) * 128
                    ]


def attention_backward(
    useg, place, order, kaug, vt, qa, doa, qt, dot_t, dqold, more_in, parts, joint, heads, hw
):
    nb, lanes, _ = qa.shape
    slots = vt.shape[0] // nb
    first, last = dqold is None, parts[-1] == nb - 1
    dealt = slots == 1
    more = 2 if last and dealt else 0
    turns_out = len(parts) + more if last else joint
    base = 0 if last else parts[0]
    vm = pl.BlockSpec(memory_space=pltpu.VMEM)
    acc_shape = jax.ShapeDtypeStruct((nb, lanes, 2 * hw), F32)
    count = len(parts)

    def at(u, seg, place, order):
        u = jnp.minimum(u, slots * count - 1)
        return order[u // count * nb + u % count + parts[0]]

    def to(u, seg, place, order):
        if dealt:
            return (0, u + base, 0)
        return (u // count, u % count + base, 0)

    return pl.pallas_call(
        functools.partial(
            bwd_kernel, nb=nb, parts=parts, first=first, last=last, dealt=dealt, heads=heads, hw=hw
        ),
        out_shape=(
            jax.ShapeDtypeStruct((nb * TB, heads * hw), BF) if last else acc_shape,
            jax.ShapeDtypeStruct((slots * INNER, turns_out * TB, 2 * hw), BF),
        ),
        grid_spec=pltpu.PrefetchScalarGridSpec(
            num_scalar_prefetch=3,
            grid=(slots * count + more,),
            in_specs=[
                pl.BlockSpec((UNIT, 2 * hw), lambda *a: (at(*a), 0)),
                pl.BlockSpec((1, 2 * hw, UNIT), lambda *a: (at(*a), 0, 0)),
            ]
            + [vm] * (4 if first else 6 if last else 5)
            + ([] if first or last else [pl.BlockSpec(memory_space=pl.ANY)]),
            out_specs=(
                vm,
                pl.BlockSpec((INNER, TB, 2 * hw), to),
            ),
            scratch_shapes=([pltpu.VMEM(acc_shape.shape, F32)] if last and not first else [])
            + [
                pltpu.VMEM((2 * hw, UNIT), BF),
                pltpu.VMEM((2 * hw, UNIT), F32),
            ],
        ),
        compiler_params=pltpu.CompilerParams(vmem_limit_bytes=60 << 20),
        cost_estimate=pl.CostEstimate(
            flops=8 * 10**9 * count, bytes_accessed=12 << 20, transcendentals=2 * 10**6 * count
        ),
        input_output_aliases={} if first or last else {10: 1},
        name="attention_backward",
    )(useg, place, order, kaug, vt, qa, doa, qt, dot_t, *([] if first else [dqold, more_in]))


def exact_dot(x, ones):
    a, b, c = split3(x)
    return dot(a, ones) + dot(b, ones) + dot(c, ones)


def norm_parts(values):
    mean_val = jnp.mean(values, axis=-1, keepdims=True)
    centered = values - mean_val
    variance = jnp.mean(centered * centered, axis=-1, keepdims=True)
    inverse = lax.rsqrt(variance + 1e-05)
    return centered * inverse, inverse


def norm_back(grad, unit, inverse, gain):
    scaled = grad * gain
    shift = jnp.mean(scaled, axis=-1, keepdims=True)
    along = jnp.mean(scaled * unit, axis=-1, keepdims=True)
    return inverse * (scaled - shift - unit * along)


def piece_at(c, my_rest, dealt):
    return c % 4 * (INNER // 4) + jnp.bitwise_xor(c // 4, my_rest) if dealt else c


def put_pieces(grads_ref, where, value, first, rows, at, count, step):
    piece = rows // 2 // count
    value = value.astype(BF)
    half = first // (rows // 2)
    device = (first - half * (rows // 2)) // piece
    for k in range(step // piece):
        to = piece_at(device + k, where[1], count == INNER)
        grads_ref[to, half, at : at + piece, :] = value[k * piece : (k + 1) * piece]


def middle_kernel(
    where, x_ref, att_ref, logit_ref, code_ref, cot_ref, norm_ref, out_w, up_w, down_w,
    qt_ref, ot_ref, low_ref,
    result_ref, middle_grad_ref, logit_grad_ref, norm_grad_ref, grads_ref, qa_ref, doa_ref, dot_ref,
    att_grad_s, mixed_s, normed_s, hidden_s, pre_s, branch_s, *, count, heads
):
    rows, width = x_ref.shape
    chunk = rows
    hw = width // heads
    gain = norm_ref[...].astype(F32)
    lane = lax.broadcasted_iota(jnp.int32, (chunk, 128), 1)
    head = lax.broadcasted_iota(jnp.int32, (128, width), 0)
    column = lax.broadcasted_iota(jnp.int32, (128, width), 1)
    widen = jnp.where(column // hw == head, 1.0, 0.0).astype(BF)
    narrow = jnp.where(
        lax.broadcasted_iota(jnp.int32, (width, 128), 0) // hw
        == lax.broadcasted_iota(jnp.int32, (width, 128), 1),
        1.0, 0.0,
    ).astype(BF)
    if True:
        at = slice(None)
        code = code_ref[at, :]
        chosen = ((code // heads == lane) | (code % heads == lane)) & (lane < heads)
        lifted = jnp.where(chosen, logit_ref[at, :], -1e30)
        raised = jnp.where(
            chosen, jnp.exp(lifted - jnp.max(lifted, axis=-1, keepdims=True)), 0.0
        )
        gate = raised / jnp.sum(raised, axis=-1, keepdims=True)
        gates = exact_dot(gate, widen)
        attended = att_ref[at, :]
        mixed = (gates * attended).astype(BF)
        mixed_s[at, :] = mixed
        middle = x_ref[at, :].astype(F32) + dot(mixed, out_w[...])
        unit, inverse = norm_parts(middle)
        normed = (unit * gain).astype(BF)
        normed_s[at, :] = normed
        cot = cot_ref[at, :]
        back = jnp.zeros((chunk, width), F32)
        step = 1024

        def hidden_block(k, sums):
            total, back = sums
            to = pl.ds(pl.multiple_of(k * step, step), step)
            pre = dot(normed, up_w[:, to])
            inside = 0.7978845608028654 * (pre + 0.044715 * pre * pre * pre)
            t = jnp.tanh(inside)
            half = 0.5 * (1.0 + t)
            hidden = (pre * half).astype(BF)
            slope = half + 0.5 * pre * (1.0 - t * t) * (
                0.7978845608028654 * (1.0 + 3 * 0.044715 * pre * pre)
            )
            hidden_s[:, to] = hidden
            pre_grad = (outer(cot, down_w[to, :]) * slope).astype(BF)
            pre_s[:, to] = pre_grad
            return total + dot(hidden, down_w[to, :]), back + outer(pre_grad, up_w[:, to])

        total, back = lax.fori_loop(0, up_w.shape[1] // step, hidden_block, (middle, back))
        result_ref[at, :] = total.astype(BF)
        norm_grad_ref[...] = jnp.sum(
            (back * unit).reshape(chunk // 8, 8, width), axis=0
        )
        middle_grad = cot.astype(F32) + norm_back(back, unit, inverse, gain)
        middle_grad_ref[at, :] = middle_grad
        branch = middle_grad.astype(BF)
        branch_s[at, :] = branch
        mixed_grad = outer(branch, out_w[...])
        gate_grad = exact_dot(mixed_grad * attended, narrow)
        logit_grad_ref[at, :] = (
            gate * (gate_grad - jnp.sum(gate * gate_grad, axis=-1, keepdims=True))
        ).astype(BF)
        att_grad_s[at, :] = (gates * mixed_grad).astype(BF)
    prepare_kernel(
        qt_ref, ot_ref, low_ref, att_grad_s, qa_ref, doa_ref, dot_ref,
        nb=qt_ref.shape[0], heads=heads, hw=hw,
    )
    ff = hidden_s.shape[1]
    across = width
    half, down_rows = width // 2, ff // 2 // count

    def down_block(k, carry):
        at = pl.ds(pl.multiple_of(k * width, width), width)
        put_pieces(grads_ref, where, inner(hidden_s[:, at], cot), k * width, ff, 0, count, width)
        return carry

    lax.fori_loop(0, ff // width, down_block, 0)

    block = half // 2

    def up_block(k, carry):
        at = pl.ds(pl.multiple_of(k * block, block), block)
        up = inner(normed_s[:, at], pre_s[...])
        piece = half // count
        for c in range(ff // width):
            put_pieces(
                grads_ref, where, up[:, c * width : (c + 1) * width], k * block, width,
                down_rows + c * piece, count, block,
            )
        put_pieces(
            grads_ref, where, inner(mixed_s[:, at], branch_s[...]), k * block, width,
            down_rows + ff // width * piece, count, block,
        )
        return carry

    lax.fori_loop(0, width // block, up_block, 0)


def middle_pass(core, x, attended, logits, code, cot, norm_b, out_w, up_w, down_w, kept, heads, count):
    rows, width = x.shape
    nb, hw, lanes = kept[0].shape
    ff = up_w.shape[1]
    piece_rows = (ff * 2 + width) // (2 * count)
    vm = pl.BlockSpec(memory_space=pltpu.VMEM)
    shape = jax.ShapeDtypeStruct
    return pl.pallas_call(
        functools.partial(middle_kernel, count=count, heads=heads),
        out_shape=(
            shape((rows, width), BF),
            shape((rows, width), F32),
            shape((rows, 128), BF),
            shape((8, width), F32),
            shape((count, 2, piece_rows, width), BF),
            shape((nb, lanes, 2 * hw), BF),
            shape((nb, lanes, 2 * hw), BF),
            shape((nb, hw, lanes), BF),
        ),
        in_specs=[pl.BlockSpec(memory_space=pltpu.SMEM)] + [vm] * 12,
        out_specs=(vm,) * 8,
        scratch_shapes=[
            pltpu.VMEM((rows, width), BF),
            pltpu.VMEM((rows, width), BF),
            pltpu.VMEM((rows, width), BF),
            pltpu.VMEM((rows, ff), BF),
            pltpu.VMEM((rows, ff), BF),
            pltpu.VMEM((rows, width), BF),
        ],
        compiler_params=pltpu.CompilerParams(vmem_limit_bytes=60 << 20),
        cost_estimate=pl.CostEstimate(
            flops=9 * 10**9, bytes_accessed=24 << 20, transcendentals=2 * 10**6
        ),
        name="middle_pass",
    )(core, x, attended, logits, code, cot, norm_b, out_w, up_w, down_w, *kept)


class Layout:
    def __init__(self, ctx_count):
        sizes = [4]
        while math.prod(sizes) < ctx_count:
            sizes.append(2)
        assert math.prod(sizes) == ctx_count
        self.sizes = tuple(sizes)
        self.axes = tuple(f"c{k}" for k in range(len(sizes)))
        cut = len(sizes)
        while math.prod(sizes[cut:]) < INNER:
            cut -= 1
        assert math.prod(sizes[cut:]) == INNER
        self.outer_axes, self.inner_axes = self.axes[:cut], self.axes[cut:]
        self.count = ctx_count


def exchange(x, axis, size, step):
    return lax.ppermute(x, axis, [(i, i ^ step) for i in range(size)])


def spread(x, order, lay, start=0, stop=None):
    for axis in order[start:stop]:
        size = lay.sizes[lay.axes.index(axis)]
        x = jnp.concatenate([x] + [exchange(x, axis, size, step) for step in range(1, size)])
    return x


def gather_near(x, lay):
    return spread(x[None], lay.axes[:-2], lay)


def gather_sides(near, lay):
    y_axis, x_axis = lay.axes[-2:]
    return exchange(near, x_axis, 2, 1), exchange(near, y_axis, 2, 1)


def gather_far(near_x, near_y, lay, cut):
    y_axis, x_axis = lay.axes[-2:]
    return exchange(near_x[:, :cut], y_axis, 2, 1), exchange(near_y[:, cut:], x_axis, 2, 1)


def deal(x, lay):
    rows, width = x.shape
    packed = x.reshape(rows // (RUN * INNER), INNER, RUN, width).transpose(1, 0, 2, 3)
    packed = packed.reshape(INNER, rows // INNER, width)
    return lax.all_to_all(packed, lay.inner_axes, 0, 0, tiled=True)


def move_back(x, lay):
    rows, width = x.shape
    return lax.all_to_all(x.reshape(INNER, rows // INNER, width), lay.inner_axes, 0, 0, tiled=True)


def take_back(back):
    rows, width = back.shape[0] * back.shape[1], back.shape[2]
    back = back.reshape(INNER, rows // (RUN * INNER), RUN, width).transpose(1, 0, 2, 3)
    return back.reshape(rows, width)


def tie(*values):
    return lax.optimization_barrier(values)


def order_pieces(pieces, mine, lay):
    if lay.count == INNER:
        return pieces
    index = jnp.arange(lay.count, dtype=jnp.int32)
    quarter = lay.count // 4
    rest = jnp.bitwise_xor(index % quarter, mine // 4)
    return jnp.take(pieces, rest * 4 + index // quarter, axis=0)


def plane_swap(pieces, lay):
    return lax.all_to_all(pieces, lay.axes[-2:], 0, 0, tiled=True)


def plane_sum(pieces):
    return add_pieces(pieces.reshape((4, -1) + pieces.shape[1:]))


def rest_terms(pieces, lay):
    axes = list(zip(lay.axes, lay.sizes))[:-2]
    for k, (axis, size) in enumerate(axes):
        pieces = pieces.reshape((size, -1) + pieces.shape[1:])
        terms = [pieces[0]] + [exchange(pieces[step], axis, size, step) for step in range(1, size)]
        if k < len(axes) - 1:
            pieces = sum(term.astype(F32) for term in terms).astype(BF)
    return [term[0] for term in terms]


def add_pieces(pieces):
    return jnp.sum(pieces.astype(F32), axis=0).astype(BF)


def add_terms(refs):
    total = refs[0][...].astype(F32)
    for ref in refs[1:]:
        total = total + ref[...].astype(F32)
    return total.astype(BF)


def last_kernel(
    core, order, x_ref, base_ref, middle_grad_ref, logit_ref, norm_b_ref, gain_ref, keyval_w, *rest,
    heads, dealt
):
    first, *terms, grad_ref, small_ref, keyval_s = rest
    rows, width = x_ref.shape
    gain = gain_ref[...].astype(F32)
    unit, inverse = norm_parts(x_ref[...].astype(F32))
    normed = (unit * gain).astype(BF)
    early, late = first[...], add_terms(terms)
    late_rows = rows - early.shape[0]
    turned = jnp.concatenate([early, late[:late_rows]], axis=0)
    for k in range(rows // TB):
        to = pl.multiple_of((order[k] if dealt else k) * TB, TB)
        keyval_s[pl.ds(to, TB), :] = turned[k * TB : (k + 1) * TB]
    keyval_grad = keyval_s[...]
    grad = base_ref[...] + outer(keyval_grad, keyval_w[...])
    grad_ref[...] = (middle_grad_ref[...] + norm_back(grad, unit, inverse, gain)).astype(BF)
    keyval_sum = inner(normed, keyval_grad).astype(BF)
    thin = jnp.concatenate(
        [
            inner(logit_ref[...], normed)[:heads],
            jnp.sum(grad * unit, axis=0, keepdims=True),
            jnp.sum(norm_b_ref[...], axis=0, keepdims=True),
            jnp.zeros((-(heads + 2) % 16, width), F32),
        ],
        axis=0,
    ).astype(BF)
    half, query_half = width // 2, (late.shape[0] - late_rows) // 2
    for side in range(2):
        to = jnp.bitwise_xor(core[0], side)
        small_ref[to, :half, :] = keyval_sum[side * half : (side + 1) * half]
        first = half
        for c in range(side * half, (side + 1) * half, 128):
            small_ref[to, first : first + thin.shape[0], :] = thin[:, c : c + 128]
            first += thin.shape[0]
        small_ref[to, first:, :] = late[late_rows + side * query_half :][:query_half]


def last_pass(core, order, dealt, x, base, middle_grad, logit_low, norm_b_part, gain, keyval_w, early, late, heads):
    rows, width = x.shape
    query_half = (late[0].shape[0] + early[0].shape[0] - rows) // 2
    thin_rows = (heads + 2 + -(heads + 2) % 16) * (width // 2) // 128
    sums = width // 2 + thin_rows
    arrays = (x, base, middle_grad, logit_low, norm_b_part, gain, keyval_w, *early, *late)
    vm = pl.BlockSpec(memory_space=pltpu.VMEM)
    grad, small = pl.pallas_call(
        functools.partial(last_kernel, heads=heads, dealt=dealt),
        out_shape=(
            jax.ShapeDtypeStruct((rows, width), BF),
            jax.ShapeDtypeStruct((2, sums + query_half, 128), BF),
        ),
        grid=(1,),
        in_specs=[pl.BlockSpec(memory_space=pltpu.SMEM)] * 2
        + [pl.BlockSpec(a.shape, lambda g: (0, 0)) for a in arrays],
        out_specs=(vm,) * 2,
        scratch_shapes=[pltpu.VMEM((rows, keyval_w.shape[1]), BF)],
        compiler_params=pltpu.CompilerParams(vmem_limit_bytes=40 << 20),
        cost_estimate=pl.CostEstimate(flops=10**9, bytes_accessed=6 << 20, transcendentals=0),
        name="last_pass",
    )(core, order, *arrays)
    return grad, small, sums


def sum_and_gather(total, rest, axis, lay):
    sums, height = total.shape[0], rest.shape[1]
    size = lay.sizes[lay.axes.index(axis)]
    send = jnp.concatenate([total, rest.reshape(-1, 128)], axis=0)
    got = [exchange(send, axis, size, step) for step in range(1, size)]
    terms = [total.astype(F32)] + [other[:sums].astype(F32) for other in got]
    while len(terms) > 1:
        terms = [terms[k] + terms[k + 1] for k in range(0, len(terms), 2)]
    rest = jnp.concatenate(
        [rest] + [other[sums:].reshape(-1, height, 128) for other in got], axis=0
    )
    return terms[0].astype(BF), rest


def query_kernel(mine, rest_ref, out_ref, *, count):
    piece = out_ref.shape[0] // count
    for c in range(count):
        at = jnp.bitwise_xor(c, mine[0])
        for k in range(out_ref.shape[1] // 128):
            out_ref[c * piece : (c + 1) * piece, k * 128 : (k + 1) * 128] = rest_ref[
                at, k * piece : (k + 1) * piece, :
            ].astype(F32)


def place_query(mine, rest, shape, lay):
    vm = pl.BlockSpec(memory_space=pltpu.VMEM)
    return pl.pallas_call(
        functools.partial(query_kernel, count=lay.count),
        out_shape=jax.ShapeDtypeStruct(shape, F32),
        in_specs=[pl.BlockSpec(memory_space=pltpu.SMEM), vm],
        out_specs=vm,
        name="place_query",
    )(mine, rest)


def place_kernel(mine, near, near_x, near_y, far_a, far_b, *outs, count, across, sizes):
    *outs, piece_s = outs
    cut = far_a.shape[1]
    looped = all(out.shape[0] // count % 8 == 0 for out in outs)

    def one(c, carry):
        s = jnp.bitwise_xor(c, mine[0])
        index = near_index(s // 4, sizes)
        for side, ref in enumerate((near, near_x, near_y)):
            @pl.when(s % 4 == side)
            def _(ref=ref):
                piece_s[...] = ref[index]

        @pl.when(s % 4 == 3)
        def _():
            piece_s[:cut, :] = far_a[index]
            piece_s[cut:, :] = far_b[index]

        first = 0
        for out in outs:
            piece = out.shape[0] // count
            rows = pl.ds(pl.multiple_of(c * piece, piece) if looped else c * piece, piece)
            for k in range(out.shape[1] // across):
                out[rows, k * across : (k + 1) * across] = piece_s[
                    first : first + piece, :
                ].astype(F32)
                first += piece
        return carry

    if looped:
        lax.fori_loop(0, count, one, 0)
    else:
        for c in range(count):
            one(c, 0)


def place_pieces(pieces, mine, shapes, across, sizes):
    vm = pl.BlockSpec(memory_space=pltpu.VMEM)
    count = 4 * pieces[0].shape[0]
    return pl.pallas_call(
        functools.partial(place_kernel, count=count, across=across, sizes=sizes),
        out_shape=tuple(jax.ShapeDtypeStruct(shape, F32) for shape in shapes),
        in_specs=[pl.BlockSpec(memory_space=pltpu.SMEM)] + [vm] * 5,
        out_specs=(vm,) * len(shapes),
        scratch_shapes=[pltpu.VMEM(pieces[0].shape[1:], BF)],
        compiler_params=pltpu.CompilerParams(vmem_limit_bytes=40 << 20),
        cost_estimate=pl.CostEstimate(
            flops=0, bytes_accessed=24 * pieces[0].size, transcendentals=0
        ),
        name="place_pieces",
    )(mine, *pieces)


def layer_norm(values, gain_vec):
    mean_val = jnp.mean(values, axis=-1, keepdims=True)
    centered = values - mean_val
    variance = jnp.mean(centered * centered, axis=-1, keepdims=True)
    return centered * lax.rsqrt(variance + 1e-05) * gain_vec


def on_device(
    lay, inputs, cotangent, segments, routes, norm_first, w_query, w_keyval, w_router, w_out,
    norm_second, w_up, w_down
):
    def whole(shard):
        return lax.all_gather(shard, "w", axis=0, tiled=True)

    rows, width = inputs.shape[1:]
    head_count = w_router.shape[1]
    head_width = w_keyval.shape[1] // 2
    nb = rows // TB
    group_count = lay.count // INNER
    me = lax.axis_index(lay.inner_axes)
    group = lax.axis_index(lay.outer_axes) if lay.outer_axes else jnp.int32(0)
    place = jnp.stack([me, group]).astype(jnp.int32)
    mine = (group * INNER + me).astype(jnp.int32)[None]

    core = lax.axis_index("w")
    near_sizes = lay.sizes[:-2]

    def whole_by_exchange(shard):
        other = exchange(shard, "w", 2, 1)
        return jnp.where(
            core == 0,
            jnp.concatenate([shard, other], axis=0),
            jnp.concatenate([other, shard], axis=0),
        )

    narrow = whole(
        jnp.concatenate([w_keyval, w_router, norm_first[:, None], norm_second[:, None]], axis=1)
    )
    keyval_w = narrow[:, : 2 * head_width]
    narrow = narrow[:, 2 * head_width :]
    router_w = jnp.pad(narrow[:, :head_count], ((0, 0), (0, 128 - head_count)))
    norm_a, norm_b = narrow[:, head_count], narrow[:, head_count + 1]
    own_normed = layer_norm(inputs[0].astype(F32), norm_a.astype(F32)).astype(BF)
    spans = rows // (RUN * INNER)
    own_seg = segments[:, :: RUN * INNER].astype(BF)
    own_seg = jnp.pad(own_seg, ((0, 7), (0, 2 * head_width - spans)))
    near = gather_near(
        jnp.concatenate([dot(own_normed, keyval_w).astype(BF), own_seg], axis=0), lay
    )
    near_x, near_y = gather_sides(near, lay)
    rows_low = deal(inputs[0], lay).reshape(rows, width)
    near_x, near_y, rows_low = tie(near_x, near_y, rows_low)
    far = gather_far(near_x, near_y, lay, (nb // 2) * TB)
    query_w, out_w = whole(w_query), whole(w_out)
    up_w, down_w = whole_by_exchange(w_up), whole_by_exchange(w_down)

    quarter = lay.count // 4
    entry = [near_index(rest, near_sizes) for rest in range(quarter)]
    source = [entry.index(k) * 4 + side for side in range(4) for k in range(quarter)]
    source = jnp.bitwise_xor(jnp.array(source, jnp.int32), mine)
    far_rows = rows - (nb // 2) * TB
    all_seg = jnp.concatenate(
        [near[:, rows], near_x[:, rows], near_y[:, rows], far[1][:, far_rows]], axis=0
    ).astype(jnp.int32)
    at = source[:, None] * spans + jnp.arange(128, dtype=jnp.int32)[None]
    at = jnp.where(jnp.arange(128)[None] < spans, at, -1)
    first = jnp.arange(group_count * nb, dtype=jnp.int32) * (UNIT // (RUN * INNER))
    useg = jnp.sum(jnp.where(at[None] == first[:, None, None], all_seg[None], 0), axis=(1, 2))

    rows_in = rows_low.astype(F32)
    normed = layer_norm(rows_in, norm_a.astype(F32)).astype(BF)
    queries = dot(normed, query_w).astype(BF)
    logits = dot(normed, router_w)

    code = (routes[0, :, 0] * head_count + routes[0, :, 1]).astype(BF)
    slot_rows = rows // INNER
    code = code.reshape(rows // (RUN * INNER), INNER, RUN).transpose(1, 0, 2)
    code = jnp.pad(code.reshape(INNER, 1, slot_rows), ((0, 0), (0, RUN - 1), (0, width - slot_rows)))
    packed = cotangent[0].reshape(rows // (RUN * INNER), INNER, RUN, width).transpose(1, 0, 2, 3)
    packed = jnp.concatenate([packed.reshape(INNER, slot_rows, width), code], axis=1)
    packed, near_x, near_y = tie(packed, near_x, near_y)
    dealt = lax.all_to_all(packed, lay.inner_axes, 0, 0, tiled=True)
    if nb == 10:
        turns, one, two = (0, 1, 2, 5, 6, 7, 8, 9, 3, 4), 3, 8
    else:
        turns, one, two = tuple(range(group_count * nb)), nb // 3, nb - nb // 3
    attended, ot, low, qt, kaug, vt, order = attention_forward(
        useg, place, (near, near_x, near_y) + far, queries, head_count, head_width, near_sizes,
        turns,
    )
    attended, dealt = tie(attended, dealt)
    grad_top = dealt[:, :slot_rows].reshape(rows, width)
    code = dealt[:, slot_rows, :slot_rows].reshape(rows, 1).astype(jnp.int32)
    core_at = jnp.stack([core, me // 4]).astype(jnp.int32)
    result, middle_grad, logit_low, norm_b_part, grads, qa, doa, dot_t = middle_pass(
        core_at, rows_low, attended, logits, code, grad_top, norm_b[None], out_w, up_w, down_w,
        (qt, ot, low), head_count, lay.count,
    )
    grads = grads.reshape(lay.count, -1, width)
    grads, qa = tie(grads, qa)
    swapped = plane_swap(order_pieces(grads, mine, lay), lay)
    normed_t = normed.T

    def backward(first, stop, dq, more_in):
        return attention_backward(
            useg, place, order, kaug, vt, qa, doa, qt, dot_t, dq, more_in,
            tuple(range(first, stop)), two, head_count, head_width,
        )

    dq, dkv = backward(0, one, None, None)
    dq, dkv, swapped = tie(dq, dkv, swapped)
    halves = plane_sum(swapped)
    halves = halves.reshape(halves.shape[0], 2, -1, width)
    weights_own = lax.dynamic_index_in_dim(halves, core, 1, keepdims=False)
    weights_other = exchange(
        lax.dynamic_index_in_dim(halves, 1 - core, 1, keepdims=False), "w", 2, 1
    )
    weight_terms = rest_terms(
        (weights_own.astype(F32) + weights_other.astype(F32)).astype(BF), lay
    )
    back = move_back(result, lay)
    dq, dkv = backward(one, two, dq, dkv)
    dq, dkv, back, *weight_terms = tie(dq, dkv, back, *weight_terms)
    output = take_back(back)
    weights_near = gather_near(sum(term.astype(F32) for term in weight_terms).astype(BF), lay)
    swapped = plane_swap(order_pieces(dkv, mine, lay), lay)
    dq, late = backward(two, nb, dq, normed_t)
    dq, late, swapped, weights_near = tie(dq, late, swapped, weights_near)
    early = rest_terms(plane_sum(swapped), lay)
    if lay.count != INNER:
        query_w_grad = inner(normed, dq).astype(BF)
        piece = width // 2 // lay.count
        query_parts = query_w_grad.reshape(2, lay.count, piece, width // 128, 128)
        query_parts = query_parts.transpose(1, 0, 3, 2, 4).reshape(lay.count, -1, 128)
        late = order_pieces(jnp.concatenate([late, query_parts], axis=1), mine, lay)
    swapped = plane_swap(late, lay)
    base = outer(dq, query_w) + outer(logit_low, router_w)
    early = sum(term.astype(F32) for term in early).astype(BF)
    swapped, base, weights_near = tie(swapped, base, weights_near)
    weights_x, weights_y = gather_sides(weights_near, lay)
    late = plane_sum(swapped)
    late, early = tie(late, early)
    late = rest_terms(late, lay)
    grad_rows, small, sums = last_pass(
        core_at, order, lay.count == INNER, rows_low, base, middle_grad, logit_low, norm_b_part, norm_a[None], keyval_w,
        [early], late, head_count,
    )
    grad_rows, small, weights_x, weights_y = tie(grad_rows, small, weights_x, weights_y)
    weights_far = gather_far(weights_x, weights_y, lay, w_down.shape[0] // lay.count)
    back = move_back(grad_rows, lay)
    other = exchange(small[1], "w", 2, 1)
    both = (small[0].astype(F32) + other.astype(F32)).astype(BF)
    total, rest = both[:sums], both[sums:][None]
    for axis in lay.axes[::-1]:
        total, rest = sum_and_gather(total, rest, axis, lay)
        if axis == lay.axes[1]:
            total, rest, back = tie(total, rest, back)
        elif axis == lay.axes[-1]:
            total, rest, *weights_far = tie(total, rest, *weights_far)
    input_grad = take_back(back).astype(F32)[None]
    query_sum = place_query(mine, rest, w_query.shape, lay)
    half = width // 2
    keyval_sum = total[:half].astype(F32)
    thin = total[half:].reshape(half // 128, -1, 128).transpose(1, 0, 2).reshape(-1, half)
    thin = thin.astype(F32)
    down_sum, up_sum, out_sum = place_pieces(
        (weights_near, weights_x, weights_y, *weights_far), mine,
        [w_down.shape, w_up.shape, w_out.shape], width, near_sizes,
    )
    return (
        output[None],
        input_grad,
        thin[head_count],
        query_sum,
        keyval_sum,
        thin[:head_count].T,
        out_sum,
        thin[head_count + 1],
        up_sum,
        down_sum,
    )


def solution(mesh):
    ctx_count, core_count = mesh.shape["ctx"], mesh.shape["wshard"]
    lay = Layout(ctx_count)
    grid = Mesh(mesh.devices.reshape(lay.sizes + (core_count,)), lay.axes + ("w",))
    ctx = lay.axes
    tokens = P("w", ctx, None)
    return jax.shard_map(
        functools.partial(on_device, lay),
        mesh=grid,
        in_specs=(
            tokens, tokens, P("w", ctx), tokens,
            P("w"), P("w", None), P("w", None), P("w", None), P("w", None),
            P("w"), P("w", None), P("w", None),
        ),
        out_specs=(
            tokens, tokens,
            P("w"), P("w", None), P("w", None), P("w", None), P("w", None),
            P("w"), P("w", None), P("w", None),
        ),
        check_vma=False,
    )
```

```python
import functools
import math

import jax
import jax.numpy as jnp
from jax import lax
from jax.experimental import pallas as pl
from jax.experimental.pallas import tpu as pltpu
from jax.sharding import Mesh, PartitionSpec as P

F32 = jnp.float32
BF = jnp.bfloat16
UNIT = 1024
TB = 64
INNER = UNIT // TB
RUN = 8
LOG2E = 1.4426950408889634
BIG = 2.0**100


def dot(lhs, rhs):
    return lax.dot_general(lhs, rhs, (((1,), (0,)), ((), ())), preferred_element_type=F32)


def inner(lhs, rhs):
    return lax.dot_general(lhs, rhs, (((0,), (0,)), ((), ())), preferred_element_type=F32)


def outer(lhs, rhs):
    return lax.dot_general(lhs, rhs, (((1,), (1,)), ((), ())), preferred_element_type=F32)


def split3(x):
    a = x.astype(BF)
    rest = x - a.astype(F32)
    b = rest.astype(BF)
    return a, b, (rest - b.astype(F32)).astype(BF)


def to_lanes(x, heads, hw):
    xt = x.T
    return jnp.concatenate([xt[h * hw : (h + 1) * hw] for h in range(heads)], axis=1)


def query_offsets(index, me):
    rest = index & (TB - 1)
    return (rest >> 3) * (RUN * INNER) + me * RUN + (rest & 7)


def near_index(rest, sizes):
    digits = []
    for size in sizes[::-1]:
        digits.append(rest % size)
        rest = rest // size
    index = 0
    for digit, size in zip(digits, sizes[::-1]):
        index = index * size + digit
    return index


def fetch_pieces(pieces, count, sizes, mine, total, put):
    near, near_x, near_y, far_a, far_b = pieces
    cut = far_a.shape[1]

    def one(c, carry):
        s = jnp.bitwise_xor(c, mine)
        index = near_index(s // 4, sizes)
        for side, ref in enumerate((near, near_x, near_y)):
            @pl.when(s % 4 == side)
            def _(ref=ref):
                put(c, 0, ref[index, :total, :])

        @pl.when(s % 4 == 3)
        def _():
            put(c, 0, far_a[index])
            put(c, cut, far_b[index, : total - cut, :])

        return carry

    lax.fori_loop(0, count, one, 0)


def fwd_kernel(
    useg, place, near, near_x, near_y, far_a, far_b, q_ref, o_ref, ot_ref, l_ref, qt_ref, kaug, vt, order,
    qa, acc, ref_row, plist, rank, ranked, bad, *, nb, slots, heads, hw, sizes, turns
):
    me, group = place[0], place[1]
    scale = LOG2E / math.sqrt(hw)
    lanes = heads * TB
    units = slots * nb

    def scan(u, n):
        rank[u] = n
        plist[n] = u
        return n + jnp.where(useg[u] == 0, 1, 0)

    prompt_units = lax.fori_loop(0, units, scan, jnp.int32(0))

    def settle(u, after):
        others = u - rank[u]
        ranked[jnp.where(useg[u] == 0, rank[u], prompt_units + others)] = u
        return after

    lax.fori_loop(0, units, settle, 0)
    for k in range(units):
        order[k] = ranked[turns[k]] if slots == 1 else k
    lane = lax.broadcasted_iota(jnp.int32, (UNIT, 2 * hw), 1)
    row = lax.broadcasted_iota(jnp.int32, (2 * hw, UNIT), 0)
    extra = jnp.where(lane < hw + 3, 1.0, 0.0).astype(BF)

    def put(c, first, rows):
        at = pl.multiple_of(c * nb * TB + first, TB)
        kaug[pl.ds(at, rows.shape[0]), :] = rows

    fetch_pieces(
        (near, near_x, near_y, far_a, far_b), slots * INNER, sizes, group * INNER + me, nb * TB, put
    )

    def split(u, carry):
        rows = pl.ds(pl.multiple_of(u * UNIT, UNIT), UNIT)
        tile = kaug[rows, :]
        kaug[rows, :] = jnp.where(lane < hw, tile, extra)
        flip = tile.T
        vt[u] = jnp.where(row < hw, jnp.ones_like(flip), flip)
        return carry

    lax.fori_loop(0, units, split, 0)

    def keys_of(u):
        return kaug[pl.ds(pl.multiple_of(u * UNIT, UNIT), UNIT), :]

    def block(i, carry):
        own = group * nb + i
        full_units = jnp.where(useg[own] != 0, prompt_units, rank[own])
        rows = pl.ds(pl.multiple_of(i * TB, TB), TB)
        qt = to_lanes(q_ref[rows, :], heads, hw)
        qt_ref[i] = qt
        qa[0:hw, :] = qt
        qa[hw:, :] = jnp.zeros((hw, lanes), BF)
        mask = lax.broadcasted_iota(jnp.int32, (UNIT, lanes), 0) <= query_offsets(
            lax.broadcasted_iota(jnp.int32, (UNIT, lanes), 1), me
        )
        few = UNIT // 4
        keys = kaug[pl.ds(pl.multiple_of(own * UNIT, UNIT), few), :]
        ref_row[...] = jnp.max(
            jnp.where(mask[:few], dot(keys, qa[...]), -1e30), axis=0, keepdims=True
        )
        bad[0] = 1

        def attempt(turn, carry):
            @pl.when(bad[0] != 0)
            def _():
                @pl.when(turn == 1)
                def _():
                    qa[hw:, :] = jnp.zeros((hw, lanes), BF)

                    def highest(k, carry):
                        u = jnp.where(k // 4 < full_units, plist[k // 4], own)
                        first = k % 4 * few
                        keys = kaug[pl.ds(pl.multiple_of(u * UNIT + first, few), few), :]
                        usable = first + lax.broadcasted_iota(
                            jnp.int32, (few, lanes), 0
                        ) <= query_offsets(lax.broadcasted_iota(jnp.int32, (few, lanes), 1), me)
                        ref_row[...] = jnp.maximum(
                            ref_row[...],
                            jnp.max(
                                jnp.where(usable | (u != own), dot(keys, qa[...]), -1e30),
                                axis=0, keepdims=True,
                            ),
                        )
                        return carry

                    lax.fori_loop(0, 4 * full_units + 4, highest, 0)

                a, b, c = split3(-ref_row[...])
                qa[hw:, :] = jnp.concatenate([a, b, c, jnp.zeros((hw - 3, lanes), BF)], axis=0)
                s = jnp.where(mask, dot(keys_of(own), qa[...]) * scale, -1e30)
                acc[...] = dot(vt[own], jnp.exp2(s).astype(BF))

                def full(k, carry):
                    u = plist[k]
                    p = jnp.exp2(dot(keys_of(u), qa[...]) * scale).astype(BF)
                    acc[...] += dot(vt[u], p)
                    return carry

                lax.fori_loop(0, full_units, full, 0)
                bad[0] = jnp.where(jnp.max(acc[0:1, :]) < BIG, 0, 1)

            return carry

        lax.fori_loop(0, 2, attempt, 0)
        ot = acc[hw:, :] / acc[0:hw, :]
        ot_ref[i] = ot
        l_ref[i] = ref_row[...] + jnp.log2(acc[0:1, :]) / scale
        on = jnp.concatenate([ot[:, h * TB : (h + 1) * TB] for h in range(heads)], axis=0)
        o_ref[rows, :] = on.T
        return carry

    lax.fori_loop(0, nb, block, 0)


def attention_forward(useg, place, pieces, q, heads, hw, sizes, turns):
    rows = q.shape[0]
    nb = rows // TB
    slots = 4 * pieces[0].shape[0] // INNER
    lanes = heads * TB
    units = slots * nb
    vm = pl.BlockSpec(memory_space=pltpu.VMEM)
    sm = pl.BlockSpec(memory_space=pltpu.SMEM)
    return pl.pallas_call(
        functools.partial(fwd_kernel, nb=nb, slots=slots, heads=heads, hw=hw, sizes=sizes, turns=turns),
        out_shape=(
            jax.ShapeDtypeStruct((rows, heads * hw), F32),
            jax.ShapeDtypeStruct((nb, hw, lanes), F32),
            jax.ShapeDtypeStruct((nb, 1, lanes), F32),
            jax.ShapeDtypeStruct((nb, hw, lanes), BF),
            jax.ShapeDtypeStruct((units * UNIT, 2 * hw), BF),
            jax.ShapeDtypeStruct((units, 2 * hw, UNIT), BF),
            jax.ShapeDtypeStruct((units,), jnp.int32),
        ),
        in_specs=[sm, sm] + [vm] * 6,
        out_specs=(vm,) * 6 + (sm,),
        scratch_shapes=[
            pltpu.VMEM((2 * hw, lanes), BF),
            pltpu.VMEM((2 * hw, lanes), F32),
            pltpu.VMEM((1, lanes), F32),
            pltpu.SMEM((units + 1,), jnp.int32),
            pltpu.SMEM((units + 1,), jnp.int32),
            pltpu.SMEM((units + 1,), jnp.int32),
            pltpu.SMEM((1,), jnp.int32),
        ],
        compiler_params=pltpu.CompilerParams(vmem_limit_bytes=60 << 20),
        cost_estimate=pl.CostEstimate(
            flops=40 * 10**9, bytes_accessed=8 << 20, transcendentals=26 * 10**6
        ),
        name="attention_forward",
    )(useg, place, *pieces, q)


def prepare_kernel(qt_ref, ot_ref, l_ref, do_ref, qa_ref, doa_ref, dot_ref, *, nb, heads, hw):
    pad = jnp.zeros((hw - 3, heads * TB), BF)

    def prepare(i, carry):
        rows = pl.ds(pl.multiple_of(i * TB, TB), TB)
        a, b, c = split3(-l_ref[i])
        qa_ref[i] = jnp.concatenate([qt_ref[i], a, b, c, pad], axis=0).T
        dt = to_lanes(do_ref[rows, :], heads, hw)
        dot_ref[i] = dt
        total = jnp.sum(dt.astype(F32) * ot_ref[i], axis=0, keepdims=True)
        a, b, c = split3(-total)
        doa_ref[i] = jnp.concatenate([a, b, c, pad, dt], axis=0).T
        return carry

    lax.fori_loop(0, nb, prepare, 0)


def bwd_kernel(
    useg, place, order, kaug_ref, vt_ref, qa, doa, qt, dot_t, *rest,
    nb, parts, first, last, dealt, heads, hw
):
    if first:
        dqacc, dkv_ref, kt, dkvt = rest
    elif last:
        dqold, normed, dq_ref, dkv_ref, dqacc, kt, dkvt = rest
    else:
        dqold, _, dqacc, dkv_ref, kt, dkvt = rest
    grid_at = pl.program_id(0)
    steps = pl.num_programs(0) - (2 if last and dealt else 0)
    step_at = jnp.minimum(grid_at, steps - 1)
    me, group = place[0], place[1]
    unit = order[step_at // len(parts) * nb + step_at % len(parts) + parts[0]]
    scale = LOG2E / math.sqrt(hw)
    lanes = heads * TB

    @pl.when(grid_at == 0)
    def _():
        dqacc[...] = jnp.zeros_like(dqacc) if first else dqold[...]

    unit_seg = useg[unit]

    def block(i, carry):
        own = group * nb + i

        def step(first, size, masked):
            keys = pl.ds(first, size)
            s = dot(qa[i], kt[:, keys]) * scale
            if masked:
                mask = first + lax.broadcasted_iota(
                    jnp.int32, (lanes, size), 1
                ) <= query_offsets(lax.broadcasted_iota(jnp.int32, (lanes, size), 0), me)
                s = jnp.where(mask, s, -1e30)
            p = jnp.exp2(s)
            ds = (p * dot(doa[i], vt_ref[0, :, keys])).astype(BF)
            dkvt[hw:, keys] += dot(dot_t[i], p.astype(BF))
            dkvt[:hw, keys] += dot(qt[i], ds)
            dqacc[i] += dot(ds, kaug_ref[keys, :])

        @pl.when((unit_seg == 0) & (own != unit) & ((useg[own] != 0) | (own > unit)))
        def _():
            step(0, UNIT, False)

        @pl.when(own == unit)
        def _():
            def part_of_own(k, carry):
                step(pl.multiple_of(k * (UNIT // 2), UNIT // 2), UNIT // 2, True)
                return carry

            lax.fori_loop(0, 2, part_of_own, 0)

        return carry

    def keys():
        kt[...] = kaug_ref[...].T
        dkvt[...] = jnp.zeros_like(dkvt)
        lax.fori_loop(0, nb, block, 0)
        factor = jnp.where(
            lax.broadcasted_iota(jnp.int32, (2 * hw, 1), 0) < hw, 1 / math.sqrt(hw), 1.0
        )
        dkv = (dkvt[...] * factor).T.reshape(TB // RUN, INNER, RUN, 2 * hw)
        for d in range(INNER):
            to = piece_at(d, me // 4, dealt)
            dkv_ref[to] = dkv[:, d].reshape(TB, 2 * hw).astype(BF)

    if last and dealt:
        pl.when(grid_at < steps)(keys)
    else:
        keys()

    if last:
        @pl.when(grid_at == steps - 1)
        def _():
            def finish(i, carry):
                rows = pl.ds(pl.multiple_of(i * TB, TB), TB)
                a = dqacc[i]
                dq_ref[rows, :] = (
                    jnp.concatenate([a[h * TB : (h + 1) * TB, :hw] for h in range(heads)], axis=1)
                    * (1 / math.sqrt(hw))
                ).astype(BF)
                return carry

            lax.fori_loop(0, nb, finish, 0)

    if last and dealt:
        @pl.when(grid_at >= steps)
        def _():
            width = dq_ref.shape[1]
            half = width // 2
            rows = pl.ds(pl.multiple_of((grid_at - steps) * half, half), half)
            grad = dot(normed[rows, :], dq_ref[...]).astype(BF)
            piece = half // INNER
            for c in range(INNER):
                to = piece_at(c, me // 4, dealt)
                for k in range(width // 128):
                    dkv_ref[to, k * piece : (k + 1) * piece, :] = grad[
                        c * piece : (c + 1) * piece, k * 128 : (k + 1) * 128
                    ]


def attention_backward(
    useg, place, order, kaug, vt, qa, doa, qt, dot_t, dqold, more_in, parts, joint, heads, hw
):
    nb, lanes, _ = qa.shape
    slots = vt.shape[0] // nb
    first, last = dqold is None, parts[-1] == nb - 1
    dealt = slots == 1
    more = 2 if last and dealt else 0
    turns_out = len(parts) + more if last else joint
    base = 0 if last else parts[0]
    vm = pl.BlockSpec(memory_space=pltpu.VMEM)
    acc_shape = jax.ShapeDtypeStruct((nb, lanes, 2 * hw), F32)
    count = len(parts)

    def at(u, seg, place, order):
        u = jnp.minimum(u, slots * count - 1)
        return order[u // count * nb + u % count + parts[0]]

    def to(u, seg, place, order):
        if dealt:
            return (0, u + base, 0)
        return (u // count, u % count + base, 0)

    return pl.pallas_call(
        functools.partial(
            bwd_kernel, nb=nb, parts=parts, first=first, last=last, dealt=dealt, heads=heads, hw=hw
        ),
        out_shape=(
            jax.ShapeDtypeStruct((nb * TB, heads * hw), BF) if last else acc_shape,
            jax.ShapeDtypeStruct((slots * INNER, turns_out * TB, 2 * hw), BF),
        ),
        grid_spec=pltpu.PrefetchScalarGridSpec(
            num_scalar_prefetch=3,
            grid=(slots * count + more,),
            in_specs=[
                pl.BlockSpec((UNIT, 2 * hw), lambda *a: (at(*a), 0)),
                pl.BlockSpec((1, 2 * hw, UNIT), lambda *a: (at(*a), 0, 0)),
            ]
            + [vm] * (4 if first else 6 if last else 5)
            + ([] if first or last else [pl.BlockSpec(memory_space=pl.ANY)]),
            out_specs=(
                vm,
                pl.BlockSpec((INNER, TB, 2 * hw), to),
            ),
            scratch_shapes=([pltpu.VMEM(acc_shape.shape, F32)] if last and not first else [])
            + [
                pltpu.VMEM((2 * hw, UNIT), BF),
                pltpu.VMEM((2 * hw, UNIT), F32),
            ],
        ),
        compiler_params=pltpu.CompilerParams(vmem_limit_bytes=60 << 20),
        cost_estimate=pl.CostEstimate(
            flops=8 * 10**9 * count, bytes_accessed=12 << 20, transcendentals=2 * 10**6 * count
        ),
        input_output_aliases={} if first or last else {10: 1},
        name="attention_backward",
    )(useg, place, order, kaug, vt, qa, doa, qt, dot_t, *([] if first else [dqold, more_in]))


def exact_dot(x, ones):
    a, b, c = split3(x)
    return dot(a, ones) + dot(b, ones) + dot(c, ones)


def norm_parts(values):
    mean_val = jnp.mean(values, axis=-1, keepdims=True)
    centered = values - mean_val
    variance = jnp.mean(centered * centered, axis=-1, keepdims=True)
    inverse = lax.rsqrt(variance + 1e-05)
    return centered * inverse, inverse


def norm_back(grad, unit, inverse, gain):
    scaled = grad * gain
    shift = jnp.mean(scaled, axis=-1, keepdims=True)
    along = jnp.mean(scaled * unit, axis=-1, keepdims=True)
    return inverse * (scaled - shift - unit * along)


def piece_at(c, my_rest, dealt):
    return c % 4 * (INNER // 4) + jnp.bitwise_xor(c // 4, my_rest) if dealt else c


def put_pieces(grads_ref, where, value, first, rows, at, count, step):
    piece = rows // 2 // count
    value = value.astype(BF)
    half = first // (rows // 2)
    device = (first - half * (rows // 2)) // piece
    for k in range(step // piece):
        to = piece_at(device + k, where[1], count == INNER)
        grads_ref[to, half, at : at + piece, :] = value[k * piece : (k + 1) * piece]


def middle_kernel(
    where, x_ref, att_ref, logit_ref, code_ref, cot_ref, norm_ref, out_w, up_w, down_w,
    qt_ref, ot_ref, low_ref,
    result_ref, middle_grad_ref, logit_grad_ref, norm_grad_ref, grads_ref, qa_ref, doa_ref, dot_ref,
    att_grad_s, mixed_s, normed_s, hidden_s, pre_s, branch_s, *, count, heads
):
    rows, width = x_ref.shape
    chunk = rows
    hw = width // heads
    gain = norm_ref[...].astype(F32)
    lane = lax.broadcasted_iota(jnp.int32, (chunk, 128), 1)
    head = lax.broadcasted_iota(jnp.int32, (128, width), 0)
    column = lax.broadcasted_iota(jnp.int32, (128, width), 1)
    widen = jnp.where(column // hw == head, 1.0, 0.0).astype(BF)
    narrow = jnp.where(
        lax.broadcasted_iota(jnp.int32, (width, 128), 0) // hw
        == lax.broadcasted_iota(jnp.int32, (width, 128), 1),
        1.0, 0.0,
    ).astype(BF)
    if True:
        at = slice(None)
        code = code_ref[at, :]
        chosen = ((code // heads == lane) | (code % heads == lane)) & (lane < heads)
        lifted = jnp.where(chosen, logit_ref[at, :], -1e30)
        raised = jnp.where(
            chosen, jnp.exp(lifted - jnp.max(lifted, axis=-1, keepdims=True)), 0.0
        )
        gate = raised / jnp.sum(raised, axis=-1, keepdims=True)
        gates = exact_dot(gate, widen)
        attended = att_ref[at, :]
        mixed = (gates * attended).astype(BF)
        mixed_s[at, :] = mixed
        middle = x_ref[at, :].astype(F32) + dot(mixed, out_w[...])
        unit, inverse = norm_parts(middle)
        normed = (unit * gain).astype(BF)
        normed_s[at, :] = normed
        cot = cot_ref[at, :]
        back = jnp.zeros((chunk, width), F32)
        step = 1024

        def hidden_block(k, sums):
            total, back = sums
            to = pl.ds(pl.multiple_of(k * step, step), step)
            pre = dot(normed, up_w[:, to])
            inside = 0.7978845608028654 * (pre + 0.044715 * pre * pre * pre)
            t = jnp.tanh(inside)
            half = 0.5 * (1.0 + t)
            hidden = (pre * half).astype(BF)
            slope = half + 0.5 * pre * (1.0 - t * t) * (
                0.7978845608028654 * (1.0 + 3 * 0.044715 * pre * pre)
            )
            hidden_s[:, to] = hidden
            pre_grad = (outer(cot, down_w[to, :]) * slope).astype(BF)
            pre_s[:, to] = pre_grad
            return total + dot(hidden, down_w[to, :]), back + outer(pre_grad, up_w[:, to])

        total, back = lax.fori_loop(0, up_w.shape[1] // step, hidden_block, (middle, back))
        result_ref[at, :] = total.astype(BF)
        norm_grad_ref[...] = jnp.sum(
            (back * unit).reshape(chunk // 8, 8, width), axis=0
        )
        middle_grad = cot.astype(F32) + norm_back(back, unit, inverse, gain)
        middle_grad_ref[at, :] = middle_grad
        branch = middle_grad.astype(BF)
        branch_s[at, :] = branch
        mixed_grad = outer(branch, out_w[...])
        gate_grad = exact_dot(mixed_grad * attended, narrow)
        logit_grad_ref[at, :] = (
            gate * (gate_grad - jnp.sum(gate * gate_grad, axis=-1, keepdims=True))
        ).astype(BF)
        att_grad_s[at, :] = (gates * mixed_grad).astype(BF)
    prepare_kernel(
        qt_ref, ot_ref, low_ref, att_grad_s, qa_ref, doa_ref, dot_ref,
        nb=qt_ref.shape[0], heads=heads, hw=hw,
    )
    ff = hidden_s.shape[1]
    across = width
    half, down_rows = width // 2, ff // 2 // count

    def down_block(k, carry):
        at = pl.ds(pl.multiple_of(k * width, width), width)
        put_pieces(grads_ref, where, inner(hidden_s[:, at], cot), k * width, ff, 0, count, width)
        return carry

    lax.fori_loop(0, ff // width, down_block, 0)

    block = half // 2

    def up_block(k, carry):
        at = pl.ds(pl.multiple_of(k * block, block), block)
        up = inner(normed_s[:, at], pre_s[...])
        piece = half // count
        for c in range(ff // width):
            put_pieces(
                grads_ref, where, up[:, c * width : (c + 1) * width], k * block, width,
                down_rows + c * piece, count, block,
            )
        put_pieces(
            grads_ref, where, inner(mixed_s[:, at], branch_s[...]), k * block, width,
            down_rows + ff // width * piece, count, block,
        )
        return carry

    lax.fori_loop(0, width // block, up_block, 0)


def middle_pass(core, x, attended, logits, code, cot, norm_b, out_w, up_w, down_w, kept, heads, count):
    rows, width = x.shape
    nb, hw, lanes = kept[0].shape
    ff = up_w.shape[1]
    piece_rows = (ff * 2 + width) // (2 * count)
    vm = pl.BlockSpec(memory_space=pltpu.VMEM)
    shape = jax.ShapeDtypeStruct
    return pl.pallas_call(
        functools.partial(middle_kernel, count=count, heads=heads),
        out_shape=(
            shape((rows, width), BF),
            shape((rows, width), F32),
            shape((rows, 128), BF),
            shape((8, width), F32),
            shape((count, 2, piece_rows, width), BF),
            shape((nb, lanes, 2 * hw), BF),
            shape((nb, lanes, 2 * hw), BF),
            shape((nb, hw, lanes), BF),
        ),
        in_specs=[pl.BlockSpec(memory_space=pltpu.SMEM)] + [vm] * 12,
        out_specs=(vm,) * 8,
        scratch_shapes=[
            pltpu.VMEM((rows, width), BF),
            pltpu.VMEM((rows, width), BF),
            pltpu.VMEM((rows, width), BF),
            pltpu.VMEM((rows, ff), BF),
            pltpu.VMEM((rows, ff), BF),
            pltpu.VMEM((rows, width), BF),
        ],
        compiler_params=pltpu.CompilerParams(vmem_limit_bytes=60 << 20),
        cost_estimate=pl.CostEstimate(
            flops=9 * 10**9, bytes_accessed=24 << 20, transcendentals=2 * 10**6
        ),
        name="middle_pass",
    )(core, x, attended, logits, code, cot, norm_b, out_w, up_w, down_w, *kept)


class Layout:
    def __init__(self, ctx_count):
        sizes = [4]
        while math.prod(sizes) < ctx_count:
            sizes.append(2)
        assert math.prod(sizes) == ctx_count
        self.sizes = tuple(sizes)
        self.axes = tuple(f"c{k}" for k in range(len(sizes)))
        cut = len(sizes)
        while math.prod(sizes[cut:]) < INNER:
            cut -= 1
        assert math.prod(sizes[cut:]) == INNER
        self.outer_axes, self.inner_axes = self.axes[:cut], self.axes[cut:]
        self.count = ctx_count


def exchange(x, axis, size, step):
    return lax.ppermute(x, axis, [(i, i ^ step) for i in range(size)])


def spread(x, order, lay, start=0, stop=None):
    for axis in order[start:stop]:
        size = lay.sizes[lay.axes.index(axis)]
        x = jnp.concatenate([x] + [exchange(x, axis, size, step) for step in range(1, size)])
    return x


def gather_near(x, lay):
    return spread(x[None], lay.axes[:-2], lay)


def gather_sides(near, lay):
    y_axis, x_axis = lay.axes[-2:]
    return exchange(near, x_axis, 2, 1), exchange(near, y_axis, 2, 1)


def gather_far(near_x, near_y, lay, cut):
    y_axis, x_axis = lay.axes[-2:]
    return exchange(near_x[:, :cut], y_axis, 2, 1), exchange(near_y[:, cut:], x_axis, 2, 1)


def deal(x, lay):
    rows, width = x.shape
    packed = x.reshape(rows // (RUN * INNER), INNER, RUN, width).transpose(1, 0, 2, 3)
    packed = packed.reshape(INNER, rows // INNER, width)
    return lax.all_to_all(packed, lay.inner_axes, 0, 0, tiled=True)


def move_back(x, lay):
    rows, width = x.shape
    return lax.all_to_all(x.reshape(INNER, rows // INNER, width), lay.inner_axes, 0, 0, tiled=True)


def take_back(back):
    rows, width = back.shape[0] * back.shape[1], back.shape[2]
    back = back.reshape(INNER, rows // (RUN * INNER), RUN, width).transpose(1, 0, 2, 3)
    return back.reshape(rows, width)


def tie(*values):
    return lax.optimization_barrier(values)


def order_pieces(pieces, mine, lay):
    if lay.count == INNER:
        return pieces
    index = jnp.arange(lay.count, dtype=jnp.int32)
    quarter = lay.count // 4
    rest = jnp.bitwise_xor(index % quarter, mine // 4)
    return jnp.take(pieces, rest * 4 + index // quarter, axis=0)


def plane_swap(pieces, lay):
    return lax.all_to_all(pieces, lay.axes[-2:], 0, 0, tiled=True)


def plane_sum(pieces):
    return add_pieces(pieces.reshape((4, -1) + pieces.shape[1:]))


def rest_terms(pieces, lay):
    axes = list(zip(lay.axes, lay.sizes))[:-2]
    for k, (axis, size) in enumerate(axes):
        pieces = pieces.reshape((size, -1) + pieces.shape[1:])
        terms = [pieces[0]] + [exchange(pieces[step], axis, size, step) for step in range(1, size)]
        if k < len(axes) - 1:
            pieces = sum(term.astype(F32) for term in terms).astype(BF)
    return [term[0] for term in terms]


def add_pieces(pieces):
    return jnp.sum(pieces.astype(F32), axis=0).astype(BF)


def add_terms(refs):
    total = refs[0][...].astype(F32)
    for ref in refs[1:]:
        total = total + ref[...].astype(F32)
    return total.astype(BF)


def last_kernel(
    core, order, x_ref, base_ref, middle_grad_ref, logit_ref, norm_b_ref, gain_ref, keyval_w, *rest,
    heads, dealt
):
    first, *terms, grad_ref, small_ref, keyval_s = rest
    rows, width = x_ref.shape
    gain = gain_ref[...].astype(F32)
    unit, inverse = norm_parts(x_ref[...].astype(F32))
    normed = (unit * gain).astype(BF)
    early, late = first[...], add_terms(terms)
    late_rows = rows - early.shape[0]
    turned = jnp.concatenate([early, late[:late_rows]], axis=0)
    for k in range(rows // TB):
        to = pl.multiple_of((order[k] if dealt else k) * TB, TB)
        keyval_s[pl.ds(to, TB), :] = turned[k * TB : (k + 1) * TB]
    keyval_grad = keyval_s[...]
    grad = base_ref[...] + outer(keyval_grad, keyval_w[...])
    grad_ref[...] = (middle_grad_ref[...] + norm_back(grad, unit, inverse, gain)).astype(BF)
    keyval_sum = inner(normed, keyval_grad).astype(BF)
    thin = jnp.concatenate(
        [
            inner(logit_ref[...], normed)[:heads],
            jnp.sum(grad * unit, axis=0, keepdims=True),
            jnp.sum(norm_b_ref[...], axis=0, keepdims=True),
            jnp.zeros((-(heads + 2) % 16, width), F32),
        ],
        axis=0,
    ).astype(BF)
    half, query_half = width // 2, (late.shape[0] - late_rows) // 2
    for side in range(2):
        to = jnp.bitwise_xor(core[0], side)
        small_ref[to, :half, :] = keyval_sum[side * half : (side + 1) * half]
        first = half
        for c in range(side * half, (side + 1) * half, 128):
            small_ref[to, first : first + thin.shape[0], :] = thin[:, c : c + 128]
            first += thin.shape[0]
        small_ref[to, first:, :] = late[late_rows + side * query_half :][:query_half]


def last_pass(core, order, dealt, x, base, middle_grad, logit_low, norm_b_part, gain, keyval_w, early, late, heads):
    rows, width = x.shape
    query_half = (late[0].shape[0] + early[0].shape[0] - rows) // 2
    thin_rows = (heads + 2 + -(heads + 2) % 16) * (width // 2) // 128
    sums = width // 2 + thin_rows
    arrays = (x, base, middle_grad, logit_low, norm_b_part, gain, keyval_w, *early, *late)
    vm = pl.BlockSpec(memory_space=pltpu.VMEM)
    grad, small = pl.pallas_call(
        functools.partial(last_kernel, heads=heads, dealt=dealt),
        out_shape=(
            jax.ShapeDtypeStruct((rows, width), BF),
            jax.ShapeDtypeStruct((2, sums + query_half, 128), BF),
        ),
        grid=(1,),
        in_specs=[pl.BlockSpec(memory_space=pltpu.SMEM)] * 2
        + [pl.BlockSpec(a.shape, lambda g: (0, 0)) for a in arrays],
        out_specs=(vm,) * 2,
        scratch_shapes=[pltpu.VMEM((rows, keyval_w.shape[1]), BF)],
        compiler_params=pltpu.CompilerParams(vmem_limit_bytes=40 << 20),
        cost_estimate=pl.CostEstimate(flops=10**9, bytes_accessed=6 << 20, transcendentals=0),
        name="last_pass",
    )(core, order, *arrays)
    return grad, small, sums


def sum_and_gather(total, rest, axis, lay):
    sums, height = total.shape[0], rest.shape[1]
    size = lay.sizes[lay.axes.index(axis)]
    send = jnp.concatenate([total, rest.reshape(-1, 128)], axis=0)
    got = [exchange(send, axis, size, step) for step in range(1, size)]
    terms = [total.astype(F32)] + [other[:sums].astype(F32) for other in got]
    while len(terms) > 1:
        terms = [terms[k] + terms[k + 1] for k in range(0, len(terms), 2)]
    rest = jnp.concatenate(
        [rest] + [other[sums:].reshape(-1, height, 128) for other in got], axis=0
    )
    return terms[0].astype(BF), rest


def query_kernel(mine, rest_ref, out_ref, *, count):
    piece = out_ref.shape[0] // count
    for c in range(count):
        at = jnp.bitwise_xor(c, mine[0])
        for k in range(out_ref.shape[1] // 128):
            out_ref[c * piece : (c + 1) * piece, k * 128 : (k + 1) * 128] = rest_ref[
                at, k * piece : (k + 1) * piece, :
            ].astype(F32)


def place_query(mine, rest, shape, lay):
    vm = pl.BlockSpec(memory_space=pltpu.VMEM)
    return pl.pallas_call(
        functools.partial(query_kernel, count=lay.count),
        out_shape=jax.ShapeDtypeStruct(shape, F32),
        in_specs=[pl.BlockSpec(memory_space=pltpu.SMEM), vm],
        out_specs=vm,
        name="place_query",
    )(mine, rest)


def place_kernel(mine, near, near_x, near_y, far_a, far_b, *outs, count, across, sizes):
    *outs, piece_s = outs
    cut = far_a.shape[1]
    looped = all(out.shape[0] // count % 8 == 0 for out in outs)

    def one(c, carry):
        s = jnp.bitwise_xor(c, mine[0])
        index = near_index(s // 4, sizes)
        for side, ref in enumerate((near, near_x, near_y)):
            @pl.when(s % 4 == side)
            def _(ref=ref):
                piece_s[...] = ref[index]

        @pl.when(s % 4 == 3)
        def _():
            piece_s[:cut, :] = far_a[index]
            piece_s[cut:, :] = far_b[index]

        first = 0
        for out in outs:
            piece = out.shape[0] // count
            rows = pl.ds(pl.multiple_of(c * piece, piece) if looped else c * piece, piece)
            for k in range(out.shape[1] // across):
                out[rows, k * across : (k + 1) * across] = piece_s[
                    first : first + piece, :
                ].astype(F32)
                first += piece
        return carry

    if looped:
        lax.fori_loop(0, count, one, 0)
    else:
        for c in range(count):
            one(c, 0)


def place_pieces(pieces, mine, shapes, across, sizes):
    vm = pl.BlockSpec(memory_space=pltpu.VMEM)
    count = 4 * pieces[0].shape[0]
    return pl.pallas_call(
        functools.partial(place_kernel, count=count, across=across, sizes=sizes),
        out_shape=tuple(jax.ShapeDtypeStruct(shape, F32) for shape in shapes),
        in_specs=[pl.BlockSpec(memory_space=pltpu.SMEM)] + [vm] * 5,
        out_specs=(vm,) * len(shapes),
        scratch_shapes=[pltpu.VMEM(pieces[0].shape[1:], BF)],
        compiler_params=pltpu.CompilerParams(vmem_limit_bytes=40 << 20),
        cost_estimate=pl.CostEstimate(
            flops=0, bytes_accessed=24 * pieces[0].size, transcendentals=0
        ),
        name="place_pieces",
    )(mine, *pieces)


def layer_norm(values, gain_vec):
    mean_val = jnp.mean(values, axis=-1, keepdims=True)
    centered = values - mean_val
    variance = jnp.mean(centered * centered, axis=-1, keepdims=True)
    return centered * lax.rsqrt(variance + 1e-05) * gain_vec


def on_device(
    lay, inputs, cotangent, segments, routes, norm_first, w_query, w_keyval, w_router, w_out,
    norm_second, w_up, w_down
):
    def whole(shard):
        return lax.all_gather(shard, "w", axis=0, tiled=True)

    rows, width = inputs.shape[1:]
    head_count = w_router.shape[1]
    head_width = w_keyval.shape[1] // 2
    nb = rows // TB
    group_count = lay.count // INNER
    me = lax.axis_index(lay.inner_axes)
    group = lax.axis_index(lay.outer_axes) if lay.outer_axes else jnp.int32(0)
    place = jnp.stack([me, group]).astype(jnp.int32)
    mine = (group * INNER + me).astype(jnp.int32)[None]

    core = lax.axis_index("w")
    near_sizes = lay.sizes[:-2]

    def whole_by_exchange(shard):
        other = exchange(shard, "w", 2, 1)
        return jnp.where(
            core == 0,
            jnp.concatenate([shard, other], axis=0),
            jnp.concatenate([other, shard], axis=0),
        )

    narrow = whole(
        jnp.concatenate([w_keyval, w_router, norm_first[:, None], norm_second[:, None]], axis=1)
    )
    keyval_w = narrow[:, : 2 * head_width]
    narrow = narrow[:, 2 * head_width :]
    router_w = jnp.pad(narrow[:, :head_count], ((0, 0), (0, 128 - head_count)))
    norm_a, norm_b = narrow[:, head_count], narrow[:, head_count + 1]
    own_normed = layer_norm(inputs[0].astype(F32), norm_a.astype(F32)).astype(BF)
    spans = rows // (RUN * INNER)
    own_seg = segments[:, :: RUN * INNER].astype(BF)
    own_seg = jnp.pad(own_seg, ((0, 7), (0, 2 * head_width - spans)))
    near = gather_near(
        jnp.concatenate([dot(own_normed, keyval_w).astype(BF), own_seg], axis=0), lay
    )
    near_x, near_y = gather_sides(near, lay)
    rows_low = deal(inputs[0], lay).reshape(rows, width)
    near_x, near_y, rows_low = tie(near_x, near_y, rows_low)
    far = gather_far(near_x, near_y, lay, (nb // 2) * TB)
    query_w, out_w = whole(w_query), whole(w_out)
    up_w, down_w = whole_by_exchange(w_up), whole_by_exchange(w_down)

    quarter = lay.count // 4
    entry = [near_index(rest, near_sizes) for rest in range(quarter)]
    source = [entry.index(k) * 4 + side for side in range(4) for k in range(quarter)]
    source = jnp.bitwise_xor(jnp.array(source, jnp.int32), mine)
    far_rows = rows - (nb // 2) * TB
    all_seg = jnp.concatenate(
        [near[:, rows], near_x[:, rows], near_y[:, rows], far[1][:, far_rows]], axis=0
    ).astype(jnp.int32)
    at = source[:, None] * spans + jnp.arange(128, dtype=jnp.int32)[None]
    at = jnp.where(jnp.arange(128)[None] < spans, at, -1)
    first = jnp.arange(group_count * nb, dtype=jnp.int32) * (UNIT // (RUN * INNER))
    useg = jnp.sum(jnp.where(at[None] == first[:, None, None], all_seg[None], 0), axis=(1, 2))

    rows_in = rows_low.astype(F32)
    normed = layer_norm(rows_in, norm_a.astype(F32)).astype(BF)
    queries = dot(normed, query_w).astype(BF)
    logits = dot(normed, router_w)

    code = (routes[0, :, 0] * head_count + routes[0, :, 1]).astype(BF)
    slot_rows = rows // INNER
    code = code.reshape(rows // (RUN * INNER), INNER, RUN).transpose(1, 0, 2)
    code = jnp.pad(code.reshape(INNER, 1, slot_rows), ((0, 0), (0, RUN - 1), (0, width - slot_rows)))
    packed = cotangent[0].reshape(rows // (RUN * INNER), INNER, RUN, width).transpose(1, 0, 2, 3)
    packed = jnp.concatenate([packed.reshape(INNER, slot_rows, width), code], axis=1)
    packed, near_x, near_y = tie(packed, near_x, near_y)
    dealt = lax.all_to_all(packed, lay.inner_axes, 0, 0, tiled=True)
    if nb == 10:
        turns, one, two = (0, 1, 2, 8, 5, 6, 7, 9, 3, 4), 4, 8
    else:
        turns, one, two = tuple(range(group_count * nb)), nb // 3, nb - nb // 3
    attended, ot, low, qt, kaug, vt, order = attention_forward(
        useg, place, (near, near_x, near_y) + far, queries, head_count, head_width, near_sizes,
        turns,
    )
    attended, dealt = tie(attended, dealt)
    grad_top = dealt[:, :slot_rows].reshape(rows, width)
    code = dealt[:, slot_rows, :slot_rows].reshape(rows, 1).astype(jnp.int32)
    core_at = jnp.stack([core, me // 4]).astype(jnp.int32)
    result, middle_grad, logit_low, norm_b_part, grads, qa, doa, dot_t = middle_pass(
        core_at, rows_low, attended, logits, code, grad_top, norm_b[None], out_w, up_w, down_w,
        (qt, ot, low), head_count, lay.count,
    )
    grads = grads.reshape(lay.count, -1, width)
    grads, qa = tie(grads, qa)
    swapped = plane_swap(order_pieces(grads, mine, lay), lay)
    normed_t = normed.T

    def backward(first, stop, dq, more_in):
        return attention_backward(
            useg, place, order, kaug, vt, qa, doa, qt, dot_t, dq, more_in,
            tuple(range(first, stop)), two, head_count, head_width,
        )

    dq, dkv = backward(0, one, None, None)
    dq, dkv, swapped = tie(dq, dkv, swapped)
    halves = plane_sum(swapped)
    halves = halves.reshape(halves.shape[0], 2, -1, width)
    weights_own = lax.dynamic_index_in_dim(halves, core, 1, keepdims=False)
    weights_other = exchange(
        lax.dynamic_index_in_dim(halves, 1 - core, 1, keepdims=False), "w", 2, 1
    )
    weight_terms = rest_terms(
        (weights_own.astype(F32) + weights_other.astype(F32)).astype(BF), lay
    )
    back = move_back(result, lay)
    dq, dkv = backward(one, two, dq, dkv)
    dq, dkv, back, *weight_terms = tie(dq, dkv, back, *weight_terms)
    output = take_back(back)
    weights_near = gather_near(sum(term.astype(F32) for term in weight_terms).astype(BF), lay)
    swapped = plane_swap(order_pieces(dkv, mine, lay), lay)
    dq, late = backward(two, nb, dq, normed_t)
    dq, late, swapped, weights_near = tie(dq, late, swapped, weights_near)
    early = rest_terms(plane_sum(swapped), lay)
    if lay.count != INNER:
        query_w_grad = inner(normed, dq).astype(BF)
        piece = width // 2 // lay.count
        query_parts = query_w_grad.reshape(2, lay.count, piece, width // 128, 128)
        query_parts = query_parts.transpose(1, 0, 3, 2, 4).reshape(lay.count, -1, 128)
        late = order_pieces(jnp.concatenate([late, query_parts], axis=1), mine, lay)
    swapped = plane_swap(late, lay)
    base = outer(dq, query_w) + outer(logit_low, router_w)
    early = sum(term.astype(F32) for term in early).astype(BF)
    swapped, base, weights_near = tie(swapped, base, weights_near)
    weights_x, weights_y = gather_sides(weights_near, lay)
    late = plane_sum(swapped)
    late, early = tie(late, early)
    late = rest_terms(late, lay)
    grad_rows, small, sums = last_pass(
        core_at, order, lay.count == INNER, rows_low, base, middle_grad, logit_low, norm_b_part, norm_a[None], keyval_w,
        [early], late, head_count,
    )
    grad_rows, small, weights_x, weights_y = tie(grad_rows, small, weights_x, weights_y)
    weights_far = gather_far(weights_x, weights_y, lay, w_down.shape[0] // lay.count)
    back = move_back(grad_rows, lay)
    other = exchange(small[1], "w", 2, 1)
    both = (small[0].astype(F32) + other.astype(F32)).astype(BF)
    total, rest = both[:sums], both[sums:][None]
    for axis in lay.axes[::-1]:
        total, rest = sum_and_gather(total, rest, axis, lay)
        if axis == lay.axes[1]:
            total, rest, back = tie(total, rest, back)
        elif axis == lay.axes[-1]:
            total, rest, *weights_far = tie(total, rest, *weights_far)
    input_grad = take_back(back).astype(F32)[None]
    query_sum = place_query(mine, rest, w_query.shape, lay)
    half = width // 2
    keyval_sum = total[:half].astype(F32)
    thin = total[half:].reshape(half // 128, -1, 128).transpose(1, 0, 2).reshape(-1, half)
    thin = thin.astype(F32)
    down_sum, up_sum, out_sum = place_pieces(
        (weights_near, weights_x, weights_y, *weights_far), mine,
        [w_down.shape, w_up.shape, w_out.shape], width, near_sizes,
    )
    return (
        output[None],
        input_grad,
        thin[head_count],
        query_sum,
        keyval_sum,
        thin[:head_count].T,
        out_sum,
        thin[head_count + 1],
        up_sum,
        down_sum,
    )


def solution(mesh):
    ctx_count, core_count = mesh.shape["ctx"], mesh.shape["wshard"]
    lay = Layout(ctx_count)
    grid = Mesh(mesh.devices.reshape(lay.sizes + (core_count,)), lay.axes + ("w",))
    ctx = lay.axes
    tokens = P("w", ctx, None)
    return jax.shard_map(
        functools.partial(on_device, lay),
        mesh=grid,
        in_specs=(
            tokens, tokens, P("w", ctx), tokens,
            P("w"), P("w", None), P("w", None), P("w", None), P("w", None),
            P("w"), P("w", None), P("w", None),
        ),
        out_specs=(
            tokens, tokens,
            P("w"), P("w", None), P("w", None), P("w", None), P("w", None),
            P("w"), P("w", None), P("w", None),
        ),
        check_vma=False,
    )
```
